32 devices in a mesh: dp: 8 (over z, y), tm: 4 (over x, core).
Axes of the slice: x: 2, y: 2, z: 4, core: 2. Of those that a mesh axis runs over, the one named last changes fastest.
Arguments:
- clip_frames: bfloat16 [8, 8, 4, 32, 128], P('dp', 'tm'), may hold values from -6 to 6
- out_grad: bfloat16 [8, 8, 4, 32, 128], P('dp', 'tm'), may hold values from -6 to 6
- conv_kernel: bfloat16 [3, 3, 3, 128, 128], replicated, may hold values from -0.109375 to 0.109375
- proj_weight: bfloat16 [128, 128], replicated, may hold values from -0.5 to 0.5
Outputs:
- mixed: bfloat16 [8, 8, 4, 32, 128], P('dp', 'tm')
- input_grad: bfloat16 [8, 8, 4, 32, 128], P('dp', 'tm')
- kernel_grad: float32 [3, 3, 3, 128, 128], replicated
- proj_grad: float32 [128, 128], replicated
The draws below stay inside these ranges and needn't reach their ends.
All inputs are finite; a program needn't handle non-finite values.
Results may differ from the reference program's by a relative error of at most 0.0034.
Values may be sent and summed in bfloat16 or wider, within the bound.
No kernel may reach another device: no remote copies, remote signals or barrier semaphores. Data moves between devices by JAX's collectives and lax.ppermute only.
A program may use at most 64 MiB of HBM per device.

```python
import math
import jax
import jax.numpy as jnp
from jax import lax

CH = 128
HEIGHT = 4
WIDTH = 32
CLIPS = 8
FRAMES = 8
PIXELS = 8192


def levels(own_key, extent, split, smallest, high):
    factor_of, own = 1.0, jax.random.fold_in(own_key, 6)
    for position, shards_of in split:
        draws = jnp.exp(jax.random.uniform(jax.random.fold_in(own, position), (shards_of,), jnp.float32, smallest / len(split), high / len(split)))
        factor_of = factor_of * jnp.repeat(draws, extent[position] // shards_of).reshape([-1 if axis == position else 1 for axis in range(len(extent))])
    return factor_of


def gaussian(own_key, shape, spread, limit, split=(), held_as=jnp.bfloat16):
    loudness = levels(own_key, shape, split, -0.22, 0.18) if split else 1.0
    result = jax.random.normal(own_key, shape, jnp.float32) * spread * loudness
    return jnp.minimum(jnp.maximum(result, -limit), limit).astype(held_as)


def setup_inputs(seed: int = 0) -> dict:
    key_of = jax.random.split(jax.random.key(seed), 5)
    clip_frames = gaussian(key_of[0], (CLIPS, FRAMES, HEIGHT, WIDTH, CH), 1.0, 6.0, ((0, 8), (1, 4)))
    out_grad = gaussian(key_of[1], (CLIPS, FRAMES, HEIGHT, WIDTH, CH), 1.0, 6.0, ((0, 8), (1, 4)))
    conv_kernel = gaussian(key_of[2], (3, 3, 3, CH, CH), (27 * CH) ** -0.5, 0.109375)
    proj_weight = gaussian(key_of[3], (CH, CH), CH ** -0.5, 0.5)
    return dict(clip_frames=clip_frames, out_grad=out_grad, conv_kernel=conv_kernel, proj_weight=proj_weight)


def patches_of(stack):
    height = stack.shape[1]
    width = stack.shape[2]
    padded = jnp.pad(stack, ((0, 0), (1, 1), (1, 1), (0, 0)))
    return jnp.concatenate([padded[:, row:row + height, col:col + width] for row in range(3) for col in range(3)], axis=-1)

def contract_rows(left, right):
    return lax.dot_general(left, right, (((0,), (0,)), ((), ())), preferred_element_type=jnp.float32)

def reference(clip_frames, out_grad, conv_kernel, proj_weight):
    chans = CH
    kern = conv_kernel.reshape(3, 9 * chans, chans)
    kern_flip = jnp.swapaxes(conv_kernel[:, ::-1, ::-1], 3, 4).reshape(3, 9 * chans, chans)
    rows = FRAMES * HEIGHT * WIDTH

    def one_clip(pair):
        frames, grads = pair
        padded = jnp.pad(frames, ((2, 0), (0, 0), (0, 0), (0, 0)))
        patches = patches_of(padded)
        pre = jnp.zeros((rows, chans), jnp.float32)
        for offset in range(3):
            pre = pre + jnp.dot(patches[offset:offset + FRAMES].reshape(rows, 9 * chans), kern[offset], preferred_element_type=jnp.float32)
        sig = jax.nn.sigmoid(pre)
        hidden = (pre * sig).astype(jnp.bfloat16)
        flat_grads = grads.reshape(rows, chans)
        mixed = (frames.reshape(rows, chans).astype(jnp.float32) + jnp.dot(hidden, proj_weight, preferred_element_type=jnp.float32)).astype(jnp.bfloat16)
        proj_part = contract_rows(hidden, flat_grads)
        hidden_grad = lax.dot_general(flat_grads, proj_weight, (((1,), (1,)), ((), ())), preferred_element_type=jnp.float32)
        pre_grad = (hidden_grad * sig * (1.0 + pre * (1.0 - sig))).astype(jnp.bfloat16)
        kern_part = jnp.stack([contract_rows(patches[offset:offset + FRAMES].reshape(rows, 9 * chans), pre_grad) for offset in range(3)])
        tail = jnp.pad(pre_grad.reshape(FRAMES, HEIGHT, WIDTH, chans), ((0, 2), (0, 0), (0, 0), (0, 0)))
        back = jnp.zeros((rows, chans), jnp.float32)
        for offset in range(3):
            piece = patches_of(tail[2 - offset:2 - offset + FRAMES]).reshape(rows, 9 * chans)
            back = back + jnp.dot(piece, kern_flip[offset], preferred_element_type=jnp.float32)
        input_grad = (flat_grads.astype(jnp.float32) + back).astype(jnp.bfloat16)
        return (mixed.reshape(frames.shape), input_grad.reshape(frames.shape), kern_part, proj_part)
    mixed, input_grad, kern_parts, proj_parts = lax.map(one_clip, (clip_frames, out_grad))
    scale = 1.0 / math.sqrt(PIXELS)
    kernel_grad = (lax.optimization_barrier(jnp.sum(kern_parts, axis=0)) * scale).reshape(3, 3, 3, CH, CH)
    proj_grad = lax.optimization_barrier(jnp.sum(proj_parts, axis=0)) * scale
    return (mixed, input_grad, kernel_grad, proj_grad)
```

```python
import functools
import math

import jax
import jax.numpy as jnp
from jax import lax
from jax.experimental import pallas as pl
from jax.experimental.pallas import tpu as pltpu
from jax.sharding import PartitionSpec as P

AXES = ("dp", "tm")
HALVINGS = 4
ORDERS = ((1, 2, 3), (2, 3, 1))


def passed_along(shard, axis, by):
    size = lax.axis_size(axis)
    pairs = [(i, i + by) for i in range(size) if 0 <= i + by < size]
    return lax.ppermute(shard, axis, pairs)


def patches_of(stack):
    height = stack.shape[1]
    width = stack.shape[2]
    padded = jnp.pad(stack, ((0, 0), (1, 1), (1, 1), (0, 0)))
    return jnp.concatenate(
        [padded[:, row : row + height, col : col + width] for row in range(3) for col in range(3)],
        axis=-1,
    )


def contract_rows(left, right):
    return lax.dot_general(
        left, right, (((0,), (0,)), ((), ())), preferred_element_type=jnp.float32
    )


def device_number():
    return lax.axis_index("dp") * lax.axis_size("tm") + lax.axis_index("tm")


def swapped(array, bits):
    count = lax.axis_size("dp") * lax.axis_size("tm")
    return lax.ppermute(array, AXES, [(i, i ^ (1 << bits[i & 1])) for i in range(count)])


def bit(number, place):
    return (number >> place) & 1


def place_of(offset, orders):
    return (
        4 * bit(offset, orders[0]) + 2 * bit(offset, orders[1]) + bit(offset, orders[2])
    )


def pack_kernel(me_ref, kern_ref, proj_ref, keep_ref, send_ref):
    me = me_ref[0] & 15
    core = me & 1
    taps = kern_ref.shape[0]
    for pair in range(8):
        places = []
        for c in range(2):
            places.append(place_of((2 * pair) ^ (me & 14), ORDERS[c]))
        mine = jnp.where(core == 0, places[0], places[1])
        other = jnp.where(core == 0, places[1], places[0])
        mine_rows = pl.ds(pl.multiple_of(16 * pair + 8 * core, 8), 8)
        other_rows = pl.ds(pl.multiple_of(16 * pair + 8 * (1 - core), 8), 8)
        keep_ref[mine, :taps] = kern_ref[:, mine_rows, :]
        keep_ref[mine, taps] = proj_ref[mine_rows, :]
        send_ref[other, :taps] = kern_ref[:, other_rows, :]
        send_ref[other, taps] = proj_ref[other_rows, :]


def unpack_kernel(scale, me_ref, mine_ref, other_ref, kern_ref, proj_ref):
    me = me_ref[0] & 15
    core = me & 1
    taps = kern_ref.shape[0]
    for pair in range(8):
        places = []
        for c in range(2):
            places.append(place_of((2 * pair) ^ (me & 14), ORDERS[c]))
        mine = jnp.where(core == 0, places[0], places[1])
        other = jnp.where(core == 0, places[1], places[0])
        mine_rows = pl.ds(pl.multiple_of(16 * pair + 8 * core, 8), 8)
        other_rows = pl.ds(pl.multiple_of(16 * pair + 8 * (1 - core), 8), 8)
        kern_ref[:, mine_rows, :] = mine_ref[mine, :taps].astype(jnp.float32) * scale
        proj_ref[mine_rows, :] = mine_ref[mine, taps].astype(jnp.float32) * scale
        kern_ref[:, other_rows, :] = other_ref[other, :taps].astype(jnp.float32) * scale
        proj_ref[other_rows, :] = other_ref[other, taps].astype(jnp.float32) * scale


def in_vmem(count):
    return [pl.BlockSpec(memory_space=pltpu.VMEM) for _ in range(count)]


def summed(kern_part, proj_part, scale):
    taps, chans, _ = kern_part.shape
    me = device_number().astype(jnp.int32).reshape(1)
    half = (8, taps + 1, 8, chans)
    keep, send = pl.pallas_call(
        pack_kernel,
        out_shape=(
            jax.ShapeDtypeStruct(half, jnp.float32),
            jax.ShapeDtypeStruct(half, jnp.float32),
        ),
        in_specs=[pl.BlockSpec(memory_space=pltpu.SMEM)] + in_vmem(2),
        out_specs=tuple(in_vmem(2)),
        name="pack",
    )(me, kern_part, proj_part)
    rounds = [tuple(order[k] for order in ORDERS) for k in range(3)]
    total = keep + swapped(send, (0, 0))
    for bits, link_type in zip(rounds, (jnp.bfloat16, jnp.bfloat16, jnp.float32)):
        rest = total.shape[0] // 2
        came = swapped(total[rest:].astype(link_type), bits)
        total = total[:rest] + came.astype(jnp.float32)
    count = lax.axis_size("dp") * lax.axis_size("tm")
    place = HALVINGS
    while (1 << place) < count:
        total = total + swapped(total, (place, place))
        place += 1
    total = total.astype(jnp.bfloat16)
    for bits in reversed(rounds):
        total = jnp.concatenate([total, swapped(total, bits)], axis=0)
    other = swapped(total, (0, 0))
    return pl.pallas_call(
        functools.partial(unpack_kernel, scale),
        out_shape=(
            jax.ShapeDtypeStruct(kern_part.shape, jnp.float32),
            jax.ShapeDtypeStruct(proj_part.shape, jnp.float32),
        ),
        in_specs=[pl.BlockSpec(memory_space=pltpu.SMEM)] + in_vmem(2),
        out_specs=tuple(in_vmem(2)),
        name="unpack",
    )(me, total, other)


def shards(clip_frames, out_grad, conv_kernel, proj_weight):
    frames = clip_frames[0]
    grads = out_grad[0]
    n_frames, height, width, chans = frames.shape
    rows = n_frames * height * width
    kern = conv_kernel.reshape(3, 9 * chans, chans)
    kern_flip = jnp.swapaxes(conv_kernel[:, ::-1, ::-1], 3, 4).reshape(3, 9 * chans, chans)
    cache = passed_along(frames, "tm", 1)
    patches = patches_of(jnp.concatenate([cache, frames], axis=0))
    pre = jnp.zeros((rows, chans), jnp.float32)
    for offset in range(3):
        pre = pre + jnp.dot(
            patches[offset : offset + n_frames].reshape(rows, 9 * chans),
            kern[offset],
            preferred_element_type=jnp.float32,
        )
    sig = jax.nn.sigmoid(pre)
    hidden = (pre * sig).astype(jnp.bfloat16)
    flat_grads = grads.reshape(rows, chans)
    mixed = (
        frames.reshape(rows, chans).astype(jnp.float32)
        + jnp.dot(hidden, proj_weight, preferred_element_type=jnp.float32)
    ).astype(jnp.bfloat16)
    proj_part = contract_rows(hidden, flat_grads)
    hidden_grad = lax.dot_general(
        flat_grads, proj_weight, (((1,), (1,)), ((), ())), preferred_element_type=jnp.float32
    )
    pre_grad = (hidden_grad * sig * (1.0 + pre * (1.0 - sig))).astype(jnp.bfloat16)
    kern_part = jnp.stack(
        [
            contract_rows(patches[offset : offset + n_frames].reshape(rows, 9 * chans), pre_grad)
            for offset in range(3)
        ]
    )
    grad_maps = pre_grad.reshape(n_frames, height, width, chans)
    extended = jnp.pad(grad_maps, ((2, 2), (0, 0), (0, 0), (0, 0)))
    ext_rows = (n_frames + 2) * height * width
    total = jnp.zeros((ext_rows, chans), jnp.float32)
    for offset in range(3):
        piece = patches_of(extended[2 - offset : 2 - offset + n_frames + 2]).reshape(
            ext_rows, 9 * chans
        )
        total = total + jnp.dot(piece, kern_flip[offset], preferred_element_type=jnp.float32)
    total = total.reshape(n_frames + 2, height, width, chans)
    arrived = passed_along(total[:2], "tm", -1)
    back = total[2:] + jnp.concatenate(
        [jnp.zeros((n_frames - 2, height, width, chans), jnp.float32), arrived], axis=0
    )
    back = back.reshape(rows, chans)
    input_grad = (flat_grads.astype(jnp.float32) + back).astype(jnp.bfloat16)
    total_pixels = (
        clip_frames.shape[0] * lax.axis_size("dp") * n_frames * lax.axis_size("tm") * height * width
    )
    scale = 1.0 / math.sqrt(total_pixels)
    kernel_grad, proj_grad = summed(
        kern_part.reshape(27, chans, chans), proj_part, scale
    )
    return (
        mixed.reshape(clip_frames.shape),
        input_grad.reshape(clip_frames.shape),
        kernel_grad.reshape(3, 3, 3, chans, chans),
        proj_grad,
    )


def solution(mesh):
    placed = (P("dp", "tm", None, None, None), P("dp", "tm", None, None, None), P(), P())
    return jax.shard_map(
        shards,
        mesh=mesh,
        in_specs=placed,
        out_specs=(P("dp", "tm", None, None, None), P("dp", "tm", None, None, None), P(), P()),
        check_vma=False,
    )
```

```python
import functools
import math

import jax
import jax.numpy as jnp
from jax import lax
from jax.experimental import pallas as pl
from jax.experimental.pallas import tpu as pltpu
from jax.sharding import PartitionSpec as P

AXES = ("dp", "tm")
HALVINGS = 4
ORDERS = ((1, 2, 3), (2, 3, 1))
UNPACK_CHUNK = 7
LIMIT = pltpu.CompilerParams(vmem_limit_bytes=16 * 1024 * 1024)
SCALAR = pl.BlockSpec(memory_space=pltpu.SMEM)
VECTOR = pl.BlockSpec(memory_space=pltpu.VMEM)
ANYWHERE = pl.BlockSpec(memory_space=pl.ANY)


def passed_along(shard, axis, by):
    size = lax.axis_size(axis)
    pairs = [(i, i + by) for i in range(size) if 0 <= i + by < size]
    return lax.ppermute(shard, axis, pairs)


def device_number():
    return lax.axis_index("dp") * lax.axis_size("tm") + lax.axis_index("tm")


def swapped(array, bits):
    count = lax.axis_size("dp") * lax.axis_size("tm")
    return lax.ppermute(array, AXES, [(i, i ^ (1 << bits[i & 1])) for i in range(count)])


def bit(number, place):
    return (number >> place) & 1


def places_of(me, pair):
    offset = (2 * pair) ^ (me & 14)
    first, second = (
        4 * bit(offset, order[0]) + 2 * bit(offset, order[1]) + bit(offset, order[2])
        for order in ORDERS
    )
    core = me & 1
    return jnp.where(core == 0, first, second), jnp.where(core == 0, second, first)


def beside(flat, width):
    rows = flat.shape[0]
    wide = flat.astype(jnp.float32)
    column = lax.broadcasted_iota(jnp.int32, flat.shape, 0) % width
    before = jnp.where(column == 0, 0.0, pltpu.roll(wide, 1, 0)).astype(flat.dtype)
    after = jnp.where(column == width - 1, 0.0, pltpu.roll(wide, rows - 1, 0)).astype(flat.dtype)
    return before, after


def moved_rows(flat, map_rows, width, by):
    zero = jnp.zeros((width, flat.shape[1]), flat.dtype)
    pieces = []
    for start in range(0, flat.shape[0], map_rows):
        whole = flat[start : start + map_rows]
        pieces += [zero, whole[:-width]] if by == 1 else [whole[width:], zero]
    return jnp.concatenate(pieces, axis=0)


def dot(left, right, contract):
    return lax.dot_general(
        left, right, ((contract[:1], contract[1:]), ((), ())), preferred_element_type=jnp.float32
    )


def forward_kernel(
    shape, me_ref, halo_ref, frames_ref, grads_ref, kern_ref, proj_ref,
    keep_ref, send_ref, hidden_ref, pre_grad_ref, wide_ref,
):
    _, height, width, chans = shape
    map_rows = height * width
    rows = shape[0] * map_rows
    halo_rows = 2 * map_rows
    for ref, start in ((halo_ref, 0), (frames_ref, halo_rows)):
        flat = ref[...]
        before, after = beside(flat, width)
        here = slice(start, start + flat.shape[0])
        wide_ref[here, :chans] = before
        wide_ref[here, chans : 2 * chans] = flat
        wide_ref[here, 2 * chans :] = after
    sums = None
    for tau in range(3):
        weights = jnp.concatenate(
            [kern_ref[tau, row].reshape(3 * chans, chans) for row in range(3)], axis=1
        )
        term = dot(wide_ref[tau * map_rows : tau * map_rows + rows], weights, (1, 0))
        sums = term if sums is None else sums + term
    pre = (
        moved_rows(sums[:, :chans], map_rows, width, 1)
        + sums[:, chans : 2 * chans]
        + moved_rows(sums[:, 2 * chans :], map_rows, width, -1)
    )
    sig = jax.nn.sigmoid(pre)
    hidden = (pre * sig).astype(jnp.bfloat16)
    grads = grads_ref[...]
    hidden_grad = dot(grads, proj_ref[...], (1, 1))
    pre_grad = (hidden_grad * sig * (1.0 + pre * (1.0 - sig))).astype(jnp.bfloat16)
    hidden_ref[...] = hidden
    pre_grad_ref[...] = pre_grad
    me = me_ref[0]
    core = me & 1
    places = [places_of(me, pair) for pair in range(8)]

    def put(tap, value):
        for pair in range(8):
            even = value[16 * pair : 16 * pair + 8]
            odd = value[16 * pair + 8 : 16 * pair + 16]
            mine, other = places[pair]
            keep_ref[mine, tap] = jnp.where(core == 0, even, odd)
            send_ref[other, tap] = jnp.where(core == 0, odd, even).astype(send_ref.dtype)

    put(27, dot(hidden, grads, (0, 0)))
    grad_rows = jnp.concatenate(
        [
            moved_rows(pre_grad, map_rows, width, -1),
            pre_grad,
            moved_rows(pre_grad, map_rows, width, 1),
        ],
        axis=1,
    )
    for tau in range(3):
        part = dot(wide_ref[tau * map_rows : tau * map_rows + rows], grad_rows, (0, 0))
        for row in range(3):
            for col in range(3):
                put(
                    tau * 9 + row * 3 + col,
                    part[col * chans : (col + 1) * chans, row * chans : (row + 1) * chans],
                )


def backward_kernel(
    shape, pre_grad_ref, next_ref, hidden_ref, frames_ref, grads_ref, kern_ref, proj_ref,
    mixed_ref, input_grad_ref, wide_ref,
):
    _, height, width, chans = shape
    map_rows = height * width
    rows = shape[0] * map_rows
    for ref, start in ((pre_grad_ref, 0), (next_ref, rows)):
        flat = ref[...]
        before, after = beside(flat, width)
        here = slice(start, start + flat.shape[0])
        wide_ref[here, :chans] = after
        wide_ref[here, chans : 2 * chans] = flat
        wide_ref[here, 2 * chans :] = before
    sums = None
    for tau in range(3):
        weights = jnp.concatenate(
            [kern_ref[tau, :, col].reshape(3 * chans, chans) for col in range(3)], axis=1
        )
        start = (2 - tau) * map_rows
        term = dot(wide_ref[start : start + rows], weights, (1, 1))
        sums = term if sums is None else sums + term
    back = (
        moved_rows(sums[:, :chans], map_rows, width, -1)
        + sums[:, chans : 2 * chans]
        + moved_rows(sums[:, 2 * chans :], map_rows, width, 1)
    )
    input_grad_ref[...] = (grads_ref[...].astype(jnp.float32) + back).astype(jnp.bfloat16)
    mixed_ref[...] = (
        frames_ref[...].astype(jnp.float32) + dot(hidden_ref[...], proj_ref[...], (1, 0))
    ).astype(jnp.bfloat16)


def unpack_kernel(scale, me_ref, mine_ref, other_ref, kern_ref, proj_ref, out_ref, sems):
    me = me_ref[0]
    core = me & 1
    taps = kern_ref.shape[0]
    copies = []
    for first in range(0, taps + 1, UNPACK_CHUNK):
        last = min(first + UNPACK_CHUNK, taps + 1)
        for pair in range(8):
            mine, other = places_of(me, pair)
            mine_rows = pl.ds(pl.multiple_of(16 * pair + 8 * core, 8), 8)
            other_rows = pl.ds(pl.multiple_of(16 * pair + 8 * (1 - core), 8), 8)
            out_ref[first:last, mine_rows, :] = (
                mine_ref[mine, first:last].astype(jnp.float32) * scale
            )
            out_ref[first:last, other_rows, :] = (
                other_ref[other, first:last].astype(jnp.float32) * scale
            )
        inside = min(last, taps)
        copies.append(
            pltpu.make_async_copy(
                out_ref.at[first:inside], kern_ref.at[first:inside], sems.at[len(copies)]
            )
        )
        copies[-1].start()
    copies.append(pltpu.make_async_copy(out_ref.at[taps], proj_ref, sems.at[len(copies)]))
    copies[-1].start()
    for copy in copies:
        copy.wait()


def summed(me, keep, send, scale):
    taps, chans = keep.shape[1] - 1, keep.shape[3]
    rounds = [tuple(order[k] for order in ORDERS) for k in range(3)]
    total = keep + swapped(send, (0, 0)).astype(jnp.float32)
    for bits, link_type in zip(rounds, (jnp.bfloat16, jnp.bfloat16, jnp.float32)):
        rest = total.shape[0] // 2
        came = swapped(total[rest:].astype(link_type), bits)
        total = total[:rest] + came.astype(jnp.float32)
    count = lax.axis_size("dp") * lax.axis_size("tm")
    place = HALVINGS
    while (1 << place) < count:
        total = total + swapped(total, (place, place))
        place += 1
    total = total.astype(jnp.bfloat16)
    for bits in reversed(rounds):
        total = jnp.concatenate([total, swapped(total, bits)], axis=0)
    other = swapped(total, (0, 0))
    return pl.pallas_call(
        functools.partial(unpack_kernel, scale),
        out_shape=(
            jax.ShapeDtypeStruct((taps, chans, chans), jnp.float32),
            jax.ShapeDtypeStruct((chans, chans), jnp.float32),
        ),
        in_specs=[SCALAR, VECTOR, VECTOR],
        out_specs=(ANYWHERE, ANYWHERE),
        scratch_shapes=[
            pltpu.VMEM((taps + 1, chans, chans), jnp.float32),
            pltpu.SemaphoreType.DMA((pl.cdiv(taps + 1, UNPACK_CHUNK) + 1,)),
        ],
        compiler_params=LIMIT,
        name="unpack",
    )(me, total, other)


def forward(shape, me, halo, frames, grads, conv_kernel, proj_weight):
    n_frames, height, width, chans = shape
    rows = n_frames * height * width
    half = (8, 28, 8, chans)
    return pl.pallas_call(
        functools.partial(forward_kernel, shape),
        out_shape=(
            jax.ShapeDtypeStruct(half, jnp.float32),
            jax.ShapeDtypeStruct(half, jnp.float32),
            jax.ShapeDtypeStruct((rows, chans), jnp.bfloat16),
            jax.ShapeDtypeStruct((rows, chans), jnp.bfloat16),
        ),
        in_specs=[SCALAR] + [VECTOR] * 5,
        out_specs=(VECTOR,) * 4,
        scratch_shapes=[pltpu.VMEM((rows + 2 * height * width, 3 * chans), jnp.bfloat16)],
        compiler_params=LIMIT,
        name="forward",
    )(me, halo, frames, grads, conv_kernel, proj_weight)


def backward(shape, pre_grad, following, hidden, frames, grads, conv_kernel, proj_weight):
    n_frames, height, width, chans = shape
    rows = n_frames * height * width
    flops = 2 * rows * 28 * chans * chans
    return pl.pallas_call(
        functools.partial(backward_kernel, shape),
        out_shape=(jax.ShapeDtypeStruct((rows, chans), jnp.bfloat16),) * 2,
        in_specs=[VECTOR] * 7,
        out_specs=(VECTOR,) * 2,
        scratch_shapes=[pltpu.VMEM((rows + 2 * height * width, 3 * chans), jnp.bfloat16)],
        compiler_params=LIMIT,
        cost_estimate=pl.CostEstimate(flops=flops, bytes_accessed=1 << 20, transcendentals=0),
        name="backward",
    )(pre_grad, following, hidden, frames, grads, conv_kernel, proj_weight)


def shards(clip_frames, out_grad, conv_kernel, proj_weight):
    shape = clip_frames.shape[1:]
    n_frames, height, width, chans = shape
    rows = n_frames * height * width
    halo_rows = 2 * height * width
    frames = clip_frames.reshape(rows, chans)
    grads = out_grad.reshape(rows, chans)
    me = device_number().astype(jnp.int32).reshape(1)
    halo = passed_along(frames[rows - halo_rows :], "tm", 1)
    keep, send, hidden, pre_grad = forward(
        shape, me, halo, frames, grads, conv_kernel, proj_weight
    )
    following = passed_along(pre_grad[:halo_rows], "tm", -1)
    mixed, input_grad = backward(
        shape, pre_grad, following, hidden, frames, grads, conv_kernel, proj_weight
    )
    total_pixels = lax.axis_size("dp") * lax.axis_size("tm") * rows
    kernel_grad, proj_grad = summed(me, keep, send, 1.0 / math.sqrt(total_pixels))
    return (
        mixed.reshape(clip_frames.shape),
        input_grad.reshape(clip_frames.shape),
        kernel_grad.reshape(conv_kernel.shape),
        proj_grad,
    )


def solution(mesh):
    placed = (P("dp", "tm", None, None, None), P("dp", "tm", None, None, None), P(), P())
    return jax.shard_map(
        shards,
        mesh=mesh,
        in_specs=placed,
        out_specs=(P("dp", "tm", None, None, None), P("dp", "tm", None, None, None), P(), P()),
        check_vma=False,
    )
```

```python
import functools
import math

import jax
import jax.numpy as jnp
from jax import lax
from jax.experimental import pallas as pl
from jax.experimental.pallas import tpu as pltpu
from jax.sharding import PartitionSpec as P

AXES = ("dp", "tm")
ORDERS = ((1, 2, 3, 4), (2, 3, 4, 1))
UNPACK_CHUNK = 7
LIMIT = pltpu.CompilerParams(vmem_limit_bytes=16 * 1024 * 1024)
SCALAR = pl.BlockSpec(memory_space=pltpu.SMEM)
VECTOR = pl.BlockSpec(memory_space=pltpu.VMEM)
OUTSIDE = pl.BlockSpec(memory_space=pltpu.HBM)


def passed_along(shard, axis, by):
    size = lax.axis_size(axis)
    pairs = [(i, i + by) for i in range(size) if 0 <= i + by < size]
    return lax.ppermute(shard, axis, pairs)


def device_number():
    return lax.axis_index("dp") * lax.axis_size("tm") + lax.axis_index("tm")


def swapped(array, bits):
    count = lax.axis_size("dp") * lax.axis_size("tm")
    return lax.ppermute(array, AXES, [(i, i ^ (1 << bits[i & 1])) for i in range(count)])


def halves_of(me):
    first, second = (
        4 * ((me >> order[0]) & 1) + 2 * ((me >> order[1]) & 1) + ((me >> order[2]) & 1)
        for order in ORDERS
    )
    core = me & 1
    return jnp.where(core == 0, first, second), jnp.where(core == 0, second, first)


def beside(flat, width):
    rows = flat.shape[0]
    wide = flat.astype(jnp.float32)
    column = lax.broadcasted_iota(jnp.int32, flat.shape, 0) % width
    before = jnp.where(column == 0, 0.0, pltpu.roll(wide, 1, 0)).astype(flat.dtype)
    after = jnp.where(column == width - 1, 0.0, pltpu.roll(wide, rows - 1, 0)).astype(flat.dtype)
    return before, after


def moved_rows(flat, map_rows, width, by):
    zero = jnp.zeros((width, flat.shape[1]), flat.dtype)
    pieces = []
    for start in range(0, flat.shape[0], map_rows):
        whole = flat[start : start + map_rows]
        pieces += [zero, whole[:-width]] if by == 1 else [whole[width:], zero]
    return jnp.concatenate(pieces, axis=0)


def dot(left, right, contract):
    return lax.dot_general(
        left, right, ((contract[:1], contract[1:]), ((), ())), preferred_element_type=jnp.float32
    )


def spread(flat, width, wide_ref, flipped=False):
    chans = flat.shape[1]
    before, after = beside(flat, width)
    wide_ref[:, :chans] = after if flipped else before
    wide_ref[:, chans : 2 * chans] = flat
    wide_ref[:, 2 * chans :] = before if flipped else after


def weights_of(kern_ref, tau):
    chans = kern_ref.shape[-1]
    return jnp.concatenate(
        [kern_ref[tau, row].reshape(3 * chans, chans) for row in range(3)], axis=1
    )


def prepare_kernel(
    shape, frames_hbm, grads_hbm, kern_hbm, proj_hbm,
    frames_ref, grads_ref, kern_ref, proj_ref, wide_ref, sums_ref, hidden_grad_ref, sems,
):
    _, height, width, chans = shape
    map_rows = height * width
    rows = shape[0] * map_rows
    pairs = (
        (frames_hbm, frames_ref), (kern_hbm, kern_ref), (grads_hbm, grads_ref), (proj_hbm, proj_ref)
    )
    copies = [pltpu.make_async_copy(*pair, sems.at[i]) for i, pair in enumerate(pairs)]
    for copy in copies:
        copy.start()
    copies[0].wait()
    spread(frames_ref[...], width, wide_ref)
    copies[1].wait()
    sums_ref[...] = dot(wide_ref[...], weights_of(kern_ref, 2), (1, 0))
    for tau in range(2):
        skip = (2 - tau) * map_rows
        if skip < rows:
            sums_ref[skip:] += dot(wide_ref[: rows - skip], weights_of(kern_ref, tau), (1, 0))
    copies[2].wait()
    copies[3].wait()
    hidden_grad_ref[...] = dot(grads_ref[...], proj_ref[...], (1, 1))


def forward_kernel(
    shape, me_ref, halo_ref, grads_ref, kern_ref, own_ref, sums_ref, hidden_grad_ref,
    keep_ref, send_ref, hidden_ref, pre_grad_ref, wide_ref,
):
    _, height, width, chans = shape
    map_rows = height * width
    rows = shape[0] * map_rows
    spread(halo_ref[...], width, wide_ref)
    term = dot(wide_ref[...], weights_of(kern_ref, 0), (1, 0))
    early = dot(wide_ref[map_rows:], weights_of(kern_ref, 1), (1, 0))
    head = jnp.concatenate([term[:map_rows] + early, term[map_rows:]], axis=0)
    sums = sums_ref[...]
    if rows > 2 * map_rows:
        sums = jnp.concatenate(
            [sums[: 2 * map_rows] + head, sums[2 * map_rows :]], axis=0
        )
    else:
        sums = sums + head
    pre = (
        moved_rows(sums[:, :chans], map_rows, width, 1)
        + sums[:, chans : 2 * chans]
        + moved_rows(sums[:, 2 * chans :], map_rows, width, -1)
    )
    sig = jax.nn.sigmoid(pre)
    hidden = (pre * sig).astype(jnp.bfloat16)
    grads = grads_ref[...]
    pre_grad = (hidden_grad_ref[...] * sig * (1.0 + pre * (1.0 - sig))).astype(jnp.bfloat16)
    hidden_ref[...] = hidden
    pre_grad_ref[...] = pre_grad
    me = me_ref[0]
    core = me & 1
    mine, other = halves_of(me)

    def put(tap, value):
        for block in range(8):
            even = value[16 * block : 16 * block + 8]
            odd = value[16 * block + 8 : 16 * block + 16]
            keep_ref[block ^ mine, tap] = jnp.where(core == 0, even, odd)
            send_ref[block ^ other, tap] = jnp.where(core == 0, odd, even)

    put(27, dot(hidden, grads, (0, 0)))
    grad_rows = jnp.concatenate(
        [
            moved_rows(pre_grad, map_rows, width, -1),
            pre_grad,
            moved_rows(pre_grad, map_rows, width, 1),
        ],
        axis=1,
    )
    for tau in range(3):
        skip = (2 - tau) * map_rows
        part = dot(own_ref[: rows - skip], grad_rows[skip:], (0, 0)) if skip < rows else None
        if skip:
            term = dot(wide_ref[tau * map_rows :], grad_rows[:skip], (0, 0))
            part = term if part is None else part + term
        for row in range(3):
            for col in range(3):
                put(
                    tau * 9 + row * 3 + col,
                    part[col * chans : (col + 1) * chans, row * chans : (row + 1) * chans],
                )


def backward_kernel(
    shape, pre_grad_ref, next_ref, hidden_ref, frames_ref, grads_ref, kern_ref, proj_ref,
    mixed_ref, input_grad_ref, wide_ref,
):
    _, height, width, chans = shape
    map_rows = height * width
    rows = shape[0] * map_rows
    spread(pre_grad_ref[...], width, wide_ref.at[:rows], flipped=True)
    spread(next_ref[...], width, wide_ref.at[rows:], flipped=True)
    sums = None
    for tau in range(3):
        weights = jnp.concatenate(
            [kern_ref[tau, :, col].reshape(3 * chans, chans) for col in range(3)], axis=1
        )
        start = (2 - tau) * map_rows
        term = dot(wide_ref[start : start + rows], weights, (1, 1))
        sums = term if sums is None else sums + term
    back = (
        moved_rows(sums[:, :chans], map_rows, width, -1)
        + sums[:, chans : 2 * chans]
        + moved_rows(sums[:, 2 * chans :], map_rows, width, 1)
    )
    input_grad_ref[...] = (grads_ref[...].astype(jnp.float32) + back).astype(jnp.bfloat16)
    mixed_ref[...] = (
        frames_ref[...].astype(jnp.float32) + dot(hidden_ref[...], proj_ref[...], (1, 0))
    ).astype(jnp.bfloat16)


def unpack_kernel(scale, me_ref, mine_ref, other_ref, kern_ref, proj_ref, out_ref, sems):
    me = me_ref[0]
    core = me & 1
    mine, other = halves_of(me)
    taps = kern_ref.shape[0]
    copies = []
    for first in range(0, taps + 1, UNPACK_CHUNK):
        last = min(first + UNPACK_CHUNK, taps + 1)
        for block in range(8):
            mine_rows = pl.ds(pl.multiple_of(16 * block + 8 * core, 8), 8)
            other_rows = pl.ds(pl.multiple_of(16 * block + 8 * (1 - core), 8), 8)
            out_ref[first:last, mine_rows, :] = (
                mine_ref[block ^ mine, first:last].astype(jnp.float32) * scale
            )
            out_ref[first:last, other_rows, :] = (
                other_ref[block ^ other, first:last].astype(jnp.float32) * scale
            )
        inside = min(last, taps)
        copies.append(
            pltpu.make_async_copy(
                out_ref.at[first:inside], kern_ref.at[first:inside], sems.at[len(copies)]
            )
        )
        copies[-1].start()
    copies.append(pltpu.make_async_copy(out_ref.at[taps], proj_ref, sems.at[len(copies)]))
    copies[-1].start()
    for copy in copies:
        copy.wait()


def summed(me, keep, send, scale, beside_second, beside_third):
    taps, chans = keep.shape[1] - 1, keep.shape[3]
    rounds = [tuple(order[k] for order in ORDERS) for k in range(4)]
    total = keep + swapped(send, (0, 0))
    done = ()
    for bits, link_type, work in zip(
        rounds[:3],
        (jnp.bfloat16, jnp.bfloat16, jnp.float32),
        (lambda nothing: nothing, beside_second, beside_third),
    ):
        rest = total.shape[0] // 2
        done = work(done)
        total, done = lax.optimization_barrier((total, done))
        came = swapped(total[rest:].astype(link_type), bits)
        total = total[:rest] + came.astype(jnp.float32)
    total = total + swapped(total, rounds[3])
    count = lax.axis_size("dp") * lax.axis_size("tm")
    place = 1 + len(rounds)
    while (1 << place) < count:
        total = total + swapped(total, (place, place))
        place += 1
    total = total.astype(jnp.bfloat16)
    for bits in reversed(rounds[:3]):
        total = jnp.concatenate([total, swapped(total, bits)], axis=0)
    other = swapped(total, (0, 0))
    return pl.pallas_call(
        functools.partial(unpack_kernel, scale),
        out_shape=(
            jax.ShapeDtypeStruct((taps, chans, chans), jnp.float32),
            jax.ShapeDtypeStruct((chans, chans), jnp.float32),
        ),
        in_specs=[SCALAR, VECTOR, VECTOR],
        out_specs=(OUTSIDE, OUTSIDE),
        scratch_shapes=[
            pltpu.VMEM((taps + 1, chans, chans), jnp.float32),
            pltpu.SemaphoreType.DMA((pl.cdiv(taps + 1, UNPACK_CHUNK) + 1,)),
        ],
        compiler_params=LIMIT,
        name="unpack",
    )(me, total, other), done


def prepare(shape, frames, grads, conv_kernel, proj_weight):
    n_frames, height, width, chans = shape
    rows = n_frames * height * width
    return pl.pallas_call(
        functools.partial(prepare_kernel, shape),
        out_shape=(
            jax.ShapeDtypeStruct(frames.shape, frames.dtype),
            jax.ShapeDtypeStruct(grads.shape, grads.dtype),
            jax.ShapeDtypeStruct(conv_kernel.shape, conv_kernel.dtype),
            jax.ShapeDtypeStruct(proj_weight.shape, proj_weight.dtype),
            jax.ShapeDtypeStruct((rows, 3 * chans), jnp.bfloat16),
            jax.ShapeDtypeStruct((rows, 3 * chans), jnp.float32),
            jax.ShapeDtypeStruct((rows, chans), jnp.float32),
        ),
        in_specs=[OUTSIDE] * 4,
        out_specs=(VECTOR,) * 7,
        scratch_shapes=[pltpu.SemaphoreType.DMA((4,))],
        compiler_params=LIMIT,
        cost_estimate=pl.CostEstimate(
            flops=2 * rows * 20 * chans * chans, bytes_accessed=1 << 20, transcendentals=0
        ),
        name="prepare",
    )(*(pltpu.with_memory_space_constraint(x, pltpu.HBM) for x in (frames, grads, conv_kernel, proj_weight)))


def forward(shape, me, halo, grads, conv_kernel, own, sums, hidden_grad):
    n_frames, height, width, chans = shape
    rows = n_frames * height * width
    half = (8, 28, 8, chans)
    return pl.pallas_call(
        functools.partial(forward_kernel, shape),
        out_shape=(
            jax.ShapeDtypeStruct(half, jnp.float32),
            jax.ShapeDtypeStruct(half, jnp.float32),
            jax.ShapeDtypeStruct((rows, chans), jnp.bfloat16),
            jax.ShapeDtypeStruct((rows, chans), jnp.bfloat16),
        ),
        in_specs=[SCALAR] + [VECTOR] * 6,
        out_specs=(VECTOR,) * 4,
        scratch_shapes=[pltpu.VMEM((2 * height * width, 3 * chans), jnp.bfloat16)],
        compiler_params=LIMIT,
        name="forward",
    )(me, halo, grads, conv_kernel, own, sums, hidden_grad)


def backward(shape, pre_grad, following, hidden, frames, grads, conv_kernel, proj_weight):
    n_frames, height, width, chans = shape
    rows = n_frames * height * width
    flops = 2 * rows * 28 * chans * chans
    return pl.pallas_call(
        functools.partial(backward_kernel, shape),
        out_shape=(jax.ShapeDtypeStruct((rows, chans), jnp.bfloat16),) * 2,
        in_specs=[VECTOR] * 7,
        out_specs=(VECTOR,) * 2,
        scratch_shapes=[pltpu.VMEM((rows + 2 * height * width, 3 * chans), jnp.bfloat16)],
        compiler_params=LIMIT,
        cost_estimate=pl.CostEstimate(flops=flops, bytes_accessed=1 << 20, transcendentals=0),
        name="backward",
    )(pre_grad, following, hidden, frames, grads, conv_kernel, proj_weight)


def shards(clip_frames, out_grad, conv_kernel, proj_weight):
    shape = clip_frames.shape[1:]
    n_frames, height, width, chans = shape
    rows = n_frames * height * width
    halo_rows = 2 * height * width
    frames = clip_frames.reshape(rows, chans)
    grads = out_grad.reshape(rows, chans)
    me = device_number().astype(jnp.int32).reshape(1)
    halo = passed_along(frames[rows - halo_rows :], "tm", 1)
    frames, grads, conv_kernel, proj_weight, own, sums, hidden_grad = prepare(
        shape, frames, grads, conv_kernel, proj_weight
    )
    keep, send, hidden, pre_grad = forward(
        shape, me, halo, grads, conv_kernel, own, sums, hidden_grad
    )
    total_pixels = lax.axis_size("dp") * lax.axis_size("tm") * rows
    (kernel_grad, proj_grad), (mixed, input_grad) = summed(
        me,
        keep,
        send,
        1.0 / math.sqrt(total_pixels),
        lambda _: passed_along(pre_grad[:halo_rows], "tm", -1),
        lambda following: backward(
            shape, pre_grad, following, hidden, frames, grads, conv_kernel, proj_weight
        ),
    )
    return (
        mixed.reshape(clip_frames.shape),
        input_grad.reshape(clip_frames.shape),
        kernel_grad.reshape(conv_kernel.shape),
        proj_grad,
    )


def solution(mesh):
    placed = (P("dp", "tm", None, None, None), P("dp", "tm", None, None, None), P(), P())
    return jax.shard_map(
        shards,
        mesh=mesh,
        in_specs=placed,
        out_specs=(P("dp", "tm", None, None, None), P("dp", "tm", None, None, None), P(), P()),
        check_vma=False,
    )
```

```python
import functools
import math

import jax
import jax.numpy as jnp
from jax import lax
from jax.experimental import pallas as pl
from jax.experimental.pallas import tpu as pltpu
from jax.sharding import PartitionSpec as P

AXES = ("dp", "tm")
PAIRS = (((1, 2), (3, 4)), ((3, 4), (1, 2)))
UNPACK_CHUNK = 7
LIMIT = pltpu.CompilerParams(vmem_limit_bytes=16 * 1024 * 1024)
SCALAR = pl.BlockSpec(memory_space=pltpu.SMEM)
VECTOR = pl.BlockSpec(memory_space=pltpu.VMEM)
OUTSIDE = pl.BlockSpec(memory_space=pltpu.HBM)


def passed_along(shard, axis, by):
    size = lax.axis_size(axis)
    pairs = [(i, i + by) for i in range(size) if 0 <= i + by < size]
    return lax.ppermute(shard, axis, pairs)


def device_number():
    return lax.axis_index("dp") * lax.axis_size("tm") + lax.axis_index("tm")


def swapped(array, masks):
    count = lax.axis_size("dp") * lax.axis_size("tm")
    return lax.ppermute(array, AXES, [(i, i ^ masks[i & 1]) for i in range(count)])


def masks_of(stage, offset):
    return tuple(
        (offset >> 1) << pairs[stage][0] | (offset & 1) << pairs[stage][1] for pairs in PAIRS
    )


def halves_of(me):
    first, second = (4 * ((me >> split[0]) & 1) + 2 * ((me >> split[1]) & 1) for split, _ in PAIRS)
    core = me & 1
    return jnp.where(core == 0, first, second), jnp.where(core == 0, second, first)


def beside(flat, width):
    rows = flat.shape[0]
    wide = flat.astype(jnp.float32)
    column = lax.broadcasted_iota(jnp.int32, flat.shape, 0) % width
    before = jnp.where(column == 0, 0.0, pltpu.roll(wide, 1, 0)).astype(flat.dtype)
    after = jnp.where(column == width - 1, 0.0, pltpu.roll(wide, rows - 1, 0)).astype(flat.dtype)
    return before, after


def moved_rows(flat, map_rows, width, by):
    zero = jnp.zeros((width, flat.shape[1]), flat.dtype)
    pieces = []
    for start in range(0, flat.shape[0], map_rows):
        whole = flat[start : start + map_rows]
        pieces += [zero, whole[:-width]] if by == 1 else [whole[width:], zero]
    return jnp.concatenate(pieces, axis=0)


def dot(left, right, contract):
    return lax.dot_general(
        left, right, ((contract[:1], contract[1:]), ((), ())), preferred_element_type=jnp.float32
    )


def spread(flat, width, wide_ref, flipped=False):
    chans = flat.shape[1]
    before, after = beside(flat, width)
    wide_ref[:, :chans] = after if flipped else before
    wide_ref[:, chans : 2 * chans] = flat
    wide_ref[:, 2 * chans :] = before if flipped else after


def weights_of(kern_ref, tau):
    chans = kern_ref.shape[-1]
    return jnp.concatenate(
        [kern_ref[tau, row].reshape(3 * chans, chans) for row in range(3)], axis=1
    )


def prepare_kernel(
    shape, frames_hbm, grads_hbm, kern_hbm, proj_hbm,
    frames_ref, grads_ref, kern_ref, proj_ref, wide_ref, sums_ref, hidden_grad_ref, sems,
):
    _, height, width, chans = shape
    map_rows = height * width
    rows = shape[0] * map_rows
    pairs = (
        (frames_hbm, frames_ref), (kern_hbm, kern_ref), (grads_hbm, grads_ref), (proj_hbm, proj_ref)
    )
    copies = [pltpu.make_async_copy(*pair, sems.at[i]) for i, pair in enumerate(pairs)]
    for copy in copies:
        copy.start()
    copies[0].wait()
    spread(frames_ref[...], width, wide_ref)
    copies[1].wait()
    sums_ref[...] = dot(wide_ref[...], weights_of(kern_ref, 2), (1, 0))
    for tau in range(2):
        skip = (2 - tau) * map_rows
        if skip < rows:
            sums_ref[skip:] += dot(wide_ref[: rows - skip], weights_of(kern_ref, tau), (1, 0))
    copies[2].wait()
    copies[3].wait()
    hidden_grad_ref[...] = dot(grads_ref[...], proj_ref[...], (1, 1))


def forward_kernel(
    shape, me_ref, halo_ref, grads_ref, kern_ref, own_ref, sums_ref, hidden_grad_ref,
    keep_ref, send_ref, hidden_ref, pre_grad_ref, wide_ref,
):
    _, height, width, chans = shape
    map_rows = height * width
    rows = shape[0] * map_rows
    spread(halo_ref[...], width, wide_ref)
    term = dot(wide_ref[...], weights_of(kern_ref, 0), (1, 0))
    early = dot(wide_ref[map_rows:], weights_of(kern_ref, 1), (1, 0))
    head = jnp.concatenate([term[:map_rows] + early, term[map_rows:]], axis=0)
    sums = sums_ref[...]
    if rows > 2 * map_rows:
        sums = jnp.concatenate(
            [sums[: 2 * map_rows] + head, sums[2 * map_rows :]], axis=0
        )
    else:
        sums = sums + head
    pre = (
        moved_rows(sums[:, :chans], map_rows, width, 1)
        + sums[:, chans : 2 * chans]
        + moved_rows(sums[:, 2 * chans :], map_rows, width, -1)
    )
    sig = jax.nn.sigmoid(pre)
    hidden = (pre * sig).astype(jnp.bfloat16)
    grads = grads_ref[...]
    pre_grad = (hidden_grad_ref[...] * sig * (1.0 + pre * (1.0 - sig))).astype(jnp.bfloat16)
    hidden_ref[...] = hidden
    pre_grad_ref[...] = pre_grad
    me = me_ref[0]
    core = me & 1
    mine, other = halves_of(me)

    def put(tap, value):
        for block in range(8):
            even = value[16 * block : 16 * block + 8]
            odd = value[16 * block + 8 : 16 * block + 16]
            keep_ref[block ^ mine, tap] = jnp.where(core == 0, even, odd)
            send_ref[block ^ other, tap] = jnp.where(core == 0, odd, even)

    put(27, dot(hidden, grads, (0, 0)))
    grad_rows = jnp.concatenate(
        [
            moved_rows(pre_grad, map_rows, width, -1),
            pre_grad,
            moved_rows(pre_grad, map_rows, width, 1),
        ],
        axis=1,
    )
    for tau in range(3):
        skip = (2 - tau) * map_rows
        part = dot(own_ref[: rows - skip], grad_rows[skip:], (0, 0)) if skip < rows else None
        if skip:
            term = dot(wide_ref[tau * map_rows :], grad_rows[:skip], (0, 0))
            part = term if part is None else part + term
        for row in range(3):
            for col in range(3):
                put(
                    tau * 9 + row * 3 + col,
                    part[col * chans : (col + 1) * chans, row * chans : (row + 1) * chans],
                )


def backward_kernel(
    shape, pre_grad_ref, next_ref, hidden_ref, frames_ref, grads_ref, kern_ref, proj_ref,
    mixed_ref, input_grad_ref, wide_ref,
):
    _, height, width, chans = shape
    map_rows = height * width
    rows = shape[0] * map_rows
    spread(pre_grad_ref[...], width, wide_ref.at[:rows], flipped=True)
    spread(next_ref[...], width, wide_ref.at[rows:], flipped=True)
    sums = None
    for tau in range(3):
        weights = jnp.concatenate(
            [kern_ref[tau, :, col].reshape(3 * chans, chans) for col in range(3)], axis=1
        )
        start = (2 - tau) * map_rows
        term = dot(wide_ref[start : start + rows], weights, (1, 1))
        sums = term if sums is None else sums + term
    back = (
        moved_rows(sums[:, :chans], map_rows, width, -1)
        + sums[:, chans : 2 * chans]
        + moved_rows(sums[:, 2 * chans :], map_rows, width, 1)
    )
    input_grad_ref[...] = (grads_ref[...].astype(jnp.float32) + back).astype(jnp.bfloat16)
    mixed_ref[...] = (
        frames_ref[...].astype(jnp.float32) + dot(hidden_ref[...], proj_ref[...], (1, 0))
    ).astype(jnp.bfloat16)


def unpack_kernel(scale, me_ref, mine_ref, other_ref, kern_ref, proj_ref, out_ref, sems):
    me = me_ref[0]
    core = me & 1
    mine, other = halves_of(me)
    taps = kern_ref.shape[0]
    copies = []
    for first in range(0, taps + 1, UNPACK_CHUNK):
        last = min(first + UNPACK_CHUNK, taps + 1)
        for block in range(8):
            mine_rows = pl.ds(pl.multiple_of(16 * block + 8 * core, 8), 8)
            other_rows = pl.ds(pl.multiple_of(16 * block + 8 * (1 - core), 8), 8)
            out_ref[first:last, mine_rows, :] = (
                mine_ref[block ^ mine, first:last].astype(jnp.float32) * scale
            )
            out_ref[first:last, other_rows, :] = (
                other_ref[block ^ other, first:last].astype(jnp.float32) * scale
            )
        inside = min(last, taps)
        copies.append(
            pltpu.make_async_copy(
                out_ref.at[first:inside], kern_ref.at[first:inside], sems.at[len(copies)]
            )
        )
        copies[-1].start()
    copies.append(pltpu.make_async_copy(out_ref.at[taps], proj_ref, sems.at[len(copies)]))
    copies[-1].start()
    for copy in copies:
        copy.wait()


def summed(me, keep, send, scale, beside_split, beside_exchange):
    taps, chans = keep.shape[1] - 1, keep.shape[3]
    total = keep + swapped(send, (1, 1))
    part = total.shape[0] // 4
    came = [
        swapped(total[offset * part : (offset + 1) * part].astype(jnp.bfloat16), masks_of(0, offset))
        for offset in (3, 2, 1)
    ]
    total = total[:part]
    for piece in came:
        total = total + piece.astype(jnp.float32)
    done = beside_split()
    total, done = lax.optimization_barrier((total, done))
    total = lax.reduce_precision(total, 8, 7)
    third, second, first = (
        swapped(total.astype(jnp.bfloat16), masks_of(1, offset)).astype(jnp.float32)
        for offset in (3, 2, 1)
    )
    total = (total + first) + (second + third)
    count = lax.axis_size("dp") * lax.axis_size("tm")
    mask = 1 << (1 + sum(len(pair) for pair in PAIRS[0]))
    while mask < count:
        total = total + swapped(total, (mask, mask))
        mask *= 2
    done = beside_exchange(done)
    total = total.astype(jnp.bfloat16)
    total, done = lax.optimization_barrier((total, done))
    third, second, first = (swapped(total, masks_of(0, offset)) for offset in (3, 2, 1))
    total = jnp.concatenate([total, first, second, third], axis=0)
    other = swapped(total, (1, 1))
    return pl.pallas_call(
        functools.partial(unpack_kernel, scale),
        out_shape=(
            jax.ShapeDtypeStruct((taps, chans, chans), jnp.float32),
            jax.ShapeDtypeStruct((chans, chans), jnp.float32),
        ),
        in_specs=[SCALAR, VECTOR, VECTOR],
        out_specs=(OUTSIDE, OUTSIDE),
        scratch_shapes=[
            pltpu.VMEM((taps + 1, chans, chans), jnp.float32),
            pltpu.SemaphoreType.DMA((pl.cdiv(taps + 1, UNPACK_CHUNK) + 1,)),
        ],
        compiler_params=LIMIT,
        name="unpack",
    )(me, total, other), done


def prepare(shape, frames, grads, conv_kernel, proj_weight):
    n_frames, height, width, chans = shape
    rows = n_frames * height * width
    return pl.pallas_call(
        functools.partial(prepare_kernel, shape),
        out_shape=(
            jax.ShapeDtypeStruct(frames.shape, frames.dtype),
            jax.ShapeDtypeStruct(grads.shape, grads.dtype),
            jax.ShapeDtypeStruct(conv_kernel.shape, conv_kernel.dtype),
            jax.ShapeDtypeStruct(proj_weight.shape, proj_weight.dtype),
            jax.ShapeDtypeStruct((rows, 3 * chans), jnp.bfloat16),
            jax.ShapeDtypeStruct((rows, 3 * chans), jnp.float32),
            jax.ShapeDtypeStruct((rows, chans), jnp.float32),
        ),
        in_specs=[OUTSIDE] * 4,
        out_specs=(VECTOR,) * 7,
        scratch_shapes=[pltpu.SemaphoreType.DMA((4,))],
        compiler_params=LIMIT,
        cost_estimate=pl.CostEstimate(
            flops=2 * rows * 20 * chans * chans, bytes_accessed=1 << 20, transcendentals=0
        ),
        name="prepare",
    )(*(pltpu.with_memory_space_constraint(x, pltpu.HBM) for x in (frames, grads, conv_kernel, proj_weight)))


def forward(shape, me, halo, grads, conv_kernel, own, sums, hidden_grad):
    n_frames, height, width, chans = shape
    rows = n_frames * height * width
    half = (8, 28, 8, chans)
    return pl.pallas_call(
        functools.partial(forward_kernel, shape),
        out_shape=(
            jax.ShapeDtypeStruct(half, jnp.float32),
            jax.ShapeDtypeStruct(half, jnp.float32),
            jax.ShapeDtypeStruct((rows, chans), jnp.bfloat16),
            jax.ShapeDtypeStruct((rows, chans), jnp.bfloat16),
        ),
        in_specs=[SCALAR] + [VECTOR] * 6,
        out_specs=(VECTOR,) * 4,
        scratch_shapes=[pltpu.VMEM((2 * height * width, 3 * chans), jnp.bfloat16)],
        compiler_params=LIMIT,
        name="forward",
    )(me, halo, grads, conv_kernel, own, sums, hidden_grad)


def backward(shape, pre_grad, following, hidden, frames, grads, conv_kernel, proj_weight):
    n_frames, height, width, chans = shape
    rows = n_frames * height * width
    flops = 2 * rows * 28 * chans * chans
    return pl.pallas_call(
        functools.partial(backward_kernel, shape),
        out_shape=(jax.ShapeDtypeStruct((rows, chans), jnp.bfloat16),) * 2,
        in_specs=[VECTOR] * 7,
        out_specs=(VECTOR,) * 2,
        scratch_shapes=[pltpu.VMEM((rows + 2 * height * width, 3 * chans), jnp.bfloat16)],
        compiler_params=LIMIT,
        cost_estimate=pl.CostEstimate(flops=flops, bytes_accessed=1 << 20, transcendentals=0),
        name="backward",
    )(pre_grad, following, hidden, frames, grads, conv_kernel, proj_weight)


def shards(clip_frames, out_grad, conv_kernel, proj_weight):
    shape = clip_frames.shape[1:]
    n_frames, height, width, chans = shape
    rows = n_frames * height * width
    halo_rows = 2 * height * width
    frames = clip_frames.reshape(rows, chans)
    grads = out_grad.reshape(rows, chans)
    me = device_number().astype(jnp.int32).reshape(1)
    halo = passed_along(frames[rows - halo_rows :], "tm", 1)
    frames, grads, conv_kernel, proj_weight, own, sums, hidden_grad = prepare(
        shape, frames, grads, conv_kernel, proj_weight
    )
    keep, send, hidden, pre_grad = forward(
        shape, me, halo, grads, conv_kernel, own, sums, hidden_grad
    )
    total_pixels = lax.axis_size("dp") * lax.axis_size("tm") * rows
    (kernel_grad, proj_grad), (mixed, input_grad) = summed(
        me,
        keep,
        send,
        1.0 / math.sqrt(total_pixels),
        lambda: passed_along(pre_grad[:halo_rows], "tm", -1),
        lambda following: backward(
            shape, pre_grad, following, hidden, frames, grads, conv_kernel, proj_weight
        ),
    )
    return (
        mixed.reshape(clip_frames.shape),
        input_grad.reshape(clip_frames.shape),
        kernel_grad.reshape(conv_kernel.shape),
        proj_grad,
    )


def solution(mesh):
    placed = (P("dp", "tm", None, None, None), P("dp", "tm", None, None, None), P(), P())
    return jax.shard_map(
        shards,
        mesh=mesh,
        in_specs=placed,
        out_specs=(P("dp", "tm", None, None, None), P("dp", "tm", None, None, None), P(), P()),
        check_vma=False,
    )
```

```python
import functools
import math

import jax
import jax.numpy as jnp
from jax import lax
from jax.experimental import pallas as pl
from jax.experimental.pallas import tpu as pltpu
from jax.sharding import PartitionSpec as P

AXES = ("dp", "tm")
PAIRS = (((1, 2), (3, 4)), ((3, 4), (1, 2)))
UNPACK_CHUNK = 7
LIMIT = pltpu.CompilerParams(vmem_limit_bytes=16 * 1024 * 1024)
SCALAR = pl.BlockSpec(memory_space=pltpu.SMEM)
VECTOR = pl.BlockSpec(memory_space=pltpu.VMEM)
OUTSIDE = pl.BlockSpec(memory_space=pltpu.HBM)


def passed_round(shard, axis, by):
    size = lax.axis_size(axis)
    return lax.ppermute(shard, axis, [(i, (i + by) % size) for i in range(size)])


def device_number():
    return lax.axis_index("dp") * lax.axis_size("tm") + lax.axis_index("tm")


def swapped(array, masks):
    count = lax.axis_size("dp") * lax.axis_size("tm")
    return lax.ppermute(array, AXES, [(i, i ^ masks[i & 1]) for i in range(count)])


def masks_of(stage, offset):
    return tuple(
        (offset >> 1) << pairs[stage][0] | (offset & 1) << pairs[stage][1] for pairs in PAIRS
    )


def halves_of(me):
    first, second = (4 * ((me >> split[0]) & 1) + 2 * ((me >> split[1]) & 1) for split, _ in PAIRS)
    core = me & 1
    return jnp.where(core == 0, first, second), jnp.where(core == 0, second, first)


def beside(flat, width):
    rows = flat.shape[0]
    wide = flat.astype(jnp.float32)
    column = lax.broadcasted_iota(jnp.int32, flat.shape, 0) % width
    before = jnp.where(column == 0, 0.0, pltpu.roll(wide, 1, 0)).astype(flat.dtype)
    after = jnp.where(column == width - 1, 0.0, pltpu.roll(wide, rows - 1, 0)).astype(flat.dtype)
    return before, after


def moved_rows(flat, map_rows, width, by):
    zero = jnp.zeros((width, flat.shape[1]), flat.dtype)
    pieces = []
    for start in range(0, flat.shape[0], map_rows):
        whole = flat[start : start + map_rows]
        pieces += [zero, whole[:-width]] if by == 1 else [whole[width:], zero]
    return jnp.concatenate(pieces, axis=0)


def dot(left, right, contract):
    return lax.dot_general(
        left, right, ((contract[:1], contract[1:]), ((), ())), preferred_element_type=jnp.float32
    )


def spread(flat, width, wide_ref, flipped=False):
    chans = flat.shape[1]
    before, after = beside(flat, width)
    wide_ref[:, :chans] = after if flipped else before
    wide_ref[:, chans : 2 * chans] = flat
    wide_ref[:, 2 * chans :] = before if flipped else after


def spread_unless(outside, ref, width, wide_ref, flipped=False):
    @pl.when(outside)
    def _():
        wide_ref[...] = jnp.zeros(wide_ref.shape, wide_ref.dtype)

    @pl.when(jnp.logical_not(outside))
    def _():
        spread(ref[...], width, wide_ref, flipped)


def weights_of(kern_ref, tau):
    chans = kern_ref.shape[-1]
    return jnp.concatenate(
        [kern_ref[tau, row].reshape(3 * chans, chans) for row in range(3)], axis=1
    )


def prepare_kernel(
    shape, frames_hbm, grads_hbm, kern_hbm, proj_hbm,
    frames_ref, grads_ref, kern_ref, proj_ref, wide_ref, sums_ref, hidden_grad_ref, sems,
):
    _, height, width, chans = shape
    map_rows = height * width
    rows = shape[0] * map_rows
    pairs = [(frames_hbm, frames_ref)]
    pairs += [(kern_hbm.at[tau], kern_ref.at[tau]) for tau in (2, 1, 0)]
    pairs += [(proj_hbm, proj_ref), (grads_hbm, grads_ref)]
    copies = [pltpu.make_async_copy(*pair, sems.at[i]) for i, pair in enumerate(pairs)]
    for copy in copies:
        copy.start()
    copies[0].wait()
    spread(frames_ref[...], width, wide_ref)
    for place, tau in enumerate((2, 1, 0)):
        copies[1 + place].wait()
        skip = place * map_rows
        if place == 0:
            sums_ref[...] = dot(wide_ref[...], weights_of(kern_ref, tau), (1, 0))
        elif skip < rows:
            sums_ref[skip:] += dot(wide_ref[: rows - skip], weights_of(kern_ref, tau), (1, 0))
    copies[4].wait()
    copies[5].wait()
    hidden_grad_ref[...] = dot(grads_ref[...], proj_ref[...], (1, 1))


def forward_kernel(
    shape, where_ref, halo_ref, grads_ref, kern_ref, own_ref, sums_ref, hidden_grad_ref,
    keep_ref, send_ref, hidden_ref, pre_grad_ref, wide_ref,
):
    _, height, width, chans = shape
    map_rows = height * width
    rows = shape[0] * map_rows
    spread_unless((where_ref[0] & 2) != 0, halo_ref, width, wide_ref)
    term = dot(wide_ref[...], weights_of(kern_ref, 0), (1, 0))
    early = dot(wide_ref[map_rows:], weights_of(kern_ref, 1), (1, 0))
    head = jnp.concatenate([term[:map_rows] + early, term[map_rows:]], axis=0)
    sums = sums_ref[...]
    if rows > 2 * map_rows:
        sums = jnp.concatenate(
            [sums[: 2 * map_rows] + head, sums[2 * map_rows :]], axis=0
        )
    else:
        sums = sums + head
    pre = (
        moved_rows(sums[:, :chans], map_rows, width, 1)
        + sums[:, chans : 2 * chans]
        + moved_rows(sums[:, 2 * chans :], map_rows, width, -1)
    )
    sig = jax.nn.sigmoid(pre)
    hidden = (pre * sig).astype(jnp.bfloat16)
    grads = grads_ref[...]
    pre_grad = (hidden_grad_ref[...] * sig * (1.0 + pre * (1.0 - sig))).astype(jnp.bfloat16)
    hidden_ref[...] = hidden
    pre_grad_ref[...] = pre_grad
    me = where_ref[0] >> 2
    core = me & 1
    mine, other = halves_of(me)

    def put(tap, value):
        for block in range(8):
            even = value[16 * block : 16 * block + 8]
            odd = value[16 * block + 8 : 16 * block + 16]
            keep_ref[block ^ mine, tap] = jnp.where(core == 0, even, odd)
            send_ref[block ^ other, tap] = jnp.where(core == 0, odd, even)

    put(27, dot(hidden, grads, (0, 0)))
    grad_rows = jnp.concatenate(
        [
            moved_rows(pre_grad, map_rows, width, -1),
            pre_grad,
            moved_rows(pre_grad, map_rows, width, 1),
        ],
        axis=1,
    )
    for tau in range(3):
        skip = (2 - tau) * map_rows
        part = dot(own_ref[: rows - skip], grad_rows[skip:], (0, 0)) if skip < rows else None
        if skip:
            term = dot(wide_ref[tau * map_rows :], grad_rows[:skip], (0, 0))
            part = term if part is None else part + term
        for row in range(3):
            for col in range(3):
                put(
                    tau * 9 + row * 3 + col,
                    part[col * chans : (col + 1) * chans, row * chans : (row + 1) * chans],
                )


def backward_kernel(
    shape, where_ref, pre_grad_ref, next_ref, hidden_ref, frames_ref, grads_ref, kern_ref, proj_ref,
    mixed_ref, input_grad_ref, wide_ref,
):
    _, height, width, chans = shape
    map_rows = height * width
    rows = shape[0] * map_rows
    spread(pre_grad_ref[...], width, wide_ref.at[:rows], flipped=True)
    spread_unless((where_ref[0] & 1) != 0, next_ref, width, wide_ref.at[rows:], flipped=True)
    sums = None
    for tau in range(3):
        weights = jnp.concatenate(
            [kern_ref[tau, :, col].reshape(3 * chans, chans) for col in range(3)], axis=1
        )
        start = (2 - tau) * map_rows
        term = dot(wide_ref[start : start + rows], weights, (1, 1))
        sums = term if sums is None else sums + term
    back = (
        moved_rows(sums[:, :chans], map_rows, width, -1)
        + sums[:, chans : 2 * chans]
        + moved_rows(sums[:, 2 * chans :], map_rows, width, 1)
    )
    input_grad_ref[...] = (grads_ref[...].astype(jnp.float32) + back).astype(jnp.bfloat16)
    mixed_ref[...] = (
        frames_ref[...].astype(jnp.float32) + dot(hidden_ref[...], proj_ref[...], (1, 0))
    ).astype(jnp.bfloat16)


def unpack_kernel(scale, where_ref, mine_ref, other_ref, kern_ref, proj_ref, out_ref, sems):
    me = where_ref[0] >> 2
    core = me & 1
    mine, other = halves_of(me)
    taps = kern_ref.shape[0]
    copies = []
    for first in range(0, taps + 1, UNPACK_CHUNK):
        last = min(first + UNPACK_CHUNK, taps + 1)
        for block in range(8):
            mine_rows = pl.ds(pl.multiple_of(16 * block + 8 * core, 8), 8)
            other_rows = pl.ds(pl.multiple_of(16 * block + 8 * (1 - core), 8), 8)
            out_ref[first:last, mine_rows, :] = (
                mine_ref[block ^ mine, first:last].astype(jnp.float32) * scale
            )
            out_ref[first:last, other_rows, :] = (
                other_ref[block ^ other, first:last].astype(jnp.float32) * scale
            )
        inside = min(last, taps)
        copies.append(
            pltpu.make_async_copy(
                out_ref.at[first:inside], kern_ref.at[first:inside], sems.at[len(copies)]
            )
        )
        copies[-1].start()
    copies.append(pltpu.make_async_copy(out_ref.at[taps], proj_ref, sems.at[len(copies)]))
    copies[-1].start()
    for copy in copies:
        copy.wait()


def summed(where, keep, send, scale, beside_split, beside_exchange):
    taps, chans = keep.shape[1] - 1, keep.shape[3]
    total = keep + swapped(send, (1, 1))
    part = total.shape[0] // 4
    came = [
        swapped(total[offset * part : (offset + 1) * part].astype(jnp.bfloat16), masks_of(0, offset))
        for offset in (3, 2, 1)
    ]
    total = total[:part]
    for piece in came:
        total = total + piece.astype(jnp.float32)
    done = beside_split()
    total, done = lax.optimization_barrier((total, done))
    total = lax.reduce_precision(total, 8, 7)
    third, second, first = (
        swapped(total.astype(jnp.bfloat16), masks_of(1, offset)).astype(jnp.float32)
        for offset in (3, 2, 1)
    )
    total = (total + first) + (second + third)
    count = lax.axis_size("dp") * lax.axis_size("tm")
    mask = 1 << (1 + sum(len(pair) for pair in PAIRS[0]))
    while mask < count:
        total = total + swapped(total, (mask, mask))
        mask *= 2
    done = beside_exchange(done)
    total = total.astype(jnp.bfloat16)
    total, done = lax.optimization_barrier((total, done))
    third, second, first = (swapped(total, masks_of(0, offset)) for offset in (3, 2, 1))
    total = jnp.concatenate([total, first, second, third], axis=0)
    other = swapped(total, (1, 1))
    return pl.pallas_call(
        functools.partial(unpack_kernel, scale),
        out_shape=(
            jax.ShapeDtypeStruct((taps, chans, chans), jnp.float32),
            jax.ShapeDtypeStruct((chans, chans), jnp.float32),
        ),
        in_specs=[SCALAR, VECTOR, VECTOR],
        out_specs=(OUTSIDE, OUTSIDE),
        scratch_shapes=[
            pltpu.VMEM((taps + 1, chans, chans), jnp.float32),
            pltpu.SemaphoreType.DMA((pl.cdiv(taps + 1, UNPACK_CHUNK) + 1,)),
        ],
        compiler_params=LIMIT,
        name="unpack",
    )(where, total, other), done


def prepare(shape, frames, grads, conv_kernel, proj_weight):
    n_frames, height, width, chans = shape
    rows = n_frames * height * width
    return pl.pallas_call(
        functools.partial(prepare_kernel, shape),
        out_shape=(
            jax.ShapeDtypeStruct(frames.shape, frames.dtype),
            jax.ShapeDtypeStruct(grads.shape, grads.dtype),
            jax.ShapeDtypeStruct(conv_kernel.shape, conv_kernel.dtype),
            jax.ShapeDtypeStruct(proj_weight.shape, proj_weight.dtype),
            jax.ShapeDtypeStruct((rows, 3 * chans), jnp.bfloat16),
            jax.ShapeDtypeStruct((rows, 3 * chans), jnp.float32),
            jax.ShapeDtypeStruct((rows, chans), jnp.float32),
        ),
        in_specs=[OUTSIDE] * 4,
        out_specs=(VECTOR,) * 7,
        scratch_shapes=[pltpu.SemaphoreType.DMA((6,))],
        compiler_params=LIMIT,
        cost_estimate=pl.CostEstimate(
            flops=2 * rows * 20 * chans * chans, bytes_accessed=1 << 20, transcendentals=0
        ),
        name="prepare",
    )(*(pltpu.with_memory_space_constraint(x, pltpu.HBM) for x in (frames, grads, conv_kernel, proj_weight)))


def forward(shape, where, halo, grads, conv_kernel, own, sums, hidden_grad):
    n_frames, height, width, chans = shape
    rows = n_frames * height * width
    half = (8, 28, 8, chans)
    return pl.pallas_call(
        functools.partial(forward_kernel, shape),
        out_shape=(
            jax.ShapeDtypeStruct(half, jnp.float32),
            jax.ShapeDtypeStruct(half, jnp.float32),
            jax.ShapeDtypeStruct((rows, chans), jnp.bfloat16),
            jax.ShapeDtypeStruct((rows, chans), jnp.bfloat16),
        ),
        in_specs=[SCALAR] + [VECTOR] * 6,
        out_specs=(VECTOR,) * 4,
        scratch_shapes=[pltpu.VMEM((2 * height * width, 3 * chans), jnp.bfloat16)],
        compiler_params=LIMIT,
        name="forward",
    )(where, halo, grads, conv_kernel, own, sums, hidden_grad)


def backward(shape, where, pre_grad, following, hidden, frames, grads, conv_kernel, proj_weight):
    n_frames, height, width, chans = shape
    rows = n_frames * height * width
    flops = 2 * rows * 28 * chans * chans
    return pl.pallas_call(
        functools.partial(backward_kernel, shape),
        out_shape=(jax.ShapeDtypeStruct((rows, chans), jnp.bfloat16),) * 2,
        in_specs=[SCALAR] + [VECTOR] * 7,
        out_specs=(VECTOR,) * 2,
        scratch_shapes=[pltpu.VMEM((rows + 2 * height * width, 3 * chans), jnp.bfloat16)],
        compiler_params=LIMIT,
        cost_estimate=pl.CostEstimate(flops=flops, bytes_accessed=1 << 20, transcendentals=0),
        name="backward",
    )(where, pre_grad, following, hidden, frames, grads, conv_kernel, proj_weight)


def shards(clip_frames, out_grad, conv_kernel, proj_weight):
    shape = clip_frames.shape[1:]
    n_frames, height, width, chans = shape
    rows = n_frames * height * width
    halo_rows = 2 * height * width
    frames = clip_frames.reshape(rows, chans)
    grads = out_grad.reshape(rows, chans)
    block = lax.axis_index("tm")
    first = (block == 0).astype(jnp.int32)
    last = (block == lax.axis_size("tm") - 1).astype(jnp.int32)
    where = (4 * device_number() + 2 * first + last).astype(jnp.int32).reshape(1)
    halo = passed_round(frames[rows - halo_rows :], "tm", 1)
    frames, grads, conv_kernel, proj_weight, own, sums, hidden_grad = prepare(
        shape, frames, grads, conv_kernel, proj_weight
    )
    keep, send, hidden, pre_grad = forward(
        shape, where, halo, grads, conv_kernel, own, sums, hidden_grad
    )
    total_pixels = lax.axis_size("dp") * lax.axis_size("tm") * rows
    (kernel_grad, proj_grad), (mixed, input_grad) = summed(
        where,
        keep,
        send,
        1.0 / math.sqrt(total_pixels),
        lambda: passed_round(pre_grad[:halo_rows], "tm", -1),
        lambda following: backward(
            shape, where, pre_grad, following, hidden, frames, grads, conv_kernel, proj_weight
        ),
    )
    return (
        mixed.reshape(clip_frames.shape),
        input_grad.reshape(clip_frames.shape),
        kernel_grad.reshape(conv_kernel.shape),
        proj_grad,
    )


def solution(mesh):
    placed = (P("dp", "tm", None, None, None), P("dp", "tm", None, None, None), P(), P())
    return jax.shard_map(
        shards,
        mesh=mesh,
        in_specs=placed,
        out_specs=(P("dp", "tm", None, None, None), P("dp", "tm", None, None, None), P(), P()),
        check_vma=False,
    )
```

```python
import functools
import math

import jax
import jax.numpy as jnp
from jax import lax
from jax.experimental import pallas as pl
from jax.experimental.pallas import tpu as pltpu
from jax.sharding import PartitionSpec as P

AXES = ("dp", "tm")
PAIRS = (((1, 2), (3, 4)), ((3, 4), (1, 2)))
UNPACK_CHUNK = 7
LIMIT = pltpu.CompilerParams(vmem_limit_bytes=16 * 1024 * 1024)
SCALAR = pl.BlockSpec(memory_space=pltpu.SMEM)
VECTOR = pl.BlockSpec(memory_space=pltpu.VMEM)
OUTSIDE = pl.BlockSpec(memory_space=pltpu.HBM)


def passed_round(shard, axis, by):
    size = lax.axis_size(axis)
    return lax.ppermute(shard, axis, [(i, (i + by) % size) for i in range(size)])


def device_number():
    return lax.axis_index("dp") * lax.axis_size("tm") + lax.axis_index("tm")


def swapped(array, masks):
    count = lax.axis_size("dp") * lax.axis_size("tm")
    return lax.ppermute(array, AXES, [(i, i ^ masks[i & 1]) for i in range(count)])


def masks_of(stage, offset):
    return tuple(
        (offset >> 1) << pairs[stage][0] | (offset & 1) << pairs[stage][1] for pairs in PAIRS
    )


def halves_of(me):
    first, second = (4 * ((me >> split[0]) & 1) + 2 * ((me >> split[1]) & 1) for split, _ in PAIRS)
    core = me & 1
    return jnp.where(core == 0, first, second), jnp.where(core == 0, second, first)


def beside(flat, width):
    rows = flat.shape[0]
    wide = flat.astype(jnp.float32)
    column = lax.broadcasted_iota(jnp.int32, flat.shape, 0) % width
    before = jnp.where(column == 0, 0.0, pltpu.roll(wide, 1, 0)).astype(flat.dtype)
    after = jnp.where(column == width - 1, 0.0, pltpu.roll(wide, rows - 1, 0)).astype(flat.dtype)
    return before, after


def moved_rows(flat, map_rows, width, by):
    zero = jnp.zeros((width, flat.shape[1]), flat.dtype)
    pieces = []
    for start in range(0, flat.shape[0], map_rows):
        whole = flat[start : start + map_rows]
        pieces += [zero, whole[:-width]] if by == 1 else [whole[width:], zero]
    return jnp.concatenate(pieces, axis=0)


def dot(left, right, contract):
    return lax.dot_general(
        left, right, ((contract[:1], contract[1:]), ((), ())), preferred_element_type=jnp.float32
    )


def spread(flat, width, wide_ref, flipped=False):
    chans = flat.shape[1]
    before, after = beside(flat, width)
    wide_ref[:, :chans] = after if flipped else before
    wide_ref[:, chans : 2 * chans] = flat
    wide_ref[:, 2 * chans :] = before if flipped else after


def spread_unless(outside, ref, width, wide_ref, flipped=False):
    @pl.when(outside)
    def _():
        wide_ref[...] = jnp.zeros(wide_ref.shape, wide_ref.dtype)

    @pl.when(jnp.logical_not(outside))
    def _():
        spread(ref[...], width, wide_ref, flipped)


def weights_of(kern_ref, tau):
    chans = kern_ref.shape[-1]
    return jnp.concatenate(
        [kern_ref[tau, row].reshape(3 * chans, chans) for row in range(3)], axis=1
    )


def prepare_kernel(
    shape, frames_hbm, grads_hbm, kern_hbm, proj_hbm,
    frames_ref, grads_ref, kern_ref, proj_ref, wide_ref, sums_ref, hidden_grad_ref, sems,
):
    _, height, width, chans = shape
    map_rows = height * width
    rows = shape[0] * map_rows
    pairs = [(frames_hbm, frames_ref)]
    pairs += [(kern_hbm.at[tau], kern_ref.at[tau]) for tau in (2, 1, 0)]
    pairs += [(proj_hbm, proj_ref), (grads_hbm, grads_ref)]
    copies = [pltpu.make_async_copy(*pair, sems.at[i]) for i, pair in enumerate(pairs)]
    for copy in copies:
        copy.start()
    copies[0].wait()
    spread(frames_ref[...], width, wide_ref)
    for place, tau in enumerate((2, 1, 0)):
        copies[1 + place].wait()
        skip = place * map_rows
        if place == 0:
            sums_ref[...] = dot(wide_ref[...], weights_of(kern_ref, tau), (1, 0))
        elif skip < rows:
            sums_ref[skip:] += dot(wide_ref[: rows - skip], weights_of(kern_ref, tau), (1, 0))
    copies[4].wait()
    copies[5].wait()
    hidden_grad_ref[...] = dot(grads_ref[...], proj_ref[...], (1, 1))


def forward_kernel(
    shape, where_ref, halo_ref, grads_ref, kern_ref, own_ref, sums_ref, hidden_grad_ref,
    keep_ref, send_ref, hidden_ref, pre_grad_ref, wide_ref,
):
    _, height, width, chans = shape
    map_rows = height * width
    rows = shape[0] * map_rows
    spread_unless((where_ref[0] & 2) != 0, halo_ref, width, wide_ref)
    term = dot(wide_ref[...], weights_of(kern_ref, 0), (1, 0))
    early = dot(wide_ref[map_rows:], weights_of(kern_ref, 1), (1, 0))
    head = jnp.concatenate([term[:map_rows] + early, term[map_rows:]], axis=0)
    sums = sums_ref[...]
    if rows > 2 * map_rows:
        sums = jnp.concatenate(
            [sums[: 2 * map_rows] + head, sums[2 * map_rows :]], axis=0
        )
    else:
        sums = sums + head
    pre = (
        moved_rows(sums[:, :chans], map_rows, width, 1)
        + sums[:, chans : 2 * chans]
        + moved_rows(sums[:, 2 * chans :], map_rows, width, -1)
    )
    sig = jax.nn.sigmoid(pre)
    hidden = (pre * sig).astype(jnp.bfloat16)
    grads = grads_ref[...]
    pre_grad = (hidden_grad_ref[...] * sig * (1.0 + pre * (1.0 - sig))).astype(jnp.bfloat16)
    hidden_ref[...] = hidden
    pre_grad_ref[...] = pre_grad
    me = where_ref[0] >> 2
    core = me & 1
    mine, other = halves_of(me)

    def put(tap, value):
        for block in range(8):
            even = value[16 * block : 16 * block + 8]
            odd = value[16 * block + 8 : 16 * block + 16]
            keep_ref[block ^ mine, tap] = jnp.where(core == 0, even, odd)
            send_ref[block ^ other, tap] = jnp.where(core == 0, odd, even)

    put(27, dot(hidden, grads, (0, 0)))
    grad_rows = jnp.concatenate(
        [
            moved_rows(pre_grad, map_rows, width, -1),
            pre_grad,
            moved_rows(pre_grad, map_rows, width, 1),
        ],
        axis=1,
    )
    for tau in range(3):
        skip = (2 - tau) * map_rows
        part = dot(own_ref[: rows - skip], grad_rows[skip:], (0, 0)) if skip < rows else None
        if skip:
            term = dot(wide_ref[tau * map_rows :], grad_rows[:skip], (0, 0))
            part = term if part is None else part + term
        for row in range(3):
            for col in range(3):
                put(
                    tau * 9 + row * 3 + col,
                    part[col * chans : (col + 1) * chans, row * chans : (row + 1) * chans],
                )


def backward_kernel(
    shape, where_ref, pre_grad_ref, next_ref, hidden_ref, frames_ref, grads_ref, kern_ref, proj_ref,
    mixed_ref, input_grad_ref, wide_ref,
):
    _, height, width, chans = shape
    map_rows = height * width
    rows = shape[0] * map_rows
    spread(pre_grad_ref[...], width, wide_ref.at[:rows], flipped=True)
    spread_unless((where_ref[0] & 1) != 0, next_ref, width, wide_ref.at[rows:], flipped=True)
    sums = None
    for tau in range(3):
        weights = jnp.concatenate(
            [kern_ref[tau, :, col].reshape(3 * chans, chans) for col in range(3)], axis=1
        )
        start = (2 - tau) * map_rows
        term = dot(wide_ref[start : start + rows], weights, (1, 1))
        sums = term if sums is None else sums + term
    back = (
        moved_rows(sums[:, :chans], map_rows, width, -1)
        + sums[:, chans : 2 * chans]
        + moved_rows(sums[:, 2 * chans :], map_rows, width, 1)
    )
    input_grad_ref[...] = (grads_ref[...].astype(jnp.float32) + back).astype(jnp.bfloat16)
    mixed_ref[...] = (
        frames_ref[...].astype(jnp.float32) + dot(hidden_ref[...], proj_ref[...], (1, 0))
    ).astype(jnp.bfloat16)


def unpack_kernel(scale, where_ref, mine_ref, other_ref, kern_ref, proj_ref, out_ref, sems):
    me = where_ref[0] >> 2
    core = me & 1
    mine, other = halves_of(me)
    taps = kern_ref.shape[0]
    copies = []
    for first in range(0, taps + 1, UNPACK_CHUNK):
        last = min(first + UNPACK_CHUNK, taps + 1)
        for block in range(8):
            mine_rows = pl.ds(pl.multiple_of(16 * block + 8 * core, 8), 8)
            other_rows = pl.ds(pl.multiple_of(16 * block + 8 * (1 - core), 8), 8)
            out_ref[first:last, mine_rows, :] = (
                mine_ref[block ^ mine, first:last].astype(jnp.float32) * scale
            )
            out_ref[first:last, other_rows, :] = (
                other_ref[block ^ other, first:last].astype(jnp.float32) * scale
            )
        inside = min(last, taps)
        copies.append(
            pltpu.make_async_copy(
                out_ref.at[first:inside], kern_ref.at[first:inside], sems.at[len(copies)]
            )
        )
        copies[-1].start()
    copies.append(pltpu.make_async_copy(out_ref.at[taps], proj_ref, sems.at[len(copies)]))
    copies[-1].start()
    for copy in copies:
        copy.wait()


def summed(where, keep, send, scale, beside_split, beside_exchange):
    taps, chans = keep.shape[1] - 1, keep.shape[3]
    total = keep + swapped(send, (1, 1))
    part = total.shape[0] // 4
    came = [
        swapped(total[offset * part : (offset + 1) * part].astype(jnp.bfloat16), masks_of(0, offset))
        for offset in (2, 1, 3)
    ]
    total = total[:part]
    for piece in came:
        total = total + piece.astype(jnp.float32)
    done = beside_split()
    total, done = lax.optimization_barrier((total, done))
    total = lax.reduce_precision(total, 8, 7)
    second, first, third = (
        swapped(total.astype(jnp.bfloat16), masks_of(1, offset)).astype(jnp.float32)
        for offset in (2, 1, 3)
    )
    total = (total + first) + (second + third)
    count = lax.axis_size("dp") * lax.axis_size("tm")
    mask = 1 << (1 + sum(len(pair) for pair in PAIRS[0]))
    while mask < count:
        total = total + swapped(total, (mask, mask))
        mask *= 2
    done = beside_exchange(done)
    total = total.astype(jnp.bfloat16)
    total, done = lax.optimization_barrier((total, done))
    second, first, third = (swapped(total, masks_of(0, offset)) for offset in (2, 1, 3))
    total = jnp.concatenate([total, first, second, third], axis=0)
    other = swapped(total, (1, 1))
    return pl.pallas_call(
        functools.partial(unpack_kernel, scale),
        out_shape=(
            jax.ShapeDtypeStruct((taps, chans, chans), jnp.float32),
            jax.ShapeDtypeStruct((chans, chans), jnp.float32),
        ),
        in_specs=[SCALAR, VECTOR, VECTOR],
        out_specs=(OUTSIDE, OUTSIDE),
        scratch_shapes=[
            pltpu.VMEM((taps + 1, chans, chans), jnp.float32),
            pltpu.SemaphoreType.DMA((pl.cdiv(taps + 1, UNPACK_CHUNK) + 1,)),
        ],
        compiler_params=LIMIT,
        name="unpack",
    )(where, total, other), done


def prepare(shape, frames, grads, conv_kernel, proj_weight):
    n_frames, height, width, chans = shape
    rows = n_frames * height * width
    return pl.pallas_call(
        functools.partial(prepare_kernel, shape),
        out_shape=(
            jax.ShapeDtypeStruct(frames.shape, frames.dtype),
            jax.ShapeDtypeStruct(grads.shape, grads.dtype),
            jax.ShapeDtypeStruct(conv_kernel.shape, conv_kernel.dtype),
            jax.ShapeDtypeStruct(proj_weight.shape, proj_weight.dtype),
            jax.ShapeDtypeStruct((rows, 3 * chans), jnp.bfloat16),
            jax.ShapeDtypeStruct((rows, 3 * chans), jnp.float32),
            jax.ShapeDtypeStruct((rows, chans), jnp.float32),
        ),
        in_specs=[OUTSIDE] * 4,
        out_specs=(VECTOR,) * 7,
        scratch_shapes=[pltpu.SemaphoreType.DMA((6,))],
        compiler_params=LIMIT,
        cost_estimate=pl.CostEstimate(
            flops=2 * rows * 20 * chans * chans, bytes_accessed=1 << 20, transcendentals=0
        ),
        name="prepare",
    )(*(pltpu.with_memory_space_constraint(x, pltpu.HBM) for x in (frames, grads, conv_kernel, proj_weight)))


def forward(shape, where, halo, grads, conv_kernel, own, sums, hidden_grad):
    n_frames, height, width, chans = shape
    rows = n_frames * height * width
    half = (8, 28, 8, chans)
    return pl.pallas_call(
        functools.partial(forward_kernel, shape),
        out_shape=(
            jax.ShapeDtypeStruct(half, jnp.float32),
            jax.ShapeDtypeStruct(half, jnp.float32),
            jax.ShapeDtypeStruct((rows, chans), jnp.bfloat16),
            jax.ShapeDtypeStruct((rows, chans), jnp.bfloat16),
        ),
        in_specs=[SCALAR] + [VECTOR] * 6,
        out_specs=(VECTOR,) * 4,
        scratch_shapes=[pltpu.VMEM((2 * height * width, 3 * chans), jnp.bfloat16)],
        compiler_params=LIMIT,
        name="forward",
    )(where, halo, grads, conv_kernel, own, sums, hidden_grad)


def backward(shape, where, pre_grad, following, hidden, frames, grads, conv_kernel, proj_weight):
    n_frames, height, width, chans = shape
    rows = n_frames * height * width
    flops = 2 * rows * 28 * chans * chans
    return pl.pallas_call(
        functools.partial(backward_kernel, shape),
        out_shape=(jax.ShapeDtypeStruct((rows, chans), jnp.bfloat16),) * 2,
        in_specs=[SCALAR] + [VECTOR] * 7,
        out_specs=(VECTOR,) * 2,
        scratch_shapes=[pltpu.VMEM((rows + 2 * height * width, 3 * chans), jnp.bfloat16)],
        compiler_params=LIMIT,
        cost_estimate=pl.CostEstimate(flops=flops, bytes_accessed=1 << 20, transcendentals=0),
        name="backward",
    )(where, pre_grad, following, hidden, frames, grads, conv_kernel, proj_weight)


def shards(clip_frames, out_grad, conv_kernel, proj_weight):
    shape = clip_frames.shape[1:]
    n_frames, height, width, chans = shape
    rows = n_frames * height * width
    halo_rows = 2 * height * width
    frames = clip_frames.reshape(rows, chans)
    grads = out_grad.reshape(rows, chans)
    block = lax.axis_index("tm")
    first = (block == 0).astype(jnp.int32)
    last = (block == lax.axis_size("tm") - 1).astype(jnp.int32)
    where = (4 * device_number() + 2 * first + last).astype(jnp.int32).reshape(1)
    halo = passed_round(frames[rows - halo_rows :], "tm", 1)
    frames, grads, conv_kernel, proj_weight, own, sums, hidden_grad = prepare(
        shape, frames, grads, conv_kernel, proj_weight
    )
    keep, send, hidden, pre_grad = forward(
        shape, where, halo, grads, conv_kernel, own, sums, hidden_grad
    )
    total_pixels = lax.axis_size("dp") * lax.axis_size("tm") * rows
    (kernel_grad, proj_grad), (mixed, input_grad) = summed(
        where,
        keep,
        send,
        1.0 / math.sqrt(total_pixels),
        lambda: passed_round(pre_grad[:halo_rows], "tm", -1),
        lambda following: backward(
            shape, where, pre_grad, following, hidden, frames, grads, conv_kernel, proj_weight
        ),
    )
    return (
        mixed.reshape(clip_frames.shape),
        input_grad.reshape(clip_frames.shape),
        kernel_grad.reshape(conv_kernel.shape),
        proj_grad,
    )


def solution(mesh):
    placed = (P("dp", "tm", None, None, None), P("dp", "tm", None, None, None), P(), P())
    return jax.shard_map(
        shards,
        mesh=mesh,
        in_specs=placed,
        out_specs=(P("dp", "tm", None, None, None), P("dp", "tm", None, None, None), P(), P()),
        check_vma=False,
    )
```

```python
import functools
import math

import jax
import jax.numpy as jnp
from jax import lax
from jax.experimental import pallas as pl
from jax.experimental.pallas import tpu as pltpu
from jax.sharding import PartitionSpec as P

AXES = ("dp", "tm")
PAIRS = (((1, 2), (3, 4)), ((3, 4), (1, 2)))
LIMIT = pltpu.CompilerParams(vmem_limit_bytes=16 * 1024 * 1024)
SCALAR = pl.BlockSpec(memory_space=pltpu.SMEM)
VECTOR = pl.BlockSpec(memory_space=pltpu.VMEM)
OUTSIDE = pl.BlockSpec(memory_space=pltpu.HBM)


def passed_round(shard, axis, by):
    size = lax.axis_size(axis)
    return lax.ppermute(shard, axis, [(i, (i + by) % size) for i in range(size)])


def device_number():
    return lax.axis_index("dp") * lax.axis_size("tm") + lax.axis_index("tm")


def swapped(array, masks):
    count = lax.axis_size("dp") * lax.axis_size("tm")
    return lax.ppermute(array, AXES, [(i, i ^ masks[i & 1]) for i in range(count)])


def masks_of(stage, offset):
    return tuple(
        (offset >> 1) << pairs[stage][0] | (offset & 1) << pairs[stage][1] for pairs in PAIRS
    )


def halves_of(me):
    first, second = (2 * ((me >> split[0]) & 1) + ((me >> split[1]) & 1) for split, _ in PAIRS)
    core = me & 1
    return jnp.where(core == 0, first, second), jnp.where(core == 0, second, first)


def beside(flat, width):
    rows = flat.shape[0]
    wide = flat.astype(jnp.float32)
    column = lax.broadcasted_iota(jnp.int32, flat.shape, 0) % width
    before = jnp.where(column == 0, 0.0, pltpu.roll(wide, 1, 0)).astype(flat.dtype)
    after = jnp.where(column == width - 1, 0.0, pltpu.roll(wide, rows - 1, 0)).astype(flat.dtype)
    return before, after


def moved_rows(flat, map_rows, width, by):
    zero = jnp.zeros((width, flat.shape[1]), flat.dtype)
    pieces = []
    for start in range(0, flat.shape[0], map_rows):
        whole = flat[start : start + map_rows]
        pieces += [zero, whole[:-width]] if by == 1 else [whole[width:], zero]
    return jnp.concatenate(pieces, axis=0)


def dot(left, right, contract):
    return lax.dot_general(
        left, right, ((contract[:1], contract[1:]), ((), ())), preferred_element_type=jnp.float32
    )


def spread(flat, width, wide_ref, flipped=False):
    chans = flat.shape[1]
    before, after = beside(flat, width)
    wide_ref[:, :chans] = after if flipped else before
    wide_ref[:, chans : 2 * chans] = flat
    wide_ref[:, 2 * chans :] = before if flipped else after


def spread_unless(outside, ref, width, wide_ref, flipped=False):
    @pl.when(outside)
    def _():
        wide_ref[...] = jnp.zeros(wide_ref.shape, wide_ref.dtype)

    @pl.when(jnp.logical_not(outside))
    def _():
        spread(ref[...], width, wide_ref, flipped)


def weights_of(kern_ref, tau):
    chans = kern_ref.shape[-1]
    return jnp.concatenate(
        [kern_ref[tau, row].reshape(3 * chans, chans) for row in range(3)], axis=1
    )


def prepare_kernel(
    shape, frames_hbm, grads_hbm, kern_hbm, proj_hbm,
    frames_ref, grads_ref, kern_ref, proj_ref, wide_ref, sums_ref, hidden_grad_ref, sems,
):
    _, height, width, chans = shape
    map_rows = height * width
    rows = shape[0] * map_rows
    pairs = [(frames_hbm, frames_ref)]
    pairs += [(kern_hbm.at[tau], kern_ref.at[tau]) for tau in (2, 1, 0)]
    pairs += [(proj_hbm, proj_ref), (grads_hbm, grads_ref)]
    copies = [pltpu.make_async_copy(*pair, sems.at[i]) for i, pair in enumerate(pairs)]
    for copy in copies:
        copy.start()
    copies[0].wait()
    spread(frames_ref[...], width, wide_ref)
    for place, tau in enumerate((2, 1, 0)):
        copies[1 + place].wait()
        skip = place * map_rows
        if place == 0:
            sums_ref[...] = dot(wide_ref[...], weights_of(kern_ref, tau), (1, 0))
        elif skip < rows:
            sums_ref[skip:] += dot(wide_ref[: rows - skip], weights_of(kern_ref, tau), (1, 0))
    copies[4].wait()
    copies[5].wait()
    hidden_grad_ref[...] = dot(grads_ref[...], proj_ref[...], (1, 1))


def forward_kernel(
    shape, where_ref, halo_ref, grads_ref, kern_ref, own_ref, sums_ref, hidden_grad_ref,
    keep_ref, send_ref, hidden_ref, pre_grad_ref, wide_ref,
):
    _, height, width, chans = shape
    map_rows = height * width
    rows = shape[0] * map_rows
    spread_unless((where_ref[0] & 2) != 0, halo_ref, width, wide_ref)
    term = dot(wide_ref[...], weights_of(kern_ref, 0), (1, 0))
    early = dot(wide_ref[map_rows:], weights_of(kern_ref, 1), (1, 0))
    head = jnp.concatenate([term[:map_rows] + early, term[map_rows:]], axis=0)
    sums = sums_ref[...]
    if rows > 2 * map_rows:
        sums = jnp.concatenate(
            [sums[: 2 * map_rows] + head, sums[2 * map_rows :]], axis=0
        )
    else:
        sums = sums + head
    pre = (
        moved_rows(sums[:, :chans], map_rows, width, 1)
        + sums[:, chans : 2 * chans]
        + moved_rows(sums[:, 2 * chans :], map_rows, width, -1)
    )
    sig = jax.nn.sigmoid(pre)
    hidden = (pre * sig).astype(jnp.bfloat16)
    grads = grads_ref[...]
    pre_grad = (hidden_grad_ref[...] * sig * (1.0 + pre * (1.0 - sig))).astype(jnp.bfloat16)
    hidden_ref[...] = hidden
    pre_grad_ref[...] = pre_grad
    me = where_ref[0] >> 2
    core = me & 1
    mine, other = halves_of(me)

    def put(tap, value):
        block_rows = keep_ref.shape[2]
        for block in range(4):
            start = block * block_rows
            low = value[start : start + block_rows]
            high = value[chans // 2 + start : chans // 2 + start + block_rows]
            keep_ref[block ^ mine, tap] = jnp.where(core == 0, low, high)
            send_ref[block ^ other, tap] = jnp.where(core == 0, high, low)

    put(27, dot(hidden, grads, (0, 0)))
    grad_rows = jnp.concatenate(
        [
            moved_rows(pre_grad, map_rows, width, -1),
            pre_grad,
            moved_rows(pre_grad, map_rows, width, 1),
        ],
        axis=1,
    )
    for tau in range(3):
        skip = (2 - tau) * map_rows
        part = dot(own_ref[: rows - skip], grad_rows[skip:], (0, 0)) if skip < rows else None
        if skip:
            term = dot(wide_ref[tau * map_rows :], grad_rows[:skip], (0, 0))
            part = term if part is None else part + term
        for row in range(3):
            for col in range(3):
                put(
                    tau * 9 + row * 3 + col,
                    part[col * chans : (col + 1) * chans, row * chans : (row + 1) * chans],
                )


def backward_kernel(
    shape, where_ref, pre_grad_ref, next_ref, hidden_ref, frames_ref, grads_ref, kern_ref, proj_ref,
    mixed_ref, input_grad_ref, wide_ref,
):
    _, height, width, chans = shape
    map_rows = height * width
    rows = shape[0] * map_rows
    spread(pre_grad_ref[...], width, wide_ref.at[:rows], flipped=True)
    spread_unless((where_ref[0] & 1) != 0, next_ref, width, wide_ref.at[rows:], flipped=True)
    sums = None
    for tau in range(3):
        weights = jnp.concatenate(
            [kern_ref[tau, :, col].reshape(3 * chans, chans) for col in range(3)], axis=1
        )
        start = (2 - tau) * map_rows
        term = dot(wide_ref[start : start + rows], weights, (1, 1))
        sums = term if sums is None else sums + term
    back = (
        moved_rows(sums[:, :chans], map_rows, width, -1)
        + sums[:, chans : 2 * chans]
        + moved_rows(sums[:, 2 * chans :], map_rows, width, 1)
    )
    input_grad_ref[...] = (grads_ref[...].astype(jnp.float32) + back).astype(jnp.bfloat16)
    mixed_ref[...] = (
        frames_ref[...].astype(jnp.float32) + dot(hidden_ref[...], proj_ref[...], (1, 0))
    ).astype(jnp.bfloat16)


def unpack_kernel(scale, offsets, where_ref, *refs):
    count = len(offsets)
    pieces = refs[: 2 * count]
    kern_ref, proj_ref, out_ref, sems = refs[-4:]
    me = where_ref[0] >> 2
    core = me & 1
    halves = tuple(zip((core, 1 - core), halves_of(me)))
    taps, chans, _ = kern_ref.shape
    block_rows = out_ref.shape[2]
    copies = []
    for place, piece_ref in enumerate(pieces):
        half, flip = halves[place % 2]
        block = offsets[place // 2] ^ flip
        out_ref[place] = piece_ref[0].astype(jnp.float32) * scale
        rows = pl.ds(
            pl.multiple_of(half * (chans // 2) + block * block_rows, block_rows), block_rows
        )
        copies += [
            pltpu.make_async_copy(
                out_ref.at[place, :taps], kern_ref.at[:, rows, :], sems.at[2 * place]
            ),
            pltpu.make_async_copy(out_ref.at[place, taps], proj_ref.at[rows, :], sems.at[2 * place + 1]),
        ]
        copies[-2].start()
        copies[-1].start()
    for copy in copies:
        copy.wait()


def unpack(where, pieces, offsets, scale, sofar=()):
    given = [piece for offset in offsets for piece in pieces[offset]]
    _, taps, block_rows, chans = given[0].shape
    return pl.pallas_call(
        functools.partial(unpack_kernel, scale, offsets),
        out_shape=(
            jax.ShapeDtypeStruct((taps - 1, chans, chans), jnp.float32),
            jax.ShapeDtypeStruct((chans, chans), jnp.float32),
        ),
        in_specs=[SCALAR] + [VECTOR] * len(given) + [OUTSIDE] * len(sofar),
        out_specs=(OUTSIDE, OUTSIDE),
        scratch_shapes=[
            pltpu.VMEM((len(given), taps, block_rows, chans), jnp.float32),
            pltpu.SemaphoreType.DMA((2 * len(given),)),
        ],
        input_output_aliases={1 + len(given) + i: i for i in range(len(sofar))},
        compiler_params=LIMIT,
        cost_estimate=pl.CostEstimate(
            flops=taps * block_rows * chans * len(given),
            bytes_accessed=6 * taps * block_rows * chans * len(given),
            transcendentals=0,
        ),
        name="unpack",
    )(where, *given, *sofar)


def summed(where, keep, send, scale, beside_split, beside_exchange):
    total = keep + swapped(send, (1, 1))
    part = total.shape[0] // 4
    came = [
        swapped(total[offset * part : (offset + 1) * part].astype(jnp.bfloat16), masks_of(0, offset))
        for offset in (3, 2, 1)
    ]
    total = total[:part]
    for piece in came:
        total = total + piece.astype(jnp.float32)
    done = beside_split()
    total, done = lax.optimization_barrier((total, done))
    total = lax.reduce_precision(total, 8, 7)
    third, second, first = (
        swapped(total.astype(jnp.bfloat16), masks_of(1, offset)).astype(jnp.float32)
        for offset in (3, 2, 1)
    )
    total = (total + first) + (second + third)
    count = lax.axis_size("dp") * lax.axis_size("tm")
    mask = 1 << (1 + sum(len(pair) for pair in PAIRS[0]))
    while mask < count:
        total = total + swapped(total, (mask, mask))
        mask *= 2
    done = beside_exchange(done)
    total = total.astype(jnp.bfloat16)
    total, done = lax.optimization_barrier((total, done))
    mine = [total] + [swapped(total, masks_of(0, offset)) for offset in (1, 2, 3)]
    pieces = [(piece, swapped(piece, (1, 1))) for piece in mine[:3]]
    sofar = unpack(where, pieces, (0, 1, 2), scale)
    pieces.append((mine[3], swapped(mine[3], (1, 1))))
    return unpack(where, pieces, (3,), scale, sofar), done


def prepare(shape, frames, grads, conv_kernel, proj_weight):
    n_frames, height, width, chans = shape
    rows = n_frames * height * width
    return pl.pallas_call(
        functools.partial(prepare_kernel, shape),
        out_shape=(
            jax.ShapeDtypeStruct(frames.shape, frames.dtype),
            jax.ShapeDtypeStruct(grads.shape, grads.dtype),
            jax.ShapeDtypeStruct(conv_kernel.shape, conv_kernel.dtype),
            jax.ShapeDtypeStruct(proj_weight.shape, proj_weight.dtype),
            jax.ShapeDtypeStruct((rows, 3 * chans), jnp.bfloat16),
            jax.ShapeDtypeStruct((rows, 3 * chans), jnp.float32),
            jax.ShapeDtypeStruct((rows, chans), jnp.float32),
        ),
        in_specs=[OUTSIDE] * 4,
        out_specs=(VECTOR,) * 7,
        scratch_shapes=[pltpu.SemaphoreType.DMA((6,))],
        compiler_params=LIMIT,
        cost_estimate=pl.CostEstimate(
            flops=2 * rows * 20 * chans * chans, bytes_accessed=1 << 20, transcendentals=0
        ),
        name="prepare",
    )(*(pltpu.with_memory_space_constraint(x, pltpu.HBM) for x in (frames, grads, conv_kernel, proj_weight)))


def forward(shape, where, halo, grads, conv_kernel, own, sums, hidden_grad):
    n_frames, height, width, chans = shape
    rows = n_frames * height * width
    half = (4, 28, chans // 8, chans)
    return pl.pallas_call(
        functools.partial(forward_kernel, shape),
        out_shape=(
            jax.ShapeDtypeStruct(half, jnp.float32),
            jax.ShapeDtypeStruct(half, jnp.float32),
            jax.ShapeDtypeStruct((rows, chans), jnp.bfloat16),
            jax.ShapeDtypeStruct((rows, chans), jnp.bfloat16),
        ),
        in_specs=[SCALAR] + [VECTOR] * 6,
        out_specs=(VECTOR,) * 4,
        scratch_shapes=[pltpu.VMEM((2 * height * width, 3 * chans), jnp.bfloat16)],
        compiler_params=LIMIT,
        name="forward",
    )(where, halo, grads, conv_kernel, own, sums, hidden_grad)


def backward(shape, where, pre_grad, following, hidden, frames, grads, conv_kernel, proj_weight):
    n_frames, height, width, chans = shape
    rows = n_frames * height * width
    flops = 2 * rows * 28 * chans * chans
    return pl.pallas_call(
        functools.partial(backward_kernel, shape),
        out_shape=(jax.ShapeDtypeStruct((rows, chans), jnp.bfloat16),) * 2,
        in_specs=[SCALAR] + [VECTOR] * 7,
        out_specs=(VECTOR,) * 2,
        scratch_shapes=[pltpu.VMEM((rows + 2 * height * width, 3 * chans), jnp.bfloat16)],
        compiler_params=LIMIT,
        cost_estimate=pl.CostEstimate(flops=flops, bytes_accessed=1 << 20, transcendentals=0),
        name="backward",
    )(where, pre_grad, following, hidden, frames, grads, conv_kernel, proj_weight)


def shards(clip_frames, out_grad, conv_kernel, proj_weight):
    shape = clip_frames.shape[1:]
    n_frames, height, width, chans = shape
    rows = n_frames * height * width
    halo_rows = 2 * height * width
    frames = clip_frames.reshape(rows, chans)
    grads = out_grad.reshape(rows, chans)
    block = lax.axis_index("tm")
    first = (block == 0).astype(jnp.int32)
    last = (block == lax.axis_size("tm") - 1).astype(jnp.int32)
    where = (4 * device_number() + 2 * first + last).astype(jnp.int32).reshape(1)
    halo = passed_round(frames[rows - halo_rows :], "tm", 1)
    frames, grads, conv_kernel, proj_weight, own, sums, hidden_grad = prepare(
        shape, frames, grads, conv_kernel, proj_weight
    )
    keep, send, hidden, pre_grad = forward(
        shape, where, halo, grads, conv_kernel, own, sums, hidden_grad
    )
    total_pixels = lax.axis_size("dp") * lax.axis_size("tm") * rows
    (kernel_grad, proj_grad), (mixed, input_grad) = summed(
        where,
        keep,
        send,
        1.0 / math.sqrt(total_pixels),
        lambda: passed_round(pre_grad[:halo_rows], "tm", -1),
        lambda following: backward(
            shape, where, pre_grad, following, hidden, frames, grads, conv_kernel, proj_weight
        ),
    )
    return (
        mixed.reshape(clip_frames.shape),
        input_grad.reshape(clip_frames.shape),
        kernel_grad.reshape(conv_kernel.shape),
        proj_grad,
    )


def solution(mesh):
    placed = (P("dp", "tm", None, None, None), P("dp", "tm", None, None, None), P(), P())
    return jax.shard_map(
        shards,
        mesh=mesh,
        in_specs=placed,
        out_specs=(P("dp", "tm", None, None, None), P("dp", "tm", None, None, None), P(), P()),
        check_vma=False,
    )
```

```python
import functools
import math

import jax
import jax.numpy as jnp
from jax import lax
from jax.experimental import pallas as pl
from jax.experimental.pallas import tpu as pltpu
from jax.sharding import PartitionSpec as P

AXES = ("dp", "tm")
PAIRS = (((1, 2), (3, 4)), ((3, 4), (1, 2)))
LIMIT = pltpu.CompilerParams(vmem_limit_bytes=16 * 1024 * 1024)
SCALAR = pl.BlockSpec(memory_space=pltpu.SMEM)
VECTOR = pl.BlockSpec(memory_space=pltpu.VMEM)
OUTSIDE = pl.BlockSpec(memory_space=pltpu.HBM)


def passed_round(shard, axis, by):
    size = lax.axis_size(axis)
    return lax.ppermute(shard, axis, [(i, (i + by) % size) for i in range(size)])


def device_number():
    return lax.axis_index("dp") * lax.axis_size("tm") + lax.axis_index("tm")


def swapped(array, masks):
    count = lax.axis_size("dp") * lax.axis_size("tm")
    return lax.ppermute(array, AXES, [(i, i ^ masks[i & 1]) for i in range(count)])


def masks_of(stage, offset):
    return tuple(
        (offset >> 1) << pairs[stage][0] | (offset & 1) << pairs[stage][1] for pairs in PAIRS
    )


def halves_of(me):
    first, second = (2 * ((me >> split[0]) & 1) + ((me >> split[1]) & 1) for split, _ in PAIRS)
    core = me & 1
    return jnp.where(core == 0, first, second), jnp.where(core == 0, second, first)


def beside(flat, width):
    rows = flat.shape[0]
    wide = flat.astype(jnp.float32)
    column = lax.broadcasted_iota(jnp.int32, flat.shape, 0) % width
    before = jnp.where(column == 0, 0.0, pltpu.roll(wide, 1, 0)).astype(flat.dtype)
    after = jnp.where(column == width - 1, 0.0, pltpu.roll(wide, rows - 1, 0)).astype(flat.dtype)
    return before, after


def moved_rows(flat, map_rows, width, by):
    zero = jnp.zeros((width, flat.shape[1]), flat.dtype)
    pieces = []
    for start in range(0, flat.shape[0], map_rows):
        whole = flat[start : start + map_rows]
        pieces += [zero, whole[:-width]] if by == 1 else [whole[width:], zero]
    return jnp.concatenate(pieces, axis=0)


def dot(left, right, contract):
    return lax.dot_general(
        left, right, ((contract[:1], contract[1:]), ((), ())), preferred_element_type=jnp.float32
    )


def spread(flat, width, wide_ref, flipped=False):
    chans = flat.shape[1]
    before, after = beside(flat, width)
    wide_ref[:, :chans] = after if flipped else before
    wide_ref[:, chans : 2 * chans] = flat
    wide_ref[:, 2 * chans :] = before if flipped else after


def spread_unless(outside, ref, width, wide_ref, flipped=False):
    @pl.when(outside)
    def _():
        wide_ref[...] = jnp.zeros(wide_ref.shape, wide_ref.dtype)

    @pl.when(jnp.logical_not(outside))
    def _():
        spread(ref[...], width, wide_ref, flipped)


def weights_of(kern_ref, tau):
    chans = kern_ref.shape[-1]
    return jnp.concatenate(
        [kern_ref[tau, row].reshape(3 * chans, chans) for row in range(3)], axis=1
    )


def prepare_kernel(
    width, frames_hbm, grads_hbm, kern_hbm, proj_hbm,
    frames_ref, grads_ref, kern_ref, proj_ref, wide_ref, sems,
):
    pairs = (
        (frames_hbm, frames_ref), (grads_hbm, grads_ref), (kern_hbm, kern_ref), (proj_hbm, proj_ref)
    )
    copies = [pltpu.make_async_copy(*pair, sems.at[i]) for i, pair in enumerate(pairs)]
    for copy in copies:
        copy.start()
    copies[0].wait()
    spread(frames_ref[...], width, wide_ref)
    for copy in copies[1:]:
        copy.wait()


def join_kernel(
    shape, where_ref, own_ref, grads_ref, partner_ref, partner_grads_ref, kern_ref, proj_ref,
    wide_ref, pair_grads_ref, sums_ref, hidden_grad_ref,
):
    _, height, width, chans = shape
    map_rows = height * width
    rows = shape[0] * map_rows
    head = 2 * map_rows
    core = (where_ref[0] >> 2) & 1

    def part(start, index):
        return pl.ds(pl.multiple_of(start + index * rows, map_rows), rows)

    wide_ref[part(head, core)] = own_ref[...]
    spread(partner_ref[...], width, wide_ref.at[part(head, 1 - core)])
    pair_grads_ref[part(0, core)] = grads_ref[...]
    pair_grads_ref[part(0, 1 - core)] = partner_grads_ref[...]
    hidden_grad_ref[...] = dot(pair_grads_ref[...], proj_ref[...], (1, 1))
    sums_ref[...] = dot(wide_ref[head:], weights_of(kern_ref, 2), (1, 0))
    for tau in (1, 0):
        skip = (2 - tau) * map_rows
        sums_ref[skip:] += dot(
            wide_ref[head : head + 2 * rows - skip], weights_of(kern_ref, tau), (1, 0)
        )


def forward_kernel(
    shape, where_ref, first_halo_ref, second_halo_ref, grads_ref, kern_ref, _, sums_ref,
    hidden_grad_ref, keep_ref, send_ref, hidden_ref, pre_grad_ref, wide_ref,
):
    _, height, width, chans = shape
    map_rows = height * width
    rows = shape[0] * map_rows
    head = 2 * map_rows
    me = where_ref[0] >> 2
    core = me & 1
    outside = (where_ref[0] & 2) != 0
    halo_ref = wide_ref.at[:head]

    @pl.when(outside)
    def _():
        halo_ref[...] = jnp.zeros(halo_ref.shape, halo_ref.dtype)

    @pl.when(jnp.logical_not(outside) & (core == 0))
    def _():
        spread(first_halo_ref[...], width, halo_ref)

    @pl.when(jnp.logical_not(outside) & (core == 1))
    def _():
        spread(second_halo_ref[...], width, halo_ref)

    late = dot(halo_ref[...], weights_of(kern_ref, 0), (1, 0))
    early = dot(halo_ref[map_rows:], weights_of(kern_ref, 1), (1, 0))
    sums = sums_ref[...]
    sums = jnp.concatenate(
        [
            sums[:map_rows] + (late[:map_rows] + early),
            sums[map_rows:head] + late[map_rows:],
            sums[head:],
        ],
        axis=0,
    )
    pre = (
        moved_rows(sums[:, :chans], map_rows, width, 1)
        + sums[:, chans : 2 * chans]
        + moved_rows(sums[:, 2 * chans :], map_rows, width, -1)
    )
    sig = jax.nn.sigmoid(pre)
    hidden = (pre * sig).astype(jnp.bfloat16)
    pre_grad = (hidden_grad_ref[...] * sig * (1.0 + pre * (1.0 - sig))).astype(jnp.bfloat16)
    hidden_ref[...] = jnp.where(core == 0, hidden[:rows], hidden[rows:])
    pre_grad_ref[...] = jnp.where(core == 0, pre_grad[:rows], pre_grad[rows:])
    flip = halves_of(me)[0]

    def put(place, value):
        block_rows = keep_ref.shape[2]
        for block in range(4):
            rows_of = value[block * block_rows : (block + 1) * block_rows]
            keep_ref[block ^ flip, place] = rows_of
            send_ref[block ^ flip, place] = rows_of.astype(send_ref.dtype)

    grad_rows = jnp.concatenate(
        [
            moved_rows(pre_grad, map_rows, width, -1),
            pre_grad,
            moved_rows(pre_grad, map_rows, width, 1),
        ],
        axis=1,
    )

    def tap(sums, row, col):
        return sums[col * chans : (col + 1) * chans, row * chans : (row + 1) * chans]

    outer = pl.ds(pl.multiple_of(core * head, map_rows), 2 * rows)
    sums = dot(wide_ref[outer], grad_rows, (0, 0))
    for place in range(9):
        put(place, tap(sums, place // 3, place % 3))
    sums = dot(wide_ref[map_rows : map_rows + 2 * rows], grad_rows, (0, 0))
    middle = [tap(sums, place // 3, place % 3) for place in range(9)]
    middle.append(dot(hidden, grads_ref[...], (0, 0)))
    for place in range(5):
        put(9 + place, jnp.where(core == 0, middle[place], middle[5 + place]))


def backward_kernel(
    shape, where_ref, pre_grad_ref, next_ref, hidden_ref, frames_ref, grads_ref, kern_ref, proj_ref,
    mixed_ref, input_grad_ref, wide_ref,
):
    _, height, width, chans = shape
    map_rows = height * width
    rows = shape[0] * map_rows
    spread(pre_grad_ref[...], width, wide_ref.at[:rows], flipped=True)
    spread_unless((where_ref[0] & 1) != 0, next_ref, width, wide_ref.at[rows:], flipped=True)
    sums = None
    for tau in range(3):
        weights = jnp.concatenate(
            [kern_ref[tau, :, col].reshape(3 * chans, chans) for col in range(3)], axis=1
        )
        start = (2 - tau) * map_rows
        term = dot(wide_ref[start : start + rows], weights, (1, 1))
        sums = term if sums is None else sums + term
    back = (
        moved_rows(sums[:, :chans], map_rows, width, -1)
        + sums[:, chans : 2 * chans]
        + moved_rows(sums[:, 2 * chans :], map_rows, width, 1)
    )
    input_grad_ref[...] = (grads_ref[...].astype(jnp.float32) + back).astype(jnp.bfloat16)
    mixed_ref[...] = (
        frames_ref[...].astype(jnp.float32) + dot(hidden_ref[...], proj_ref[...], (1, 0))
    ).astype(jnp.bfloat16)


def unpack_kernel(scale, offsets, where_ref, *refs):
    pieces = refs[: 2 * len(offsets)]
    kern_ref, proj_ref, out_ref, sems = refs[-4:]
    me = where_ref[0] >> 2
    core = me & 1
    halves = tuple(zip((core, 1 - core), halves_of(me)))
    block_rows = out_ref.shape[2]
    copies = []
    for place, piece_ref in enumerate(pieces):
        half, flip = halves[place % 2]
        block = offsets[place // 2] ^ flip
        out_ref[place] = piece_ref[0].astype(jnp.float32) * scale
        rows = pl.ds(pl.multiple_of(block * block_rows, block_rows), block_rows)
        piece = out_ref.at[place]
        for start, target, wanted in (
            (piece.at[:9], kern_ref.at[pl.ds(18 * half, 9), rows, :], None),
            (piece.at[9:13], kern_ref.at[pl.ds(9 + 5 * half, 4), rows, :], None),
            (piece.at[13], kern_ref.at[13, rows, :], 0),
            (piece.at[13], proj_ref.at[rows, :], 1),
        ):
            copy = pltpu.make_async_copy(start, target, sems.at[len(copies)])
            copies.append((copy, None if wanted is None else half == wanted))
            do(copies[-1][1], copy.start)
    for copy, wanted in copies:
        do(wanted, copy.wait)


def do(wanted, action):
    if wanted is None:
        action()
    else:
        pl.when(wanted)(action)


def unpack(where, pieces, offsets, scale, sofar=()):
    given = [piece for offset in offsets for piece in pieces[offset]]
    _, places, block_rows, chans = given[0].shape
    return pl.pallas_call(
        functools.partial(unpack_kernel, scale, offsets),
        out_shape=(
            jax.ShapeDtypeStruct((2 * places - 1, chans, chans), jnp.float32),
            jax.ShapeDtypeStruct((chans, chans), jnp.float32),
        ),
        in_specs=[SCALAR] + [VECTOR] * len(given) + [OUTSIDE] * len(sofar),
        out_specs=(OUTSIDE, OUTSIDE),
        scratch_shapes=[
            pltpu.VMEM((len(given), places, block_rows, chans), jnp.float32),
            pltpu.SemaphoreType.DMA((4 * len(given),)),
        ],
        input_output_aliases={1 + len(given) + i: i for i in range(len(sofar))},
        compiler_params=LIMIT,
        cost_estimate=pl.CostEstimate(
            flops=places * block_rows * chans * len(given),
            bytes_accessed=6 * places * block_rows * chans * len(given),
            transcendentals=0,
        ),
        name="unpack",
    )(where, *given, *sofar)


def summed(where, keep, send, scale, beside_split, beside_exchange):
    total = keep[:1]
    for offset in (3, 2, 1):
        piece = swapped(send[offset : offset + 1], masks_of(0, offset))
        total = total + piece.astype(jnp.float32)
    done = beside_split()
    total, done = lax.optimization_barrier((total, done))
    total = lax.reduce_precision(total, 8, 7)
    third, second, first = (
        swapped(total.astype(jnp.bfloat16), masks_of(1, offset)).astype(jnp.float32)
        for offset in (3, 2, 1)
    )
    total = (total + first) + (second + third)
    count = lax.axis_size("dp") * lax.axis_size("tm")
    mask = 1 << (1 + sum(len(pair) for pair in PAIRS[0]))
    while mask < count:
        total = total + swapped(total, (mask, mask))
        mask *= 2
    done = beside_exchange(done)
    total = total.astype(jnp.bfloat16)
    total, done = lax.optimization_barrier((total, done))
    mine = [total] + [swapped(total, masks_of(0, offset)) for offset in (1, 2, 3)]
    pieces = [(piece, swapped(piece, (1, 1))) for piece in mine[:3]]
    sofar = unpack(where, pieces, (0, 1, 2), scale)
    pieces.append((mine[3], swapped(mine[3], (1, 1))))
    return unpack(where, pieces, (3,), scale, sofar), done


def prepare(width, frames, grads, conv_kernel, proj_weight):
    given = (frames, grads, conv_kernel, proj_weight)
    rows, chans = frames.shape
    return pl.pallas_call(
        functools.partial(prepare_kernel, width),
        out_shape=(
            *(jax.ShapeDtypeStruct(x.shape, x.dtype) for x in given),
            jax.ShapeDtypeStruct((rows, 3 * chans), jnp.bfloat16),
        ),
        in_specs=[OUTSIDE] * 4,
        out_specs=(VECTOR,) * 5,
        scratch_shapes=[pltpu.SemaphoreType.DMA((4,))],
        compiler_params=LIMIT,
        cost_estimate=pl.CostEstimate(flops=rows * chans, bytes_accessed=2 << 20, transcendentals=0),
        name="prepare",
    )(*(pltpu.with_memory_space_constraint(x, pltpu.HBM) for x in given))


def join(shape, where, own, grads, partner, partner_grads, conv_kernel, proj_weight):
    n_frames, height, width, chans = shape
    rows = n_frames * height * width
    head = 2 * height * width
    return pl.pallas_call(
        functools.partial(join_kernel, shape),
        out_shape=(
            jax.ShapeDtypeStruct((head + 2 * rows, 3 * chans), jnp.bfloat16),
            jax.ShapeDtypeStruct((2 * rows, chans), jnp.bfloat16),
            jax.ShapeDtypeStruct((2 * rows, 3 * chans), jnp.float32),
            jax.ShapeDtypeStruct((2 * rows, chans), jnp.float32),
        ),
        in_specs=[SCALAR] + [VECTOR] * 6,
        out_specs=(VECTOR,) * 4,
        compiler_params=LIMIT,
        cost_estimate=pl.CostEstimate(
            flops=2 * rows * 40 * chans * chans, bytes_accessed=2 << 20, transcendentals=0
        ),
        name="join",
    )(where, own, grads, partner, partner_grads, conv_kernel, proj_weight)


def forward(shape, where, first_halo, second_halo, grads, conv_kernel, wide, sums, hidden_grad):
    n_frames, height, width, chans = shape
    rows = n_frames * height * width
    half = (4, 14, chans // 4, chans)
    return pl.pallas_call(
        functools.partial(forward_kernel, shape),
        out_shape=(
            jax.ShapeDtypeStruct(half, jnp.float32),
            jax.ShapeDtypeStruct(half, jnp.bfloat16),
            jax.ShapeDtypeStruct((rows, chans), jnp.bfloat16),
            jax.ShapeDtypeStruct((rows, chans), jnp.bfloat16),
            jax.ShapeDtypeStruct(wide.shape, wide.dtype),
        ),
        in_specs=[SCALAR] + [VECTOR] * 7,
        out_specs=(VECTOR,) * 5,
        input_output_aliases={5: 4},
        compiler_params=LIMIT,
        name="forward",
    )(where, first_halo, second_halo, grads, conv_kernel, wide, sums, hidden_grad)[:4]


def backward(shape, where, pre_grad, following, hidden, frames, grads, conv_kernel, proj_weight):
    n_frames, height, width, chans = shape
    rows = n_frames * height * width
    flops = 2 * rows * 28 * chans * chans
    return pl.pallas_call(
        functools.partial(backward_kernel, shape),
        out_shape=(jax.ShapeDtypeStruct((rows, chans), jnp.bfloat16),) * 2,
        in_specs=[SCALAR] + [VECTOR] * 7,
        out_specs=(VECTOR,) * 2,
        scratch_shapes=[pltpu.VMEM((rows + 2 * height * width, 3 * chans), jnp.bfloat16)],
        compiler_params=LIMIT,
        cost_estimate=pl.CostEstimate(flops=flops, bytes_accessed=1 << 20, transcendentals=0),
        name="backward",
    )(where, pre_grad, following, hidden, frames, grads, conv_kernel, proj_weight)


def shards(clip_frames, out_grad, conv_kernel, proj_weight):
    shape = clip_frames.shape[1:]
    n_frames, height, width, chans = shape
    rows = n_frames * height * width
    halo_rows = 2 * height * width
    frames = clip_frames.reshape(rows, chans)
    grads = out_grad.reshape(rows, chans)
    block = lax.axis_index("tm")
    first = (block < 2).astype(jnp.int32)
    last = (block == lax.axis_size("tm") - 1).astype(jnp.int32)
    where = (4 * device_number() + 2 * first + last).astype(jnp.int32).reshape(1)
    tail = frames[rows - halo_rows :]
    first_halo = passed_round(tail, "tm", 1)
    second_halo = passed_round(tail, "tm", 2)
    partner = swapped(frames, (1, 1))
    partner_grads = swapped(grads, (1, 1))
    frames, grads, conv_kernel, proj_weight, own = prepare(
        width, frames, grads, conv_kernel, proj_weight
    )
    wide, pair_grads, sums, hidden_grad = join(
        shape, where, own, grads, partner, partner_grads, conv_kernel, proj_weight
    )
    keep, send, hidden, pre_grad = forward(
        shape, where, first_halo, second_halo, pair_grads, conv_kernel, wide, sums, hidden_grad
    )
    total_pixels = lax.axis_size("dp") * lax.axis_size("tm") * rows
    (kernel_grad, proj_grad), (mixed, input_grad) = summed(
        where,
        keep,
        send,
        1.0 / math.sqrt(total_pixels),
        lambda: passed_round(pre_grad[:halo_rows], "tm", -1),
        lambda following: backward(
            shape, where, pre_grad, following, hidden, frames, grads, conv_kernel, proj_weight
        ),
    )
    return (
        mixed.reshape(clip_frames.shape),
        input_grad.reshape(clip_frames.shape),
        kernel_grad.reshape(conv_kernel.shape),
        proj_grad,
    )


def solution(mesh):
    placed = (P("dp", "tm", None, None, None), P("dp", "tm", None, None, None), P(), P())
    return jax.shard_map(
        shards,
        mesh=mesh,
        in_specs=placed,
        out_specs=(P("dp", "tm", None, None, None), P("dp", "tm", None, None, None), P(), P()),
        check_vma=False,
    )
```

```python
import functools
import math

import jax
import jax.numpy as jnp
from jax import lax
from jax.experimental import pallas as pl
from jax.experimental.pallas import tpu as pltpu
from jax.sharding import PartitionSpec as P

AXES = ("dp", "tm")
PAIRS = (((1, 2), (3, 4)), ((3, 4), (1, 2)))
LIMIT = pltpu.CompilerParams(vmem_limit_bytes=16 * 1024 * 1024)
SCALAR = pl.BlockSpec(memory_space=pltpu.SMEM)
VECTOR = pl.BlockSpec(memory_space=pltpu.VMEM)
OUTSIDE = pl.BlockSpec(memory_space=pltpu.HBM)


def passed_round(shard, axis, by):
    size = lax.axis_size(axis)
    return lax.ppermute(shard, axis, [(i, (i + by) % size) for i in range(size)])


def passed_to_last_core(shard):
    clips, blocks = lax.axis_size("dp"), lax.axis_size("tm")
    pairs = [
        (clip * blocks + i, clip * blocks + (i + 2) % blocks if i & 1 else (clip ^ 1) * blocks + i)
        for clip in range(clips)
        for i in range(blocks)
    ]
    return lax.ppermute(shard, AXES, pairs)


def device_number():
    return lax.axis_index("dp") * lax.axis_size("tm") + lax.axis_index("tm")


def swapped(array, masks):
    count = lax.axis_size("dp") * lax.axis_size("tm")
    return lax.ppermute(array, AXES, [(i, i ^ masks[i & 1]) for i in range(count)])


def masks_of(stage, offset):
    return tuple(
        (offset >> 1) << pairs[stage][0] | (offset & 1) << pairs[stage][1] for pairs in PAIRS
    )


def halves_of(me):
    first, second = (2 * ((me >> split[0]) & 1) + ((me >> split[1]) & 1) for split, _ in PAIRS)
    core = me & 1
    return jnp.where(core == 0, first, second), jnp.where(core == 0, second, first)


def beside(flat, width):
    rows = flat.shape[0]
    wide = flat.astype(jnp.float32)
    column = lax.broadcasted_iota(jnp.int32, flat.shape, 0) % width
    before = jnp.where(column == 0, 0.0, pltpu.roll(wide, 1, 0)).astype(flat.dtype)
    after = jnp.where(column == width - 1, 0.0, pltpu.roll(wide, rows - 1, 0)).astype(flat.dtype)
    return before, after


def moved_rows(flat, map_rows, width, by):
    zero = jnp.zeros((width, flat.shape[1]), flat.dtype)
    pieces = []
    for start in range(0, flat.shape[0], map_rows):
        whole = flat[start : start + map_rows]
        pieces += [zero, whole[:-width]] if by == 1 else [whole[width:], zero]
    return jnp.concatenate(pieces, axis=0)


def dot(left, right, contract):
    return lax.dot_general(
        left, right, ((contract[:1], contract[1:]), ((), ())), preferred_element_type=jnp.float32
    )


def spread(flat, width, wide_ref, flipped=False):
    chans = flat.shape[1]
    before, after = beside(flat, width)
    wide_ref[:, :chans] = after if flipped else before
    wide_ref[:, chans : 2 * chans] = flat
    wide_ref[:, 2 * chans :] = before if flipped else after


def spread_unless(outside, ref, width, wide_ref, flipped=False):
    @pl.when(outside)
    def _():
        wide_ref[...] = jnp.zeros(wide_ref.shape, wide_ref.dtype)

    @pl.when(jnp.logical_not(outside))
    def _():
        spread(ref[...], width, wide_ref, flipped)


def weights_of(kern_ref, tau):
    chans = kern_ref.shape[-1]
    return jnp.concatenate(
        [kern_ref[tau, row].reshape(3 * chans, chans) for row in range(3)], axis=1
    )


def prepare_kernel(
    width, frames_hbm, grads_hbm, kern_hbm, proj_hbm,
    frames_ref, grads_ref, kern_ref, proj_ref, wide_ref, sems,
):
    pairs = (
        (frames_hbm, frames_ref), (grads_hbm, grads_ref), (kern_hbm, kern_ref), (proj_hbm, proj_ref)
    )
    copies = [pltpu.make_async_copy(*pair, sems.at[i]) for i, pair in enumerate(pairs)]
    for copy in copies:
        copy.start()
    copies[0].wait()
    spread(frames_ref[...], width, wide_ref)
    for copy in copies[1:]:
        copy.wait()


def join_kernel(
    shape, where_ref, own_ref, grads_ref, partner_ref, partner_grads_ref, kern_ref, proj_ref,
    wide_ref, pair_grads_ref, sums_ref, hidden_grad_ref,
):
    _, height, width, chans = shape
    map_rows = height * width
    rows = shape[0] * map_rows
    head = 2 * map_rows
    core = (where_ref[0] >> 2) & 1

    def part(start, index):
        return pl.ds(pl.multiple_of(start + index * rows, map_rows), rows)

    wide_ref[part(head, core)] = own_ref[...]
    spread(partner_ref[...], width, wide_ref.at[part(head, 1 - core)])
    pair_grads_ref[part(0, core)] = grads_ref[...]
    pair_grads_ref[part(0, 1 - core)] = partner_grads_ref[...]
    hidden_grad_ref[...] = dot(pair_grads_ref[...], proj_ref[...], (1, 1))
    sums_ref[...] = dot(wide_ref[head:], weights_of(kern_ref, 2), (1, 0))
    for tau in (1, 0):
        skip = (2 - tau) * map_rows
        sums_ref[skip:] += dot(
            wide_ref[head : head + 2 * rows - skip], weights_of(kern_ref, tau), (1, 0)
        )


def forward_kernel(
    shape, where_ref, second_halo_ref, first_halo_ref, grads_ref, kern_ref, _, sums_ref,
    hidden_grad_ref, keep_ref, send_ref, hidden_ref, pre_grad_ref, wide_ref,
):
    _, height, width, chans = shape
    map_rows = height * width
    rows = shape[0] * map_rows
    head = 2 * map_rows
    me = where_ref[0] >> 2
    core = me & 1
    outside = (where_ref[0] & 2) != 0
    halo_ref = wide_ref.at[:head]

    @pl.when(outside)
    def _():
        halo_ref[...] = jnp.zeros(halo_ref.shape, halo_ref.dtype)

    @pl.when(jnp.logical_not(outside) & (core == 0))
    def _():
        spread(first_halo_ref[...], width, halo_ref)

    @pl.when(jnp.logical_not(outside) & (core == 1))
    def _():
        spread(second_halo_ref[...], width, halo_ref)

    late = dot(halo_ref[...], weights_of(kern_ref, 0), (1, 0))
    early = dot(halo_ref[map_rows:], weights_of(kern_ref, 1), (1, 0))
    sums = sums_ref[...]
    sums = jnp.concatenate(
        [
            sums[:map_rows] + (late[:map_rows] + early),
            sums[map_rows:head] + late[map_rows:],
            sums[head:],
        ],
        axis=0,
    )
    pre = (
        moved_rows(sums[:, :chans], map_rows, width, 1)
        + sums[:, chans : 2 * chans]
        + moved_rows(sums[:, 2 * chans :], map_rows, width, -1)
    )
    sig = jax.nn.sigmoid(pre)
    hidden = (pre * sig).astype(jnp.bfloat16)
    pre_grad = (hidden_grad_ref[...] * sig * (1.0 + pre * (1.0 - sig))).astype(jnp.bfloat16)
    hidden_ref[...] = jnp.where(core == 0, hidden[:rows], hidden[rows:])
    pre_grad_ref[...] = jnp.where(core == 0, pre_grad[:rows], pre_grad[rows:])
    flip = halves_of(me)[0]

    def put(place, value):
        block_rows = keep_ref.shape[2]
        for block in range(4):
            rows_of = value[block * block_rows : (block + 1) * block_rows]
            keep_ref[block ^ flip, place] = rows_of
            send_ref[block ^ flip, place] = rows_of.astype(send_ref.dtype)

    grad_rows = jnp.concatenate(
        [
            moved_rows(pre_grad, map_rows, width, -1),
            pre_grad,
            moved_rows(pre_grad, map_rows, width, 1),
        ],
        axis=1,
    )

    def tap(sums, row, col):
        return sums[col * chans : (col + 1) * chans, row * chans : (row + 1) * chans]

    outer = pl.ds(pl.multiple_of(core * head, map_rows), 2 * rows)
    sums = dot(wide_ref[outer], grad_rows, (0, 0))
    for place in range(9):
        put(place, tap(sums, place // 3, place % 3))
    sums = dot(wide_ref[map_rows : map_rows + 2 * rows], grad_rows, (0, 0))
    middle = [tap(sums, place // 3, place % 3) for place in range(9)]
    middle.append(dot(hidden, grads_ref[...], (0, 0)))
    for place in range(5):
        put(9 + place, jnp.where(core == 0, middle[place], middle[5 + place]))


def backward_kernel(
    shape, where_ref, pre_grad_ref, next_ref, hidden_ref, frames_ref, grads_ref, kern_ref, proj_ref,
    mixed_ref, input_grad_ref, wide_ref,
):
    _, height, width, chans = shape
    map_rows = height * width
    rows = shape[0] * map_rows
    spread(pre_grad_ref[...], width, wide_ref.at[:rows], flipped=True)
    spread_unless((where_ref[0] & 1) != 0, next_ref, width, wide_ref.at[rows:], flipped=True)
    sums = None
    for tau in range(3):
        weights = jnp.concatenate(
            [kern_ref[tau, :, col].reshape(3 * chans, chans) for col in range(3)], axis=1
        )
        start = (2 - tau) * map_rows
        term = dot(wide_ref[start : start + rows], weights, (1, 1))
        sums = term if sums is None else sums + term
    back = (
        moved_rows(sums[:, :chans], map_rows, width, -1)
        + sums[:, chans : 2 * chans]
        + moved_rows(sums[:, 2 * chans :], map_rows, width, 1)
    )
    input_grad_ref[...] = (grads_ref[...].astype(jnp.float32) + back).astype(jnp.bfloat16)
    mixed_ref[...] = (
        frames_ref[...].astype(jnp.float32) + dot(hidden_ref[...], proj_ref[...], (1, 0))
    ).astype(jnp.bfloat16)


def unpack_kernel(scale, offsets, where_ref, *refs):
    pieces = refs[: 2 * len(offsets)]
    kern_ref, proj_ref, out_ref, sems = refs[-4:]
    me = where_ref[0] >> 2
    core = me & 1
    halves = tuple(zip((core, 1 - core), halves_of(me)))
    block_rows = out_ref.shape[2]
    copies = []
    for place, piece_ref in enumerate(pieces):
        half, flip = halves[place % 2]
        block = offsets[place // 2] ^ flip
        out_ref[place] = piece_ref[0].astype(jnp.float32) * scale
        rows = pl.ds(pl.multiple_of(block * block_rows, block_rows), block_rows)
        piece = out_ref.at[place]
        for start, target, wanted in (
            (piece.at[:9], kern_ref.at[pl.ds(18 * half, 9), rows, :], None),
            (piece.at[9:13], kern_ref.at[pl.ds(9 + 5 * half, 4), rows, :], None),
            (piece.at[13], kern_ref.at[13, rows, :], 0),
            (piece.at[13], proj_ref.at[rows, :], 1),
        ):
            copy = pltpu.make_async_copy(start, target, sems.at[len(copies)])
            copies.append((copy, None if wanted is None else half == wanted))
            do(copies[-1][1], copy.start)
    for copy, wanted in copies:
        do(wanted, copy.wait)


def do(wanted, action):
    if wanted is None:
        action()
    else:
        pl.when(wanted)(action)


def unpack(where, pieces, offsets, scale, sofar=()):
    given = [piece for offset in offsets for piece in pieces[offset]]
    _, places, block_rows, chans = given[0].shape
    return pl.pallas_call(
        functools.partial(unpack_kernel, scale, offsets),
        out_shape=(
            jax.ShapeDtypeStruct((2 * places - 1, chans, chans), jnp.float32),
            jax.ShapeDtypeStruct((chans, chans), jnp.float32),
        ),
        in_specs=[SCALAR] + [VECTOR] * len(given) + [OUTSIDE] * len(sofar),
        out_specs=(OUTSIDE, OUTSIDE),
        scratch_shapes=[
            pltpu.VMEM((len(given), places, block_rows, chans), jnp.float32),
            pltpu.SemaphoreType.DMA((4 * len(given),)),
        ],
        input_output_aliases={1 + len(given) + i: i for i in range(len(sofar))},
        compiler_params=LIMIT,
        cost_estimate=pl.CostEstimate(
            flops=places * block_rows * chans * len(given),
            bytes_accessed=6 * places * block_rows * chans * len(given),
            transcendentals=0,
        ),
        name="unpack",
    )(where, *given, *sofar)


def summed(where, keep, send, scale, beside_split, beside_exchange):
    total = keep[:1]
    for offset in (3, 2, 1):
        piece = swapped(send[offset : offset + 1], masks_of(0, offset))
        total = total + piece.astype(jnp.float32)
    done = beside_split()
    total, done = lax.optimization_barrier((total, done))
    total = lax.reduce_precision(total, 8, 7)
    third, second, first = (
        swapped(total.astype(jnp.bfloat16), masks_of(1, offset)).astype(jnp.float32)
        for offset in (3, 2, 1)
    )
    total = (total + first) + (second + third)
    count = lax.axis_size("dp") * lax.axis_size("tm")
    mask = 1 << (1 + sum(len(pair) for pair in PAIRS[0]))
    while mask < count:
        total = total + swapped(total, (mask, mask))
        mask *= 2
    done = beside_exchange(done)
    total = total.astype(jnp.bfloat16)
    total, done = lax.optimization_barrier((total, done))
    mine = [total] + [swapped(total, masks_of(0, offset)) for offset in (1, 2, 3)]
    pieces = [(piece, swapped(piece, (1, 1))) for piece in mine[:3]]
    sofar = unpack(where, pieces, (0, 1, 2), scale)
    pieces.append((mine[3], swapped(mine[3], (1, 1))))
    return unpack(where, pieces, (3,), scale, sofar), done


def prepare(width, frames, grads, conv_kernel, proj_weight):
    given = (frames, grads, conv_kernel, proj_weight)
    rows, chans = frames.shape
    return pl.pallas_call(
        functools.partial(prepare_kernel, width),
        out_shape=(
            *(jax.ShapeDtypeStruct(x.shape, x.dtype) for x in given),
            jax.ShapeDtypeStruct((rows, 3 * chans), jnp.bfloat16),
        ),
        in_specs=[OUTSIDE] * 4,
        out_specs=(VECTOR,) * 5,
        scratch_shapes=[pltpu.SemaphoreType.DMA((4,))],
        compiler_params=LIMIT,
        cost_estimate=pl.CostEstimate(flops=rows * chans, bytes_accessed=2 << 20, transcendentals=0),
        name="prepare",
    )(*(pltpu.with_memory_space_constraint(x, pltpu.HBM) for x in given))


def join(shape, where, own, grads, partner, partner_grads, conv_kernel, proj_weight):
    n_frames, height, width, chans = shape
    rows = n_frames * height * width
    head = 2 * height * width
    return pl.pallas_call(
        functools.partial(join_kernel, shape),
        out_shape=(
            jax.ShapeDtypeStruct((head + 2 * rows, 3 * chans), jnp.bfloat16),
            jax.ShapeDtypeStruct((2 * rows, chans), jnp.bfloat16),
            jax.ShapeDtypeStruct((2 * rows, 3 * chans), jnp.float32),
            jax.ShapeDtypeStruct((2 * rows, chans), jnp.float32),
        ),
        in_specs=[SCALAR] + [VECTOR] * 6,
        out_specs=(VECTOR,) * 4,
        compiler_params=LIMIT,
        cost_estimate=pl.CostEstimate(
            flops=2 * rows * 40 * chans * chans, bytes_accessed=2 << 20, transcendentals=0
        ),
        name="join",
    )(where, own, grads, partner, partner_grads, conv_kernel, proj_weight)


def forward(shape, where, first_halo, second_halo, grads, conv_kernel, wide, sums, hidden_grad):
    n_frames, height, width, chans = shape
    rows = n_frames * height * width
    half = (4, 14, chans // 4, chans)
    return pl.pallas_call(
        functools.partial(forward_kernel, shape),
        out_shape=(
            jax.ShapeDtypeStruct(half, jnp.float32),
            jax.ShapeDtypeStruct(half, jnp.bfloat16),
            jax.ShapeDtypeStruct((rows, chans), jnp.bfloat16),
            jax.ShapeDtypeStruct((rows, chans), jnp.bfloat16),
            jax.ShapeDtypeStruct(wide.shape, wide.dtype),
        ),
        in_specs=[SCALAR] + [VECTOR] * 7,
        out_specs=(VECTOR,) * 5,
        input_output_aliases={5: 4},
        compiler_params=LIMIT,
        name="forward",
    )(where, second_halo, first_halo, grads, conv_kernel, wide, sums, hidden_grad)[:4]


def backward(shape, where, pre_grad, following, hidden, frames, grads, conv_kernel, proj_weight):
    n_frames, height, width, chans = shape
    rows = n_frames * height * width
    flops = 2 * rows * 28 * chans * chans
    return pl.pallas_call(
        functools.partial(backward_kernel, shape),
        out_shape=(jax.ShapeDtypeStruct((rows, chans), jnp.bfloat16),) * 2,
        in_specs=[SCALAR] + [VECTOR] * 7,
        out_specs=(VECTOR,) * 2,
        scratch_shapes=[pltpu.VMEM((rows + 2 * height * width, 3 * chans), jnp.bfloat16)],
        compiler_params=LIMIT,
        cost_estimate=pl.CostEstimate(flops=flops, bytes_accessed=1 << 20, transcendentals=0),
        name="backward",
    )(where, pre_grad, following, hidden, frames, grads, conv_kernel, proj_weight)


def shards(clip_frames, out_grad, conv_kernel, proj_weight):
    shape = clip_frames.shape[1:]
    n_frames, height, width, chans = shape
    rows = n_frames * height * width
    halo_rows = 2 * height * width
    frames = clip_frames.reshape(rows, chans)
    grads = out_grad.reshape(rows, chans)
    block = lax.axis_index("tm")
    first = (block < 2).astype(jnp.int32)
    last = (block == lax.axis_size("tm") - 1).astype(jnp.int32)
    where = (4 * device_number() + 2 * first + last).astype(jnp.int32).reshape(1)
    tail = frames[rows - halo_rows :]
    first_halo = passed_round(tail, "tm", 1)
    second_halo = passed_to_last_core(tail)
    partner = swapped(frames, (1, 1))
    partner_grads = swapped(grads, (1, 1))
    frames, grads, conv_kernel, proj_weight, own = prepare(
        width, frames, grads, conv_kernel, proj_weight
    )
    wide, pair_grads, sums, hidden_grad = join(
        shape, where, own, grads, partner, partner_grads, conv_kernel, proj_weight
    )
    keep, send, hidden, pre_grad = forward(
        shape, where, first_halo, second_halo, pair_grads, conv_kernel, wide, sums, hidden_grad
    )
    total_pixels = lax.axis_size("dp") * lax.axis_size("tm") * rows
    (kernel_grad, proj_grad), (mixed, input_grad) = summed(
        where,
        keep,
        send,
        1.0 / math.sqrt(total_pixels),
        lambda: passed_round(pre_grad[:halo_rows], "tm", -1),
        lambda following: backward(
            shape, where, pre_grad, following, hidden, frames, grads, conv_kernel, proj_weight
        ),
    )
    return (
        mixed.reshape(clip_frames.shape),
        input_grad.reshape(clip_frames.shape),
        kernel_grad.reshape(conv_kernel.shape),
        proj_grad,
    )


def solution(mesh):
    placed = (P("dp", "tm", None, None, None), P("dp", "tm", None, None, None), P(), P())
    return jax.shard_map(
        shards,
        mesh=mesh,
        in_specs=placed,
        out_specs=(P("dp", "tm", None, None, None), P("dp", "tm", None, None, None), P(), P()),
        check_vma=False,
    )
```

```python
import functools
import math

import jax
import jax.numpy as jnp
from jax import lax
from jax.experimental import pallas as pl
from jax.experimental.pallas import tpu as pltpu
from jax.sharding import PartitionSpec as P

AXES = ("dp", "tm")
PAIRS = (((1, 2), (3, 4)), ((3, 4), (1, 2)))
LIMIT = pltpu.CompilerParams(vmem_limit_bytes=16 * 1024 * 1024)
SCALAR = pl.BlockSpec(memory_space=pltpu.SMEM)
VECTOR = pl.BlockSpec(memory_space=pltpu.VMEM)
OUTSIDE = pl.BlockSpec(memory_space=pltpu.HBM)


def passed_round(shard, axis, by):
    size = lax.axis_size(axis)
    return lax.ppermute(shard, axis, [(i, (i + by) % size) for i in range(size)])


def passed_to_last_core(shard):
    clips, blocks = lax.axis_size("dp"), lax.axis_size("tm")
    pairs = [
        (clip * blocks + i, clip * blocks + (i + 2) % blocks if i & 1 else (clip ^ 1) * blocks + i)
        for clip in range(clips)
        for i in range(blocks)
    ]
    return lax.ppermute(shard, AXES, pairs)


def device_number():
    return lax.axis_index("dp") * lax.axis_size("tm") + lax.axis_index("tm")


def swapped(array, masks):
    count = lax.axis_size("dp") * lax.axis_size("tm")
    return lax.ppermute(array, AXES, [(i, i ^ masks[i & 1]) for i in range(count)])


def masks_of(stage, offset):
    return tuple(
        (offset >> 1) << pairs[stage][0] | (offset & 1) << pairs[stage][1] for pairs in PAIRS
    )


def halves_of(me):
    first, second = (2 * ((me >> split[0]) & 1) + ((me >> split[1]) & 1) for split, _ in PAIRS)
    core = me & 1
    return jnp.where(core == 0, first, second), jnp.where(core == 0, second, first)


def beside(flat, width):
    rows = flat.shape[0]
    wide = flat.astype(jnp.float32)
    column = lax.broadcasted_iota(jnp.int32, flat.shape, 0) % width
    before = jnp.where(column == 0, 0.0, pltpu.roll(wide, 1, 0)).astype(flat.dtype)
    after = jnp.where(column == width - 1, 0.0, pltpu.roll(wide, rows - 1, 0)).astype(flat.dtype)
    return before, after


def moved_rows(flat, map_rows, width, by):
    zero = jnp.zeros((width, flat.shape[1]), flat.dtype)
    pieces = []
    for start in range(0, flat.shape[0], map_rows):
        whole = flat[start : start + map_rows]
        pieces += [zero, whole[:-width]] if by == 1 else [whole[width:], zero]
    return jnp.concatenate(pieces, axis=0)


def dot(left, right, contract):
    return lax.dot_general(
        left, right, ((contract[:1], contract[1:]), ((), ())), preferred_element_type=jnp.float32
    )


def spread(flat, width, wide_ref, flipped=False):
    chans = flat.shape[1]
    before, after = beside(flat, width)
    wide_ref[:, :chans] = after if flipped else before
    wide_ref[:, chans : 2 * chans] = flat
    wide_ref[:, 2 * chans :] = before if flipped else after


def spread_unless(outside, ref, width, wide_ref, flipped=False):
    @pl.when(outside)
    def _():
        wide_ref[...] = jnp.zeros(wide_ref.shape, wide_ref.dtype)

    @pl.when(jnp.logical_not(outside))
    def _():
        spread(ref[...], width, wide_ref, flipped)


def weights_of(kern_ref, tau):
    chans = kern_ref.shape[-1]
    return jnp.concatenate(
        [kern_ref[tau, row].reshape(3 * chans, chans) for row in range(3)], axis=1
    )


def prepare_kernel(
    width, frames_hbm, grads_hbm, kern_hbm, proj_hbm,
    frames_ref, grads_ref, kern_ref, proj_ref, wide_ref, sems,
):
    pairs = (
        (frames_hbm, frames_ref), (grads_hbm, grads_ref), (kern_hbm, kern_ref), (proj_hbm, proj_ref)
    )
    copies = [pltpu.make_async_copy(*pair, sems.at[i]) for i, pair in enumerate(pairs)]
    for copy in copies:
        copy.start()
    copies[0].wait()
    spread(frames_ref[...], width, wide_ref)
    for copy in copies[1:]:
        copy.wait()


def join_kernel(
    shape, where_ref, own_ref, grads_ref, partner_ref, partner_grads_ref, kern_ref, proj_ref,
    wide_ref, pair_grads_ref, sums_ref, hidden_grad_ref,
):
    _, height, width, chans = shape
    map_rows = height * width
    rows = shape[0] * map_rows
    head = 2 * map_rows
    core = (where_ref[0] >> 2) & 1

    def part(start, index):
        return pl.ds(pl.multiple_of(start + index * rows, map_rows), rows)

    wide_ref[part(head, core)] = own_ref[...]
    spread(partner_ref[...], width, wide_ref.at[part(head, 1 - core)])
    pair_grads_ref[part(0, core)] = grads_ref[...]
    pair_grads_ref[part(0, 1 - core)] = partner_grads_ref[...]
    hidden_grad_ref[...] = dot(pair_grads_ref[...], proj_ref[...], (1, 1))
    sums_ref[...] = dot(wide_ref[head:], weights_of(kern_ref, 2), (1, 0))
    for tau in (1, 0):
        skip = (2 - tau) * map_rows
        sums_ref[skip:] += dot(
            wide_ref[head : head + 2 * rows - skip], weights_of(kern_ref, tau), (1, 0)
        )


def forward_kernel(
    shape, where_ref, second_halo_ref, first_halo_ref, grads_ref, kern_ref, _, sums_ref,
    hidden_grad_ref, keep_ref, send_ref, hidden_ref, pre_grad_ref, wide_ref,
):
    _, height, width, chans = shape
    map_rows = height * width
    rows = shape[0] * map_rows
    head = 2 * map_rows
    me = where_ref[0] >> 2
    core = me & 1
    outside = (where_ref[0] & 2) != 0
    halo_ref = wide_ref.at[:head]

    @pl.when(outside)
    def _():
        halo_ref[...] = jnp.zeros(halo_ref.shape, halo_ref.dtype)

    @pl.when(jnp.logical_not(outside) & (core == 0))
    def _():
        spread(first_halo_ref[...], width, halo_ref)

    @pl.when(jnp.logical_not(outside) & (core == 1))
    def _():
        spread(second_halo_ref[...], width, halo_ref)

    late = dot(halo_ref[...], weights_of(kern_ref, 0), (1, 0))
    early = dot(halo_ref[map_rows:], weights_of(kern_ref, 1), (1, 0))
    sums = sums_ref[...]
    sums = jnp.concatenate(
        [
            sums[:map_rows] + (late[:map_rows] + early),
            sums[map_rows:head] + late[map_rows:],
            sums[head:],
        ],
        axis=0,
    )
    pre = (
        moved_rows(sums[:, :chans], map_rows, width, 1)
        + sums[:, chans : 2 * chans]
        + moved_rows(sums[:, 2 * chans :], map_rows, width, -1)
    )
    sig = jax.nn.sigmoid(pre)
    hidden = (pre * sig).astype(jnp.bfloat16)
    pre_grad = (hidden_grad_ref[...] * sig * (1.0 + pre * (1.0 - sig))).astype(jnp.bfloat16)
    hidden_ref[...] = jnp.where(core == 0, hidden[:rows], hidden[rows:])
    pre_grad_ref[...] = jnp.where(core == 0, pre_grad[:rows], pre_grad[rows:])
    flip = halves_of(me)[0]

    def put(place, value):
        block_rows = keep_ref.shape[2]
        for block in range(4):
            rows_of = value[block * block_rows : (block + 1) * block_rows]
            keep_ref[block ^ flip, place] = rows_of
            send_ref[block ^ flip, place] = rows_of.astype(send_ref.dtype)

    grad_rows = jnp.concatenate(
        [
            moved_rows(pre_grad, map_rows, width, -1),
            pre_grad,
            moved_rows(pre_grad, map_rows, width, 1),
        ],
        axis=1,
    )

    def tap(sums, row, col):
        return sums[col * chans : (col + 1) * chans, row * chans : (row + 1) * chans]

    outer = pl.ds(pl.multiple_of(core * head, map_rows), 2 * rows)
    sums = dot(wide_ref[outer], grad_rows, (0, 0))
    for place in range(9):
        put(place, tap(sums, place // 3, place % 3))
    sums = dot(wide_ref[map_rows : map_rows + 2 * rows], grad_rows, (0, 0))
    middle = [tap(sums, place // 3, place % 3) for place in range(9)]
    middle.append(dot(hidden, grads_ref[...], (0, 0)))
    for place in range(5):
        put(9 + place, jnp.where(core == 0, middle[place], middle[5 + place]))


def backward_kernel(
    shape, where_ref, pre_grad_ref, next_ref, hidden_ref, frames_ref, grads_ref, kern_ref, proj_ref,
    mixed_ref, input_grad_ref, wide_ref,
):
    _, height, width, chans = shape
    map_rows = height * width
    rows = shape[0] * map_rows
    spread(pre_grad_ref[...], width, wide_ref.at[:rows], flipped=True)
    spread_unless((where_ref[0] & 1) != 0, next_ref, width, wide_ref.at[rows:], flipped=True)
    sums = None
    for tau in range(3):
        weights = jnp.concatenate(
            [kern_ref[tau, :, col].reshape(3 * chans, chans) for col in range(3)], axis=1
        )
        start = (2 - tau) * map_rows
        term = dot(wide_ref[start : start + rows], weights, (1, 1))
        sums = term if sums is None else sums + term
    back = (
        moved_rows(sums[:, :chans], map_rows, width, -1)
        + sums[:, chans : 2 * chans]
        + moved_rows(sums[:, 2 * chans :], map_rows, width, 1)
    )
    input_grad_ref[...] = (grads_ref[...].astype(jnp.float32) + back).astype(jnp.bfloat16)
    mixed_ref[...] = (
        frames_ref[...].astype(jnp.float32) + dot(hidden_ref[...], proj_ref[...], (1, 0))
    ).astype(jnp.bfloat16)


def unpack_kernel(scale, offsets, where_ref, *refs):
    pieces = refs[: 2 * len(offsets)]
    kern_ref, proj_ref, out_ref, sems = refs[-4:]
    me = where_ref[0] >> 2
    core = me & 1
    halves = tuple(zip((core, 1 - core), halves_of(me)))
    block_rows = out_ref.shape[2]
    copies = []
    for place, piece_ref in enumerate(pieces):
        half, flip = halves[place % 2]
        block = offsets[place // 2] ^ flip
        out_ref[place] = piece_ref[0].astype(jnp.float32) * scale
        rows = pl.ds(pl.multiple_of(block * block_rows, block_rows), block_rows)
        piece = out_ref.at[place]
        for start, target, wanted in (
            (piece.at[:9], kern_ref.at[pl.ds(18 * half, 9), rows, :], None),
            (piece.at[9:13], kern_ref.at[pl.ds(9 + 5 * half, 4), rows, :], None),
            (piece.at[13], kern_ref.at[13, rows, :], 0),
            (piece.at[13], proj_ref.at[rows, :], 1),
        ):
            copy = pltpu.make_async_copy(start, target, sems.at[len(copies)])
            copies.append((copy, None if wanted is None else half == wanted))
            do(copies[-1][1], copy.start)
    for copy, wanted in copies:
        do(wanted, copy.wait)


def do(wanted, action):
    if wanted is None:
        action()
    else:
        pl.when(wanted)(action)


def unpack(where, pieces, offsets, scale, sofar=()):
    given = [piece for offset in offsets for piece in pieces[offset]]
    _, places, block_rows, chans = given[0].shape
    return pl.pallas_call(
        functools.partial(unpack_kernel, scale, offsets),
        out_shape=(
            jax.ShapeDtypeStruct((2 * places - 1, chans, chans), jnp.float32),
            jax.ShapeDtypeStruct((chans, chans), jnp.float32),
        ),
        in_specs=[SCALAR] + [VECTOR] * len(given) + [OUTSIDE] * len(sofar),
        out_specs=(OUTSIDE, OUTSIDE),
        scratch_shapes=[
            pltpu.VMEM((len(given), places, block_rows, chans), jnp.float32),
            pltpu.SemaphoreType.DMA((4 * len(given),)),
        ],
        input_output_aliases={1 + len(given) + i: i for i in range(len(sofar))},
        compiler_params=LIMIT,
        cost_estimate=pl.CostEstimate(
            flops=places * block_rows * chans * len(given),
            bytes_accessed=6 * places * block_rows * chans * len(given),
            transcendentals=0,
        ),
        name="unpack",
    )(where, *given, *sofar)


def summed(where, keep, send, scale, pre_grad, start_next, finish):
    total = keep[:1]
    for offset in (3, 2, 1):
        piece = swapped(send[offset : offset + 1], masks_of(0, offset))
        total = total + piece.astype(jnp.float32)
    total, pre_grad = lax.optimization_barrier((total, pre_grad))
    next_halo = start_next(pre_grad)
    total = lax.reduce_precision(total, 8, 7)
    third, second, first = (
        swapped(total.astype(jnp.bfloat16), masks_of(1, offset)).astype(jnp.float32)
        for offset in (3, 2, 1)
    )
    total = (total + first) + (second + third)
    count = lax.axis_size("dp") * lax.axis_size("tm")
    mask = 1 << (1 + sum(len(pair) for pair in PAIRS[0]))
    while mask < count:
        total = total + swapped(total, (mask, mask))
        mask *= 2
    total = total.astype(jnp.bfloat16)
    total, next_halo = lax.optimization_barrier((total, next_halo))
    mine = [total] + [swapped(total, masks_of(0, offset)) for offset in (1, 2, 3)]
    done = finish(pre_grad, next_halo)
    mine[1], done = lax.optimization_barrier((mine[1], done))
    pieces = [(piece, swapped(piece, (1, 1))) for piece in mine[:3]]
    sofar = unpack(where, pieces, (0, 1, 2), scale)
    pieces.append((mine[3], swapped(mine[3], (1, 1))))
    return unpack(where, pieces, (3,), scale, sofar), done


def prepare(width, frames, grads, conv_kernel, proj_weight):
    given = (frames, grads, conv_kernel, proj_weight)
    rows, chans = frames.shape
    return pl.pallas_call(
        functools.partial(prepare_kernel, width),
        out_shape=(
            *(jax.ShapeDtypeStruct(x.shape, x.dtype) for x in given),
            jax.ShapeDtypeStruct((rows, 3 * chans), jnp.bfloat16),
        ),
        in_specs=[OUTSIDE] * 4,
        out_specs=(VECTOR,) * 5,
        scratch_shapes=[pltpu.SemaphoreType.DMA((4,))],
        compiler_params=LIMIT,
        cost_estimate=pl.CostEstimate(flops=rows * chans, bytes_accessed=2 << 20, transcendentals=0),
        name="prepare",
    )(*(pltpu.with_memory_space_constraint(x, pltpu.HBM) for x in given))


def join(shape, where, own, grads, partner, partner_grads, conv_kernel, proj_weight):
    n_frames, height, width, chans = shape
    rows = n_frames * height * width
    head = 2 * height * width
    return pl.pallas_call(
        functools.partial(join_kernel, shape),
        out_shape=(
            jax.ShapeDtypeStruct((head + 2 * rows, 3 * chans), jnp.bfloat16),
            jax.ShapeDtypeStruct((2 * rows, chans), jnp.bfloat16),
            jax.ShapeDtypeStruct((2 * rows, 3 * chans), jnp.float32),
            jax.ShapeDtypeStruct((2 * rows, chans), jnp.float32),
        ),
        in_specs=[SCALAR] + [VECTOR] * 6,
        out_specs=(VECTOR,) * 4,
        compiler_params=LIMIT,
        cost_estimate=pl.CostEstimate(
            flops=2 * rows * 40 * chans * chans, bytes_accessed=2 << 20, transcendentals=0
        ),
        name="join",
    )(where, own, grads, partner, partner_grads, conv_kernel, proj_weight)


def forward(shape, where, first_halo, second_halo, grads, conv_kernel, wide, sums, hidden_grad):
    n_frames, height, width, chans = shape
    rows = n_frames * height * width
    half = (4, 14, chans // 4, chans)
    return pl.pallas_call(
        functools.partial(forward_kernel, shape),
        out_shape=(
            jax.ShapeDtypeStruct(half, jnp.float32),
            jax.ShapeDtypeStruct(half, jnp.bfloat16),
            jax.ShapeDtypeStruct((rows, chans), jnp.bfloat16),
            jax.ShapeDtypeStruct((rows, chans), jnp.bfloat16),
            jax.ShapeDtypeStruct(wide.shape, wide.dtype),
        ),
        in_specs=[SCALAR] + [VECTOR] * 7,
        out_specs=(VECTOR,) * 5,
        input_output_aliases={5: 4},
        compiler_params=LIMIT,
        name="forward",
    )(where, second_halo, first_halo, grads, conv_kernel, wide, sums, hidden_grad)[:4]


def backward(shape, where, pre_grad, following, hidden, frames, grads, conv_kernel, proj_weight):
    n_frames, height, width, chans = shape
    rows = n_frames * height * width
    flops = 2 * rows * 28 * chans * chans
    return pl.pallas_call(
        functools.partial(backward_kernel, shape),
        out_shape=(jax.ShapeDtypeStruct((rows, chans), jnp.bfloat16),) * 2,
        in_specs=[SCALAR] + [VECTOR] * 7,
        out_specs=(VECTOR,) * 2,
        scratch_shapes=[pltpu.VMEM((rows + 2 * height * width, 3 * chans), jnp.bfloat16)],
        compiler_params=LIMIT,
        cost_estimate=pl.CostEstimate(flops=flops, bytes_accessed=1 << 20, transcendentals=0),
        name="backward",
    )(where, pre_grad, following, hidden, frames, grads, conv_kernel, proj_weight)


def shards(clip_frames, out_grad, conv_kernel, proj_weight):
    shape = clip_frames.shape[1:]
    n_frames, height, width, chans = shape
    rows = n_frames * height * width
    halo_rows = 2 * height * width
    frames = clip_frames.reshape(rows, chans)
    grads = out_grad.reshape(rows, chans)
    block = lax.axis_index("tm")
    first = (block < 2).astype(jnp.int32)
    last = (block == lax.axis_size("tm") - 1).astype(jnp.int32)
    where = (4 * device_number() + 2 * first + last).astype(jnp.int32).reshape(1)
    tail = frames[rows - halo_rows :]
    first_halo = passed_round(tail, "tm", 1)
    second_halo = passed_to_last_core(tail)
    partner = swapped(frames, (1, 1))
    partner_grads = swapped(grads, (1, 1))
    frames, grads, conv_kernel, proj_weight, own = prepare(
        width, frames, grads, conv_kernel, proj_weight
    )
    wide, pair_grads, sums, hidden_grad = join(
        shape, where, own, grads, partner, partner_grads, conv_kernel, proj_weight
    )
    keep, send, hidden, pre_grad = forward(
        shape, where, first_halo, second_halo, pair_grads, conv_kernel, wide, sums, hidden_grad
    )
    total_pixels = lax.axis_size("dp") * lax.axis_size("tm") * rows
    (kernel_grad, proj_grad), (mixed, input_grad) = summed(
        where,
        keep,
        send,
        1.0 / math.sqrt(total_pixels),
        pre_grad,
        lambda grads_here: passed_round(grads_here[:halo_rows], "tm", -1),
        lambda grads_here, following: backward(
            shape, where, grads_here, following, hidden, frames, grads, conv_kernel, proj_weight
        ),
    )
    return (
        mixed.reshape(clip_frames.shape),
        input_grad.reshape(clip_frames.shape),
        kernel_grad.reshape(conv_kernel.shape),
        proj_grad,
    )


def solution(mesh):
    placed = (P("dp", "tm", None, None, None), P("dp", "tm", None, None, None), P(), P())
    return jax.shard_map(
        shards,
        mesh=mesh,
        in_specs=placed,
        out_specs=(P("dp", "tm", None, None, None), P("dp", "tm", None, None, None), P(), P()),
        check_vma=False,
    )
```

```python
import functools
import math

import jax
import jax.numpy as jnp
from jax import lax
from jax.experimental import pallas as pl
from jax.experimental.pallas import tpu as pltpu
from jax.sharding import PartitionSpec as P

AXES = ("dp", "tm")
PAIRS = (((1, 2), (3, 4)), ((3, 4), (1, 2)))
LIMIT = pltpu.CompilerParams(vmem_limit_bytes=16 * 1024 * 1024)
SCALAR = pl.BlockSpec(memory_space=pltpu.SMEM)
VECTOR = pl.BlockSpec(memory_space=pltpu.VMEM)
OUTSIDE = pl.BlockSpec(memory_space=pltpu.HBM)


def passed_round(shard, axis, by):
    size = lax.axis_size(axis)
    return lax.ppermute(shard, axis, [(i, (i + by) % size) for i in range(size)])


def passed_to_last_core(shard):
    clips, blocks = lax.axis_size("dp"), lax.axis_size("tm")
    pairs = [
        (clip * blocks + i, clip * blocks + (i + 2) % blocks if i & 1 else (clip ^ 1) * blocks + i)
        for clip in range(clips)
        for i in range(blocks)
    ]
    return lax.ppermute(shard, AXES, pairs)


def device_number():
    return lax.axis_index("dp") * lax.axis_size("tm") + lax.axis_index("tm")


def swapped(array, masks):
    count = lax.axis_size("dp") * lax.axis_size("tm")
    return lax.ppermute(array, AXES, [(i, i ^ masks[i & 1]) for i in range(count)])


def masks_of(stage, offset):
    return tuple(
        (offset >> 1) << pairs[stage][0] | (offset & 1) << pairs[stage][1] for pairs in PAIRS
    )


def halves_of(me):
    first, second = (2 * ((me >> split[0]) & 1) + ((me >> split[1]) & 1) for split, _ in PAIRS)
    core = me & 1
    return jnp.where(core == 0, first, second), jnp.where(core == 0, second, first)


def beside(flat, width):
    rows = flat.shape[0]
    wide = flat.astype(jnp.float32)
    column = lax.broadcasted_iota(jnp.int32, flat.shape, 0) % width
    before = jnp.where(column == 0, 0.0, pltpu.roll(wide, 1, 0)).astype(flat.dtype)
    after = jnp.where(column == width - 1, 0.0, pltpu.roll(wide, rows - 1, 0)).astype(flat.dtype)
    return before, after


def moved_rows(flat, map_rows, width, by):
    zero = jnp.zeros((width, flat.shape[1]), flat.dtype)
    pieces = []
    for start in range(0, flat.shape[0], map_rows):
        whole = flat[start : start + map_rows]
        pieces += [zero, whole[:-width]] if by == 1 else [whole[width:], zero]
    return jnp.concatenate(pieces, axis=0)


def dot(left, right, contract):
    return lax.dot_general(
        left, right, ((contract[:1], contract[1:]), ((), ())), preferred_element_type=jnp.float32
    )


def spread(flat, width, wide_ref, flipped=False):
    chans = flat.shape[1]
    before, after = beside(flat, width)
    wide_ref[:, :chans] = after if flipped else before
    wide_ref[:, chans : 2 * chans] = flat
    wide_ref[:, 2 * chans :] = before if flipped else after


def spread_unless(outside, ref, width, wide_ref, flipped=False):
    @pl.when(outside)
    def _():
        wide_ref[...] = jnp.zeros(wide_ref.shape, wide_ref.dtype)

    @pl.when(jnp.logical_not(outside))
    def _():
        spread(ref[...], width, wide_ref, flipped)


def weights_of(kern_ref, tau):
    chans = kern_ref.shape[-1]
    return jnp.concatenate(
        [kern_ref[tau, row].reshape(3 * chans, chans) for row in range(3)], axis=1
    )


def prepare_kernel(
    width, frames_hbm, grads_hbm, kern_hbm, proj_hbm,
    frames_ref, grads_ref, kern_ref, proj_ref, wide_ref, sems,
):
    pairs = (
        (frames_hbm, frames_ref), (grads_hbm, grads_ref), (kern_hbm, kern_ref), (proj_hbm, proj_ref)
    )
    copies = [pltpu.make_async_copy(*pair, sems.at[i]) for i, pair in enumerate(pairs)]
    for copy in copies:
        copy.start()
    copies[0].wait()
    spread(frames_ref[...], width, wide_ref)
    for copy in copies[1:]:
        copy.wait()


def join_kernel(
    shape, where_ref, own_ref, grads_ref, partner_ref, partner_grads_ref, kern_ref, proj_ref,
    turned_ref, pair_grads_ref, sums_ref, hidden_grad_ref, wide_ref,
):
    _, height, width, chans = shape
    map_rows = height * width
    rows = shape[0] * map_rows
    head = 2 * map_rows
    core = (where_ref[0] >> 2) & 1

    def part(start, index):
        return pl.ds(pl.multiple_of(start + index * rows, map_rows), rows)

    wide_ref[part(0, core)] = own_ref[...]
    spread(partner_ref[...], width, wide_ref.at[part(0, 1 - core)])
    pair_grads_ref[part(0, core)] = grads_ref[...]
    pair_grads_ref[part(0, 1 - core)] = partner_grads_ref[...]
    hidden_grad_ref[...] = dot(pair_grads_ref[...], proj_ref[...], (1, 1))
    sums_ref[...] = dot(wide_ref[...], weights_of(kern_ref, 2), (1, 0))
    for tau in (1, 0):
        skip = (2 - tau) * map_rows
        sums_ref[skip:] += dot(wide_ref[: 2 * rows - skip], weights_of(kern_ref, tau), (1, 0))
    turned_ref[:, head:] = wide_ref[...].T


def forward_kernel(
    shape, where_ref, second_halo_ref, first_halo_ref, grads_ref, kern_ref, _, sums_ref,
    hidden_grad_ref, keep_ref, send_ref, hidden_ref, pre_grad_ref, turned_ref, halo_ref,
):
    _, height, width, chans = shape
    map_rows = height * width
    rows = shape[0] * map_rows
    head = 2 * map_rows
    me = where_ref[0] >> 2
    core = me & 1
    outside = (where_ref[0] & 2) != 0

    @pl.when(outside)
    def _():
        halo_ref[...] = jnp.zeros(halo_ref.shape, halo_ref.dtype)

    @pl.when(jnp.logical_not(outside) & (core == 0))
    def _():
        spread(first_halo_ref[...], width, halo_ref)

    @pl.when(jnp.logical_not(outside) & (core == 1))
    def _():
        spread(second_halo_ref[...], width, halo_ref)

    turned_ref[:, :head] = halo_ref[...].T
    late = dot(halo_ref[...], weights_of(kern_ref, 0), (1, 0))
    early = dot(halo_ref[map_rows:], weights_of(kern_ref, 1), (1, 0))
    sums = sums_ref[...]
    sums = jnp.concatenate(
        [
            sums[:map_rows] + (late[:map_rows] + early),
            sums[map_rows:head] + late[map_rows:],
            sums[head:],
        ],
        axis=0,
    )
    pre = (
        moved_rows(sums[:, :chans], map_rows, width, 1)
        + sums[:, chans : 2 * chans]
        + moved_rows(sums[:, 2 * chans :], map_rows, width, -1)
    )
    sig = jax.nn.sigmoid(pre)
    hidden = (pre * sig).astype(jnp.bfloat16)
    pre_grad = (hidden_grad_ref[...] * sig * (1.0 + pre * (1.0 - sig))).astype(jnp.bfloat16)
    hidden_ref[...] = jnp.where(core == 0, hidden[:rows], hidden[rows:])
    pre_grad_ref[...] = jnp.where(core == 0, pre_grad[:rows], pre_grad[rows:])
    flip = halves_of(me)[0]

    def put(place, value):
        block_rows = keep_ref.shape[2]
        for block in range(4):
            rows_of = value[block * block_rows : (block + 1) * block_rows]
            keep_ref[block ^ flip, place] = rows_of
            send_ref[block ^ flip, place] = rows_of.astype(send_ref.dtype)

    grad_rows = jnp.concatenate(
        [
            moved_rows(pre_grad, map_rows, width, -1),
            pre_grad,
            moved_rows(pre_grad, map_rows, width, 1),
        ],
        axis=1,
    )

    def tap(sums, row, col):
        return sums[col * chans : (col + 1) * chans, row * chans : (row + 1) * chans]

    outer = pl.ds(pl.multiple_of(core * head, map_rows), 2 * rows)
    sums = dot(turned_ref[:, outer], grad_rows, (1, 0))
    for place in range(9):
        put(place + 4 * core, tap(sums, place // 3, place % 3))
    sums = dot(turned_ref[:, map_rows : map_rows + 2 * rows], grad_rows, (1, 0))
    middle = [tap(sums, place // 3, place % 3) for place in range(9)]
    middle.append(dot(hidden, grads_ref[...], (0, 0)))
    for place in range(5):
        put(
            13 if place == 4 else jnp.where(core == 0, 9 + place, place),
            jnp.where(core == 0, middle[place], middle[5 + place]),
        )


def backward_kernel(
    shape, where_ref, pre_grad_ref, next_ref, hidden_ref, frames_ref, grads_ref, kern_ref, proj_ref,
    mixed_ref, input_grad_ref, wide_ref,
):
    _, height, width, chans = shape
    map_rows = height * width
    rows = shape[0] * map_rows
    spread(pre_grad_ref[...], width, wide_ref.at[:rows], flipped=True)
    spread_unless((where_ref[0] & 1) != 0, next_ref, width, wide_ref.at[rows:], flipped=True)
    sums = None
    for tau in range(3):
        weights = jnp.concatenate(
            [kern_ref[tau, :, col].reshape(3 * chans, chans) for col in range(3)], axis=1
        )
        start = (2 - tau) * map_rows
        term = dot(wide_ref[start : start + rows], weights, (1, 1))
        sums = term if sums is None else sums + term
    back = (
        moved_rows(sums[:, :chans], map_rows, width, -1)
        + sums[:, chans : 2 * chans]
        + moved_rows(sums[:, 2 * chans :], map_rows, width, 1)
    )
    input_grad_ref[...] = (grads_ref[...].astype(jnp.float32) + back).astype(jnp.bfloat16)
    mixed_ref[...] = (
        frames_ref[...].astype(jnp.float32) + dot(hidden_ref[...], proj_ref[...], (1, 0))
    ).astype(jnp.bfloat16)


def unpack_kernel(scale, offsets, where_ref, *refs):
    pieces = refs[: 2 * len(offsets)]
    kern_ref, proj_ref, out_ref, sems = refs[-4:]
    me = where_ref[0] >> 2
    core = me & 1
    halves = tuple(zip((core, 1 - core), halves_of(me)))
    block_rows = out_ref.shape[2]
    copies = []
    for place, piece_ref in enumerate(pieces):
        half, flip = halves[place % 2]
        block = offsets[place // 2] ^ flip
        out_ref[place] = piece_ref[0].astype(jnp.float32) * scale
        rows = pl.ds(pl.multiple_of(block * block_rows, block_rows), block_rows)
        piece = out_ref.at[place]
        for start, target, wanted in (
            (piece.at[:13], kern_ref.at[pl.ds(14 * half, 13), rows, :], None),
            (piece.at[13], kern_ref.at[13, rows, :], 0),
            (piece.at[13], proj_ref.at[rows, :], 1),
        ):
            copy = pltpu.make_async_copy(start, target, sems.at[len(copies)])
            copies.append((copy, None if wanted is None else half == wanted))
            do(copies[-1][1], copy.start)
    for copy, wanted in copies:
        do(wanted, copy.wait)


def do(wanted, action):
    if wanted is None:
        action()
    else:
        pl.when(wanted)(action)


def unpack(where, pieces, offsets, scale, sofar=()):
    given = [piece for offset in offsets for piece in pieces[offset]]
    _, places, block_rows, chans = given[0].shape
    return pl.pallas_call(
        functools.partial(unpack_kernel, scale, offsets),
        out_shape=(
            jax.ShapeDtypeStruct((2 * places - 1, chans, chans), jnp.float32),
            jax.ShapeDtypeStruct((chans, chans), jnp.float32),
        ),
        in_specs=[SCALAR] + [VECTOR] * len(given) + [OUTSIDE] * len(sofar),
        out_specs=(OUTSIDE, OUTSIDE),
        scratch_shapes=[
            pltpu.VMEM((len(given), places, block_rows, chans), jnp.float32),
            pltpu.SemaphoreType.DMA((3 * len(given),)),
        ],
        input_output_aliases={1 + len(given) + i: i for i in range(len(sofar))},
        compiler_params=LIMIT,
        cost_estimate=pl.CostEstimate(
            flops=places * block_rows * chans * len(given),
            bytes_accessed=6 * places * block_rows * chans * len(given),
            transcendentals=0,
        ),
        name="unpack",
    )(where, *given, *sofar)


def summed(where, keep, send, scale, beside_split, beside_exchange):
    total = keep[:1]
    for offset in (3, 2, 1):
        piece = swapped(send[offset : offset + 1], masks_of(0, offset))
        total = total + piece.astype(jnp.float32)
    done = beside_split()
    total, done = lax.optimization_barrier((total, done))
    total = lax.reduce_precision(total, 8, 7)
    third, second, first = (
        swapped(total.astype(jnp.bfloat16), masks_of(1, offset)).astype(jnp.float32)
        for offset in (3, 2, 1)
    )
    total = (total + first) + (second + third)
    count = lax.axis_size("dp") * lax.axis_size("tm")
    mask = 1 << (1 + sum(len(pair) for pair in PAIRS[0]))
    while mask < count:
        total = total + swapped(total, (mask, mask))
        mask *= 2
    done = beside_exchange(done)
    total = total.astype(jnp.bfloat16)
    total, done = lax.optimization_barrier((total, done))
    mine = [total] + [swapped(total, masks_of(0, offset)) for offset in (1, 2, 3)]
    pieces = [(piece, swapped(piece, (1, 1))) for piece in mine[:3]]
    sofar = unpack(where, pieces, (0, 1, 2), scale)
    pieces.append((mine[3], swapped(mine[3], (1, 1))))
    return unpack(where, pieces, (3,), scale, sofar), done


def prepare(width, frames, grads, conv_kernel, proj_weight):
    given = (frames, grads, conv_kernel, proj_weight)
    rows, chans = frames.shape
    return pl.pallas_call(
        functools.partial(prepare_kernel, width),
        out_shape=(
            *(jax.ShapeDtypeStruct(x.shape, x.dtype) for x in given),
            jax.ShapeDtypeStruct((rows, 3 * chans), jnp.bfloat16),
        ),
        in_specs=[OUTSIDE] * 4,
        out_specs=(VECTOR,) * 5,
        scratch_shapes=[pltpu.SemaphoreType.DMA((4,))],
        compiler_params=LIMIT,
        cost_estimate=pl.CostEstimate(flops=rows * chans, bytes_accessed=2 << 20, transcendentals=0),
        name="prepare",
    )(*(pltpu.with_memory_space_constraint(x, pltpu.HBM) for x in given))


def join(shape, where, own, grads, partner, partner_grads, conv_kernel, proj_weight):
    n_frames, height, width, chans = shape
    rows = n_frames * height * width
    head = 2 * height * width
    return pl.pallas_call(
        functools.partial(join_kernel, shape),
        out_shape=(
            jax.ShapeDtypeStruct((3 * chans, head + 2 * rows), jnp.bfloat16),
            jax.ShapeDtypeStruct((2 * rows, chans), jnp.bfloat16),
            jax.ShapeDtypeStruct((2 * rows, 3 * chans), jnp.float32),
            jax.ShapeDtypeStruct((2 * rows, chans), jnp.float32),
        ),
        in_specs=[SCALAR] + [VECTOR] * 6,
        out_specs=(VECTOR,) * 4,
        scratch_shapes=[pltpu.VMEM((2 * rows, 3 * chans), jnp.bfloat16)],
        compiler_params=LIMIT,
        cost_estimate=pl.CostEstimate(
            flops=2 * rows * 40 * chans * chans, bytes_accessed=2 << 20, transcendentals=0
        ),
        name="join",
    )(where, own, grads, partner, partner_grads, conv_kernel, proj_weight)


def forward(shape, where, first_halo, second_halo, grads, conv_kernel, wide, sums, hidden_grad):
    n_frames, height, width, chans = shape
    rows = n_frames * height * width
    half = (4, 14, chans // 4, chans)
    return pl.pallas_call(
        functools.partial(forward_kernel, shape),
        out_shape=(
            jax.ShapeDtypeStruct(half, jnp.float32),
            jax.ShapeDtypeStruct(half, jnp.bfloat16),
            jax.ShapeDtypeStruct((rows, chans), jnp.bfloat16),
            jax.ShapeDtypeStruct((rows, chans), jnp.bfloat16),
            jax.ShapeDtypeStruct(wide.shape, wide.dtype),
        ),
        in_specs=[SCALAR] + [VECTOR] * 7,
        out_specs=(VECTOR,) * 5,
        scratch_shapes=[pltpu.VMEM((2 * height * width, 3 * chans), jnp.bfloat16)],
        input_output_aliases={5: 4},
        compiler_params=LIMIT,
        name="forward",
    )(where, second_halo, first_halo, grads, conv_kernel, wide, sums, hidden_grad)[:4]


def backward(shape, where, pre_grad, following, hidden, frames, grads, conv_kernel, proj_weight):
    n_frames, height, width, chans = shape
    rows = n_frames * height * width
    flops = 2 * rows * 28 * chans * chans
    return pl.pallas_call(
        functools.partial(backward_kernel, shape),
        out_shape=(jax.ShapeDtypeStruct((rows, chans), jnp.bfloat16),) * 2,
        in_specs=[SCALAR] + [VECTOR] * 7,
        out_specs=(VECTOR,) * 2,
        scratch_shapes=[pltpu.VMEM((rows + 2 * height * width, 3 * chans), jnp.bfloat16)],
        compiler_params=LIMIT,
        cost_estimate=pl.CostEstimate(flops=flops, bytes_accessed=1 << 20, transcendentals=0),
        name="backward",
    )(where, pre_grad, following, hidden, frames, grads, conv_kernel, proj_weight)


def shards(clip_frames, out_grad, conv_kernel, proj_weight):
    shape = clip_frames.shape[1:]
    n_frames, height, width, chans = shape
    rows = n_frames * height * width
    halo_rows = 2 * height * width
    frames = clip_frames.reshape(rows, chans)
    grads = out_grad.reshape(rows, chans)
    block = lax.axis_index("tm")
    first = (block < 2).astype(jnp.int32)
    last = (block == lax.axis_size("tm") - 1).astype(jnp.int32)
    where = (4 * device_number() + 2 * first + last).astype(jnp.int32).reshape(1)
    tail = frames[rows - halo_rows :]
    first_halo = passed_round(tail, "tm", 1)
    second_halo = passed_to_last_core(tail)
    partner = swapped(frames, (1, 1))
    partner_grads = swapped(grads, (1, 1))
    frames, grads, conv_kernel, proj_weight, own = prepare(
        width, frames, grads, conv_kernel, proj_weight
    )
    wide, pair_grads, sums, hidden_grad = join(
        shape, where, own, grads, partner, partner_grads, conv_kernel, proj_weight
    )
    keep, send, hidden, pre_grad = forward(
        shape, where, first_halo, second_halo, pair_grads, conv_kernel, wide, sums, hidden_grad
    )
    total_pixels = lax.axis_size("dp") * lax.axis_size("tm") * rows
    (kernel_grad, proj_grad), (mixed, input_grad) = summed(
        where,
        keep,
        send,
        1.0 / math.sqrt(total_pixels),
        lambda: passed_round(pre_grad[:halo_rows], "tm", -1),
        lambda following: backward(
            shape, where, pre_grad, following, hidden, frames, grads, conv_kernel, proj_weight
        ),
    )
    return (
        mixed.reshape(clip_frames.shape),
        input_grad.reshape(clip_frames.shape),
        kernel_grad.reshape(conv_kernel.shape),
        proj_grad,
    )


def solution(mesh):
    placed = (P("dp", "tm", None, None, None), P("dp", "tm", None, None, None), P(), P())
    return jax.shard_map(
        shards,
        mesh=mesh,
        in_specs=placed,
        out_specs=(P("dp", "tm", None, None, None), P("dp", "tm", None, None, None), P(), P()),
        check_vma=False,
    )
```

```python
import functools
import math

import jax
import jax.numpy as jnp
from jax import lax
from jax.experimental import pallas as pl
from jax.experimental.pallas import tpu as pltpu
from jax.sharding import PartitionSpec as P

AXES = ("dp", "tm")
PAIRS = (((1, 2), (3, 4)), ((3, 4), (1, 2)))
LIMIT = pltpu.CompilerParams(vmem_limit_bytes=16 * 1024 * 1024)
SCALAR = pl.BlockSpec(memory_space=pltpu.SMEM)
VECTOR = pl.BlockSpec(memory_space=pltpu.VMEM)
OUTSIDE = pl.BlockSpec(memory_space=pltpu.HBM)


def passed_round(shard, axis, by):
    size = lax.axis_size(axis)
    return lax.ppermute(shard, axis, [(i, (i + by) % size) for i in range(size)])


def passed_to_last_core(shard):
    clips, blocks = lax.axis_size("dp"), lax.axis_size("tm")
    pairs = [
        (clip * blocks + i, clip * blocks + (i + 2) % blocks if i & 1 else (clip ^ 1) * blocks + i)
        for clip in range(clips)
        for i in range(blocks)
    ]
    return lax.ppermute(shard, AXES, pairs)


def device_number():
    return lax.axis_index("dp") * lax.axis_size("tm") + lax.axis_index("tm")


def swapped(array, masks):
    count = lax.axis_size("dp") * lax.axis_size("tm")
    return lax.ppermute(array, AXES, [(i, i ^ masks[i & 1]) for i in range(count)])


def masks_of(stage, offset):
    return tuple(
        (offset >> 1) << pairs[stage][0] | (offset & 1) << pairs[stage][1] for pairs in PAIRS
    )


def halves_of(me):
    first, second = (2 * ((me >> split[0]) & 1) + ((me >> split[1]) & 1) for split, _ in PAIRS)
    core = me & 1
    return jnp.where(core == 0, first, second), jnp.where(core == 0, second, first)


def beside(flat, width):
    rows = flat.shape[0]
    wide = flat.astype(jnp.float32)
    column = lax.broadcasted_iota(jnp.int32, flat.shape, 0) % width
    before = jnp.where(column == 0, 0.0, pltpu.roll(wide, 1, 0)).astype(flat.dtype)
    after = jnp.where(column == width - 1, 0.0, pltpu.roll(wide, rows - 1, 0)).astype(flat.dtype)
    return before, after


def moved_rows(flat, map_rows, width, by):
    zero = jnp.zeros((width, flat.shape[1]), flat.dtype)
    pieces = []
    for start in range(0, flat.shape[0], map_rows):
        whole = flat[start : start + map_rows]
        pieces += [zero, whole[:-width]] if by == 1 else [whole[width:], zero]
    return jnp.concatenate(pieces, axis=0)


def dot(left, right, contract):
    return lax.dot_general(
        left, right, ((contract[:1], contract[1:]), ((), ())), preferred_element_type=jnp.float32
    )


def spread(flat, width, wide_ref, flipped=False):
    chans = flat.shape[1]
    before, after = beside(flat, width)
    wide_ref[:, :chans] = after if flipped else before
    wide_ref[:, chans : 2 * chans] = flat
    wide_ref[:, 2 * chans :] = before if flipped else after


def spread_unless(outside, ref, width, wide_ref, flipped=False):
    @pl.when(outside)
    def _():
        wide_ref[...] = jnp.zeros(wide_ref.shape, wide_ref.dtype)

    @pl.when(jnp.logical_not(outside))
    def _():
        spread(ref[...], width, wide_ref, flipped)


def weights_of(kern_ref, tau):
    chans = kern_ref.shape[-1]
    return jnp.concatenate(
        [kern_ref[tau, row].reshape(3 * chans, chans) for row in range(3)], axis=1
    )


def prepare_kernel(
    width, frames_hbm, grads_hbm, kern_hbm, proj_hbm,
    frames_ref, grads_ref, kern_ref, proj_ref, wide_ref, sems,
):
    pairs = (
        (frames_hbm, frames_ref), (grads_hbm, grads_ref), (kern_hbm, kern_ref), (proj_hbm, proj_ref)
    )
    copies = [pltpu.make_async_copy(*pair, sems.at[i]) for i, pair in enumerate(pairs)]
    for copy in copies:
        copy.start()
    copies[0].wait()
    spread(frames_ref[...], width, wide_ref)
    for copy in copies[1:]:
        copy.wait()


def join_kernel(
    shape, where_ref, own_ref, grads_ref, partner_ref, partner_grads_ref, kern_ref, proj_ref,
    turned_ref, pair_grads_ref, sums_ref, hidden_grad_ref, wide_ref,
):
    _, height, width, chans = shape
    map_rows = height * width
    rows = shape[0] * map_rows
    head = 2 * map_rows
    core = (where_ref[0] >> 2) & 1

    def part(start, index):
        return pl.ds(pl.multiple_of(start + index * rows, map_rows), rows)

    wide_ref[part(0, core)] = own_ref[...]
    spread(partner_ref[...], width, wide_ref.at[part(0, 1 - core)])
    pair_grads_ref[part(0, core)] = grads_ref[...]
    pair_grads_ref[part(0, 1 - core)] = partner_grads_ref[...]
    hidden_grad_ref[...] = dot(pair_grads_ref[...], proj_ref[...], (1, 1))
    sums_ref[...] = dot(wide_ref[...], weights_of(kern_ref, 2), (1, 0))
    for tau in (1, 0):
        skip = (2 - tau) * map_rows
        sums_ref[skip:] += dot(wide_ref[: 2 * rows - skip], weights_of(kern_ref, tau), (1, 0))
    turned_ref[:, head:] = wide_ref[...].T


def forward_kernel(
    shape, where_ref, second_halo_ref, first_halo_ref, grads_ref, kern_ref, _, sums_ref,
    hidden_grad_ref, keep_ref, send_ref, hidden_ref, pre_grad_ref, turned_ref, halo_ref,
):
    _, height, width, chans = shape
    map_rows = height * width
    rows = shape[0] * map_rows
    head = 2 * map_rows
    me = where_ref[0] >> 2
    core = me & 1
    outside = (where_ref[0] & 2) != 0

    @pl.when(outside)
    def _():
        halo_ref[...] = jnp.zeros(halo_ref.shape, halo_ref.dtype)

    @pl.when(jnp.logical_not(outside) & (core == 0))
    def _():
        spread(first_halo_ref[...], width, halo_ref)

    @pl.when(jnp.logical_not(outside) & (core == 1))
    def _():
        spread(second_halo_ref[...], width, halo_ref)

    turned_ref[:, :head] = halo_ref[...].T
    late = dot(halo_ref[...], weights_of(kern_ref, 0), (1, 0))
    early = dot(halo_ref[map_rows:], weights_of(kern_ref, 1), (1, 0))
    sums = sums_ref[...]
    sums = jnp.concatenate(
        [
            sums[:map_rows] + (late[:map_rows] + early),
            sums[map_rows:head] + late[map_rows:],
            sums[head:],
        ],
        axis=0,
    )
    pre = (
        moved_rows(sums[:, :chans], map_rows, width, 1)
        + sums[:, chans : 2 * chans]
        + moved_rows(sums[:, 2 * chans :], map_rows, width, -1)
    )
    sig = jax.nn.sigmoid(pre)
    hidden = (pre * sig).astype(jnp.bfloat16)
    pre_grad = (hidden_grad_ref[...] * sig * (1.0 + pre * (1.0 - sig))).astype(jnp.bfloat16)
    hidden_ref[...] = jnp.where(core == 0, hidden[:rows], hidden[rows:])
    pre_grad_ref[...] = jnp.where(core == 0, pre_grad[:rows], pre_grad[rows:])
    flip = halves_of(me)[0]

    def put(place, value):
        block_rows = keep_ref.shape[2]
        for block in range(4):
            rows_of = value[block * block_rows : (block + 1) * block_rows]
            keep_ref[block ^ flip, place] = rows_of
            send_ref[block ^ flip, place] = rows_of.astype(send_ref.dtype)

    grad_rows = jnp.concatenate(
        [
            moved_rows(pre_grad, map_rows, width, -1),
            pre_grad,
            moved_rows(pre_grad, map_rows, width, 1),
        ],
        axis=1,
    )

    def tap(sums, row, col):
        return sums[col * chans : (col + 1) * chans, row * chans : (row + 1) * chans]

    outer = pl.ds(pl.multiple_of(core * head, map_rows), 2 * rows)
    sums = dot(turned_ref[:, outer], grad_rows, (1, 0))
    for place in range(9):
        put(place + 4 * core, tap(sums, place // 3, place % 3))
    sums = dot(turned_ref[:, map_rows : map_rows + 2 * rows], grad_rows, (1, 0))
    middle = [tap(sums, place // 3, place % 3) for place in range(9)]
    middle.append(dot(hidden, grads_ref[...], (0, 0)))
    for place in range(5):
        put(
            13 if place == 4 else jnp.where(core == 0, 9 + place, place),
            jnp.where(core == 0, middle[place], middle[5 + place]),
        )


def backward_kernel(
    shape, where_ref, pre_grad_ref, next_ref, hidden_ref, frames_ref, grads_ref, kern_ref, proj_ref,
    mixed_ref, input_grad_ref, wide_ref,
):
    _, height, width, chans = shape
    map_rows = height * width
    rows = shape[0] * map_rows
    spread(pre_grad_ref[...], width, wide_ref.at[:rows], flipped=True)
    spread_unless((where_ref[0] & 1) != 0, next_ref, width, wide_ref.at[rows:], flipped=True)
    sums = None
    for tau in range(3):
        weights = jnp.concatenate(
            [kern_ref[tau, :, col].reshape(3 * chans, chans) for col in range(3)], axis=1
        )
        start = (2 - tau) * map_rows
        term = dot(wide_ref[start : start + rows], weights, (1, 1))
        sums = term if sums is None else sums + term
    back = (
        moved_rows(sums[:, :chans], map_rows, width, -1)
        + sums[:, chans : 2 * chans]
        + moved_rows(sums[:, 2 * chans :], map_rows, width, 1)
    )
    input_grad_ref[...] = (grads_ref[...].astype(jnp.float32) + back).astype(jnp.bfloat16)
    mixed_ref[...] = (
        frames_ref[...].astype(jnp.float32) + dot(hidden_ref[...], proj_ref[...], (1, 0))
    ).astype(jnp.bfloat16)


def unpack_kernel(scale, offsets, where_ref, *refs):
    pieces = refs[: 2 * len(offsets)]
    kern_ref, proj_ref, out_ref, sems = refs[-4:]
    me = where_ref[0] >> 2
    core = me & 1
    halves = tuple(zip((core, 1 - core), halves_of(me)))
    block_rows = out_ref.shape[2]
    copies = []
    for place, piece_ref in enumerate(pieces):
        half, flip = halves[place % 2]
        block = offsets[place // 2] ^ flip
        out_ref[place] = piece_ref[0].astype(jnp.float32) * scale
        rows = pl.ds(pl.multiple_of(block * block_rows, block_rows), block_rows)
        piece = out_ref.at[place]
        for start, target, wanted in (
            (piece.at[:13], kern_ref.at[pl.ds(14 * half, 13), rows, :], None),
            (piece.at[13], kern_ref.at[13, rows, :], 0),
            (piece.at[13], proj_ref.at[rows, :], 1),
        ):
            copy = pltpu.make_async_copy(start, target, sems.at[len(copies)])
            copies.append((copy, None if wanted is None else half == wanted))
            do(copies[-1][1], copy.start)
    for copy, wanted in copies:
        do(wanted, copy.wait)


def do(wanted, action):
    if wanted is None:
        action()
    else:
        pl.when(wanted)(action)


def unpack(where, pieces, offsets, scale, sofar=()):
    given = [piece for offset in offsets for piece in pieces[offset]]
    _, places, block_rows, chans = given[0].shape
    return pl.pallas_call(
        functools.partial(unpack_kernel, scale, offsets),
        out_shape=(
            jax.ShapeDtypeStruct((2 * places - 1, chans, chans), jnp.float32),
            jax.ShapeDtypeStruct((chans, chans), jnp.float32),
        ),
        in_specs=[SCALAR] + [VECTOR] * len(given) + [OUTSIDE] * len(sofar),
        out_specs=(OUTSIDE, OUTSIDE),
        scratch_shapes=[
            pltpu.VMEM((len(given), places, block_rows, chans), jnp.float32),
            pltpu.SemaphoreType.DMA((3 * len(given),)),
        ],
        input_output_aliases={1 + len(given) + i: i for i in range(len(sofar))},
        compiler_params=LIMIT,
        cost_estimate=pl.CostEstimate(
            flops=places * block_rows * chans * len(given),
            bytes_accessed=6 * places * block_rows * chans * len(given),
            transcendentals=0,
        ),
        name="unpack",
    )(where, *given, *sofar)


def summed(where, keep, send, scale, pre_grad, start_next, finish):
    total = keep[:1]
    for offset in (3, 2, 1):
        piece = swapped(send[offset : offset + 1], masks_of(0, offset))
        total = total + piece.astype(jnp.float32)
    total, pre_grad = lax.optimization_barrier((total, pre_grad))
    next_halo = start_next(pre_grad)
    total = lax.reduce_precision(total, 8, 7)
    third, second, first = (
        swapped(total.astype(jnp.bfloat16), masks_of(1, offset)).astype(jnp.float32)
        for offset in (3, 2, 1)
    )
    total = (total + first) + (second + third)
    count = lax.axis_size("dp") * lax.axis_size("tm")
    mask = 1 << (1 + sum(len(pair) for pair in PAIRS[0]))
    while mask < count:
        total = total + swapped(total, (mask, mask))
        mask *= 2
    total = total.astype(jnp.bfloat16)
    total, next_halo = lax.optimization_barrier((total, next_halo))
    mine = [total] + [swapped(total, masks_of(0, offset)) for offset in (1, 2, 3)]
    done = finish(pre_grad, next_halo)
    mine[1], done = lax.optimization_barrier((mine[1], done))
    pieces = [(piece, swapped(piece, (1, 1))) for piece in mine[:3]]
    sofar = unpack(where, pieces, (0, 1, 2), scale)
    pieces.append((mine[3], swapped(mine[3], (1, 1))))
    return unpack(where, pieces, (3,), scale, sofar), done


def prepare(width, frames, grads, conv_kernel, proj_weight):
    given = (frames, grads, conv_kernel, proj_weight)
    rows, chans = frames.shape
    return pl.pallas_call(
        functools.partial(prepare_kernel, width),
        out_shape=(
            *(jax.ShapeDtypeStruct(x.shape, x.dtype) for x in given),
            jax.ShapeDtypeStruct((rows, 3 * chans), jnp.bfloat16),
        ),
        in_specs=[OUTSIDE] * 4,
        out_specs=(VECTOR,) * 5,
        scratch_shapes=[pltpu.SemaphoreType.DMA((4,))],
        compiler_params=LIMIT,
        cost_estimate=pl.CostEstimate(flops=rows * chans, bytes_accessed=2 << 20, transcendentals=0),
        name="prepare",
    )(*(pltpu.with_memory_space_constraint(x, pltpu.HBM) for x in given))


def join(shape, where, own, grads, partner, partner_grads, conv_kernel, proj_weight):
    n_frames, height, width, chans = shape
    rows = n_frames * height * width
    head = 2 * height * width
    return pl.pallas_call(
        functools.partial(join_kernel, shape),
        out_shape=(
            jax.ShapeDtypeStruct((3 * chans, head + 2 * rows), jnp.bfloat16),
            jax.ShapeDtypeStruct((2 * rows, chans), jnp.bfloat16),
            jax.ShapeDtypeStruct((2 * rows, 3 * chans), jnp.float32),
            jax.ShapeDtypeStruct((2 * rows, chans), jnp.float32),
        ),
        in_specs=[SCALAR] + [VECTOR] * 6,
        out_specs=(VECTOR,) * 4,
        scratch_shapes=[pltpu.VMEM((2 * rows, 3 * chans), jnp.bfloat16)],
        compiler_params=LIMIT,
        cost_estimate=pl.CostEstimate(
            flops=2 * rows * 40 * chans * chans, bytes_accessed=2 << 20, transcendentals=0
        ),
        name="join",
    )(where, own, grads, partner, partner_grads, conv_kernel, proj_weight)


def forward(shape, where, first_halo, second_halo, grads, conv_kernel, wide, sums, hidden_grad):
    n_frames, height, width, chans = shape
    rows = n_frames * height * width
    half = (4, 14, chans // 4, chans)
    return pl.pallas_call(
        functools.partial(forward_kernel, shape),
        out_shape=(
            jax.ShapeDtypeStruct(half, jnp.float32),
            jax.ShapeDtypeStruct(half, jnp.bfloat16),
            jax.ShapeDtypeStruct((rows, chans), jnp.bfloat16),
            jax.ShapeDtypeStruct((rows, chans), jnp.bfloat16),
            jax.ShapeDtypeStruct(wide.shape, wide.dtype),
        ),
        in_specs=[SCALAR] + [VECTOR] * 7,
        out_specs=(VECTOR,) * 5,
        scratch_shapes=[pltpu.VMEM((2 * height * width, 3 * chans), jnp.bfloat16)],
        input_output_aliases={5: 4},
        compiler_params=LIMIT,
        name="forward",
    )(where, second_halo, first_halo, grads, conv_kernel, wide, sums, hidden_grad)[:4]


def backward(shape, where, pre_grad, following, hidden, frames, grads, conv_kernel, proj_weight):
    n_frames, height, width, chans = shape
    rows = n_frames * height * width
    flops = 2 * rows * 28 * chans * chans
    return pl.pallas_call(
        functools.partial(backward_kernel, shape),
        out_shape=(jax.ShapeDtypeStruct((rows, chans), jnp.bfloat16),) * 2,
        in_specs=[SCALAR] + [VECTOR] * 7,
        out_specs=(VECTOR,) * 2,
        scratch_shapes=[pltpu.VMEM((rows + 2 * height * width, 3 * chans), jnp.bfloat16)],
        compiler_params=LIMIT,
        cost_estimate=pl.CostEstimate(flops=flops, bytes_accessed=1 << 20, transcendentals=0),
        name="backward",
    )(where, pre_grad, following, hidden, frames, grads, conv_kernel, proj_weight)


def shards(clip_frames, out_grad, conv_kernel, proj_weight):
    shape = clip_frames.shape[1:]
    n_frames, height, width, chans = shape
    rows = n_frames * height * width
    halo_rows = 2 * height * width
    frames = clip_frames.reshape(rows, chans)
    grads = out_grad.reshape(rows, chans)
    block = lax.axis_index("tm")
    first = (block < 2).astype(jnp.int32)
    last = (block == lax.axis_size("tm") - 1).astype(jnp.int32)
    where = (4 * device_number() + 2 * first + last).astype(jnp.int32).reshape(1)
    tail = frames[rows - halo_rows :]
    first_halo = passed_round(tail, "tm", 1)
    second_halo = passed_to_last_core(tail)
    partner = swapped(frames, (1, 1))
    partner_grads = swapped(grads, (1, 1))
    frames, grads, conv_kernel, proj_weight, own = prepare(
        width, frames, grads, conv_kernel, proj_weight
    )
    wide, pair_grads, sums, hidden_grad = join(
        shape, where, own, grads, partner, partner_grads, conv_kernel, proj_weight
    )
    keep, send, hidden, pre_grad = forward(
        shape, where, first_halo, second_halo, pair_grads, conv_kernel, wide, sums, hidden_grad
    )
    total_pixels = lax.axis_size("dp") * lax.axis_size("tm") * rows
    (kernel_grad, proj_grad), (mixed, input_grad) = summed(
        where,
        keep,
        send,
        1.0 / math.sqrt(total_pixels),
        pre_grad,
        lambda grads_here: passed_round(grads_here[:halo_rows], "tm", -1),
        lambda grads_here, following: backward(
            shape, where, grads_here, following, hidden, frames, grads, conv_kernel, proj_weight
        ),
    )
    return (
        mixed.reshape(clip_frames.shape),
        input_grad.reshape(clip_frames.shape),
        kernel_grad.reshape(conv_kernel.shape),
        proj_grad,
    )


def solution(mesh):
    placed = (P("dp", "tm", None, None, None), P("dp", "tm", None, None, None), P(), P())
    return jax.shard_map(
        shards,
        mesh=mesh,
        in_specs=placed,
        out_specs=(P("dp", "tm", None, None, None), P("dp", "tm", None, None, None), P(), P()),
        check_vma=False,
    )
```
